32 devices in a mesh: seq: 8 (over z, y), chan: 4 (over x, core).
Axes of the slice: x: 2, y: 2, z: 4, core: 2. Of those that a mesh axis runs over, the one named last changes fastest.
Arguments:
- tokens: bfloat16 [4096, 4096], P('seq', 'chan'), may hold values from -6 to 6
- grad_out: bfloat16 [4096, 4096], P('seq', 'chan'), may hold values from -0.125 to 0.125
- in_weight: bfloat16 [4096, 3, 256], P('seq', None, 'chan'), may hold values from -0.09375 to 0.09375
- out_weight: bfloat16 [4096, 256], P('seq', 'chan'), may hold values from -0.09375 to 0.09375
- conv_out: bfloat16 [4096, 256], P('seq', 'chan'), may hold values from -6 to 6
- residues: float32 [16, 128], P(None, 'chan'), may hold values from -1.5 to 1.5
- decay_length: float32 [16, 128], P(None, 'chan'), may hold values from 8 to 262144
Outputs:
- grad_in_weight: float32 [4096, 3, 256], P('seq', None, 'chan')
- grad_out_weight: float32 [4096, 256], P('seq', 'chan')
The draws below stay inside these ranges and needn't reach their ends.
All inputs are finite; a program needn't handle non-finite values.
Results may differ from the reference program's by a relative error of at most 0.0041.
Values may be sent and summed in bfloat16 or wider, within the bound.
A program may use at most 64 MiB of HBM per device.

```python
import math
import jax
import jax.numpy as jnp
from jax import lax

D = 4096
C = 256
MODES = 16
SEQ = 4096
FILTERS = 128


def strengthened(array, rng, source, target, blocks, factor):
    def block_of(position):
        return (jnp.arange(array.shape[position]) // (array.shape[position] // blocks)).reshape((-1,) + (1,) * (array.ndim - 1 - position))

    first = jax.random.permutation(rng, blocks)[block_of(target)]
    other_side = (block_of(target) + blocks // 2) % blocks
    return jnp.where((block_of(source) == first) | (block_of(source) == other_side), factor * array, array)


def steps_of(own_key, shape, split, smallest, top_value):
    loudness, own = 1.0, jax.random.fold_in(own_key, 6)
    for axis_at, blocks in split:
        draws = jnp.exp(jax.random.uniform(jax.random.fold_in(own, axis_at), (blocks,), jnp.float32, smallest / len(split), top_value / len(split)))
        loudness = loudness * jnp.repeat(draws, shape[axis_at] // blocks).reshape([-1 if axis == axis_at else 1 for axis in range(len(shape))])
    return loudness


def bell_draw(stream_key, dims, scale, bound, split=(), held_as=jnp.bfloat16):
    entries = scale * jax.random.normal(stream_key, dims, jnp.float32)
    if split:
        entries = entries * steps_of(stream_key, dims, split, -0.22, 0.18)
    return jnp.clip(entries, -bound, bound).astype(held_as)


def gaussian_with(rng, shape, deviation, most, split, heavy, dtype=jnp.bfloat16):
    array = deviation * jax.random.normal(rng, shape, jnp.float32)
    if split:
        array = array * steps_of(rng, shape, split, -0.22, 0.18)
    return jnp.clip(strengthened(array, jax.random.fold_in(rng, 3), *heavy), -most, most).astype(dtype)


def setup_inputs(seed: int = 0) -> dict:
    keys = jax.random.split(jax.random.key(seed), 8)
    return {
        "tokens": gaussian_with(keys[0], (SEQ, D), 1.0, 6.0, ((0, 8), (1, 4)), (0, 1, 8, 2.0)),
        "grad_out": gaussian_with(keys[1], (SEQ, D), SEQ ** -0.5, 0.125, ((0, 8), (1, 4)), (0, 1, 8, 2.0)),
        "in_weight": bell_draw(keys[2], (D, 3, C), D ** -0.5, 0.09375, ((0, 8), (2, 4))),
        "out_weight": bell_draw(keys[3], (D, C), D ** -0.5, 0.09375, ((0, 8), (1, 4))),
        "conv_out": bell_draw(keys[4], (SEQ, C), 1.0, 6.0, ((0, 8), (1, 4))),
        "residues": bell_draw(keys[5], (MODES, FILTERS), MODES ** -0.5, 1.5, ((1, 4),), jnp.float32),
        "decay_length": jnp.clip(jnp.exp(math.log(262144.0) - 10.3972077 * jax.random.uniform(keys[6], (MODES, FILTERS), jnp.float32) ** steps_of(keys[6], (MODES, FILTERS), ((1, 4),), -0.2, 0.2)), 8.0, 262144.0),
    }


def filter_taps(residues, decay_length):
    inverse_len = 1.0 / decay_length
    weight = residues * jnp.sqrt(-jnp.expm1(-2.0 * inverse_len))
    moments = jnp.arange(SEQ).astype(jnp.float32)

    def add_mode(running, inputs):
        mode_weight, mode_rate = inputs
        return (running + mode_weight[None, :] * jnp.exp(-moments[:, None] * mode_rate[None, :]), None)
    impulse, _ = lax.scan(add_mode, jnp.zeros((SEQ, FILTERS), jnp.float32), (weight, inverse_len))
    return impulse

def correlate(impulse, signal):
    paired = signal[:, 0::2] + 1j * signal[:, 1::2]
    spectrum = jnp.fft.fft(paired, n=2 * SEQ, axis=0)
    response = jnp.conj(jnp.fft.fft(impulse, n=2 * SEQ, axis=0))
    result = jnp.fft.ifft(spectrum * response, axis=0)[:SEQ]
    return jnp.stack([jnp.real(result), jnp.imag(result)], axis=2).reshape(SEQ, C)

def reference(tokens, grad_out, in_weight, out_weight, conv_out, residues, decay_length):
    projected = jnp.dot(tokens, in_weight.reshape(D, 3 * C), preferred_element_type=jnp.float32)
    streams = projected.astype(jnp.bfloat16).reshape(SEQ, 3, C)
    gate_first = streams[:, 0].astype(jnp.float32)
    gate_second = streams[:, 1].astype(jnp.float32)
    value_stream = streams[:, 2].astype(jnp.float32)
    conv_value = conv_out.astype(jnp.float32)
    gated = (gate_second * conv_value).astype(jnp.bfloat16)
    upstream = jnp.dot(grad_out, out_weight, preferred_element_type=jnp.float32)
    grad_second = (upstream * conv_value).astype(jnp.bfloat16)
    grad_conv = upstream * gate_second
    grad_source = correlate(filter_taps(residues, decay_length), grad_conv)
    grad_first = (grad_source * value_stream).astype(jnp.bfloat16)
    grad_value = (grad_source * gate_first).astype(jnp.bfloat16)
    grad_streams = jnp.stack([grad_first, grad_second, grad_value], axis=1).reshape(SEQ, 3 * C)
    grad_in = lax.dot_general(tokens, grad_streams, (((0,), (0,)), ((), ())), preferred_element_type=jnp.float32)
    grad_proj = lax.dot_general(grad_out, gated, (((0,), (0,)), ((), ())), preferred_element_type=jnp.float32)
    return (grad_in.reshape(D, 3, C), grad_proj)
```

```python
import functools
import math

import jax
import jax.numpy as jnp
from jax import lax
from jax.experimental import pallas as pl
from jax.experimental.pallas import tpu as pltpu
from jax.sharding import PartitionSpec as P

precise = lax.Precision.HIGHEST
MESH = pl.DeviceIdType.MESH


def remote(source, target, send_sem, recv_sem, device):
    return pltpu.make_async_remote_copy(
        src_ref=source,
        dst_ref=target,
        send_sem=send_sem,
        recv_sem=recv_sem,
        device_id=device,
        device_id_type=MESH,
    )


def greet(devices_seq, devices_chan, seq_wide):
    seq, chan = lax.axis_index("seq"), lax.axis_index("chan")
    barrier = pltpu.get_barrier_semaphore()
    count = 0
    if seq_wide == "all":

        def hello(step, carry):
            pl.semaphore_signal(
                barrier,
                inc=1,
                device_id=(lax.rem(seq + step, devices_seq), chan),
                device_id_type=MESH,
            )
            return carry

        lax.fori_loop(1, devices_seq, hello, 0)
        count += devices_seq - 1
    else:
        groups = devices_seq // 2

        def hello_group(step, carry):
            there = lax.rem(seq // 2 + step, groups) * 2 + seq % 2
            pl.semaphore_signal(barrier, inc=1, device_id=(there, chan), device_id_type=MESH)
            return carry

        lax.fori_loop(1, groups, hello_group, 0)
        pl.semaphore_signal(
            barrier, inc=1, device_id=(seq + 1 - 2 * (seq % 2), chan), device_id_type=MESH
        )
        count += groups
    if devices_chan:
        groups = devices_chan // 2
        for step in range(1, groups):
            there = lax.rem(chan // 2 + step, groups) * 2 + chan % 2
            pl.semaphore_signal(barrier, inc=1, device_id=(seq, there), device_id_type=MESH)
        pl.semaphore_signal(
            barrier, inc=1, device_id=(seq, chan + 1 - 2 * (chan % 2)), device_id_type=MESH
        )
        count += groups
    pl.semaphore_wait(barrier, count)


def gather_kernel(
    devices_seq,
    devices_chan,
    tokens,
    grads,
    weights,
    tokens_out,
    grads_out,
    projected,
    upstream,
    all_tokens,
    all_grads,
    all_weights,
    keep_sem,
    store_sem,
    chan_send,
    chan_recv,
    chan_pass,
    chan_passed,
    seq_send,
    seq_recv,
    seq_pass,
    seq_passed,
):
    seq, chan = lax.axis_index("seq"), lax.axis_index("chan")
    seq_groups, chan_groups = devices_seq // 2, devices_chan // 2
    seq_pair = (seq + 1 - 2 * (seq % 2), chan)
    chan_pair = (seq, chan + 1 - 2 * (chan % 2))
    columns = tokens.shape[1]
    rows = weights.shape[0]
    greet(devices_seq, devices_chan, "pairs")

    def block(ref, lines, index):
        return ref.at[lines, pl.ds(pl.multiple_of(index * columns, columns), columns)]

    def piece(index):
        return all_weights.at[pl.ds(pl.multiple_of(index * rows, rows), rows)]

    def chan_member(step, parity):
        return lax.rem(chan // 2 - step + chan_groups, chan_groups) * 2 + parity

    def seq_member(step, parity):
        return lax.rem(seq // 2 - step + seq_groups, seq_groups) * 2 + parity

    height = tokens.shape[0] // 2
    parts = [
        (own, whole, out, pl.ds(half * height, height))
        for own, whole, out in ((tokens, all_tokens, tokens_out), (grads, all_grads, grads_out))
        for half in range(2)
    ]

    def chan_copy(array, step):
        own, whole, _, lines = parts[array]
        there = lax.rem(chan // 2 + step, chan_groups) * 2 + chan % 2
        return remote(
            own.at[lines],
            block(whole, lines, chan),
            chan_send.at[array, step],
            chan_recv.at[array, step],
            (seq, there),
        )

    def chan_forward(array, step):
        own, whole, _, lines = parts[array]
        here = chan_member(step, chan % 2)
        return remote(
            own.at[lines] if step == 0 else block(whole, lines, here),
            block(whole, lines, here),
            chan_pass.at[array, step],
            chan_passed.at[array, step],
            chan_pair,
        )

    def seq_copy(step):
        there = lax.rem(seq // 2 + step, seq_groups) * 2 + seq % 2
        return remote(weights, piece(seq), seq_send.at[step], seq_recv.at[step], (there, chan))

    def seq_forward(step):
        here = seq_member(step, seq % 2)
        return remote(piece(here), piece(here), seq_pass.at[step], seq_passed.at[step], seq_pair)

    own_piece = remote(weights, piece(seq), seq_pass.at[0], seq_passed.at[0], seq_pair)

    def each(call):
        def body(step, carry):
            call(step)
            return carry

        lax.fori_loop(1, seq_groups, body, 0)

    def store(array):
        _, whole, out, lines = parts[array]
        return pltpu.make_async_copy(whole.at[lines], out.at[lines], store_sem.at[array])

    for array in range(4):
        for step in range(1, chan_groups):
            chan_copy(array, step).start()
    each(lambda step: seq_copy(step).start())
    own_piece.start()
    for array in range(4):
        chan_forward(array, 0).start()
    keeps = [pltpu.make_async_copy(weights, piece(seq), keep_sem.at[4])]
    for array, (own, whole, _, lines) in enumerate(parts):
        keeps.append(
            pltpu.make_async_copy(own.at[lines], block(whole, lines, chan), keep_sem.at[array])
        )
    for keep in keeps:
        keep.start()

    def pass_on(step):
        seq_copy(step).wait_recv()
        seq_forward(step).start()

    def pass_part(array):
        for step in range(1, chan_groups):
            chan_copy(array, step).wait_recv()
            chan_forward(array, step).start()

    pass_part(0)
    each(pass_on)
    for keep in keeps:
        keep.wait()
    own_piece.wait()

    def finish(step):
        seq_copy(step).wait_send()
        seq_forward(step).wait()

    each(finish)
    tile = math.gcd(height, 128)
    for array, (_, whole, _, lines) in enumerate(parts):
        if array + 1 < len(parts):
            pass_part(array + 1)
        for step in range(chan_groups):
            chan_forward(array, step).wait()
        store(array).start()
        target, first = (projected, 0) if array < 2 else (upstream, all_weights.shape[1] // 2)

        def product(index, carry):
            here = pl.ds(pl.multiple_of(array % 2 * height + index * tile, tile), tile)
            target[here] = jnp.dot(
                whole[here], all_weights[:, first:], preferred_element_type=jnp.float32
            )
            return carry

        lax.fori_loop(0, height // tile, product, 0)
    for array in range(4):
        store(array).wait()
        for step in range(1, chan_groups):
            chan_copy(array, step).wait_send()


def gathered(tokens, grads, weights):
    devices_seq, devices_chan = lax.axis_size("seq"), lax.axis_size("chan")
    dma = pltpu.SemaphoreType.DMA
    seq_groups, chan_groups = devices_seq // 2, devices_chan // 2
    vmem, anywhere = pl.BlockSpec(memory_space=pltpu.VMEM), pl.BlockSpec(memory_space=pl.ANY)
    wide = jax.ShapeDtypeStruct((tokens.shape[0], tokens.shape[1] * devices_chan), tokens.dtype)
    tall = jax.ShapeDtypeStruct((weights.shape[0] * devices_seq, weights.shape[1]), weights.dtype)
    return pl.pallas_call(
        functools.partial(gather_kernel, devices_seq, devices_chan),
        out_shape=(
            wide,
            wide,
            jax.ShapeDtypeStruct((tokens.shape[0], weights.shape[1]), jnp.float32),
            jax.ShapeDtypeStruct((tokens.shape[0], weights.shape[1] // 2), jnp.float32),
        ),
        in_specs=[vmem] * 3,
        out_specs=(anywhere, anywhere, vmem, vmem),
        scratch_shapes=[
            pltpu.VMEM(wide.shape, wide.dtype),
            pltpu.VMEM(wide.shape, wide.dtype),
            pltpu.VMEM(tall.shape, tall.dtype),
            dma((5,)),
            dma((4,)),
        ]
        + [dma((4, chan_groups))] * 4
        + [dma((seq_groups,))] * 4,
        compiler_params=pltpu.CompilerParams(collective_id=0, has_side_effects=True),
        name="gather_inputs",
    )(tokens, grads, weights)


def reduce_kernel(
    devices_seq,
    tile,
    state,
    rate,
    weight,
    inner,
    value,
    gate,
    early_in,
    early_out,
    tokens_hbm,
    grads_hbm,
    total,
    tokens,
    grads,
    states,
    late,
    parts,
    near,
    paired,
    far,
    load_sem,
    state_send,
    state_recv,
    pair_send,
    pair_recv,
    far_send,
    far_recv,
):
    seq, chan = lax.axis_index("seq"), lax.axis_index("chan")
    groups = devices_seq // 2
    group, parity = seq // 2, seq % 2
    rows, channels = inner.shape
    owned = near.shape[2]
    loads = [
        pltpu.make_async_copy(tokens_hbm, tokens, load_sem.at[0]),
        pltpu.make_async_copy(grads_hbm, grads, load_sem.at[1]),
    ]
    for load in loads:
        load.start()
    greet(devices_seq, 0, "all")

    def loop(start, stop, call):
        def body(step, carry):
            call(step)
            return carry

        lax.fori_loop(start, stop, body, 0)

    def state_copy(step):
        there = lax.rem(seq + step, devices_seq)
        return remote(
            state, states.at[step], state_send.at[step], state_recv.at[step], (there, chan)
        )

    def member(step):
        return lax.rem(group + step, groups)

    def piece(half, index):
        return parts.at[half, pl.ds(pl.multiple_of(index * owned, owned), owned)]

    def pair_copy(half, step):
        return remote(
            piece(half, member(step) * 2 + 1 - parity),
            near.at[half, step],
            pair_send.at[half, step],
            pair_recv.at[half, step],
            (group * 2 + 1 - parity, chan),
        )

    def far_copy(half, step):
        return remote(
            paired.at[half, step],
            far.at[half, step],
            far_send.at[half, step],
            far_recv.at[half, step],
            (member(step) * 2 + parity, chan),
        )

    def summed(left, right):
        return lax.dot_general(
            left, right, (((0,), (0,)), ((), ())), preferred_element_type=jnp.float32
        )

    def span(index):
        return pl.ds(pl.multiple_of(index * tile, tile), tile)

    loop(1, devices_seq, lambda step: state_copy(step).start())
    for load in loads:
        load.wait()

    def early_tile(index):
        product = summed(tokens[:, span(index)], early_in[...])
        product += summed(grads[:, span(index)], early_out[...])
        parts[0, span(index)] = product.astype(parts.dtype)

    loop(0, tokens.shape[1] // tile, early_tile)
    loop(1, groups, lambda step: pair_copy(0, step).start())
    pair_copy(0, 0).start()

    def absorb(step, following):
        state_copy(step).wait_recv()
        gap = lax.rem(seq - step + devices_seq, devices_seq) - seq - 1
        reach = (jnp.maximum(gap, 0) * rows).astype(jnp.float32)
        present = (gap >= 0).astype(jnp.float32)
        return following + present * states[step] * jnp.exp(-reach * rate[...])

    following = lax.fori_loop(1, devices_seq, absorb, jnp.zeros(rate.shape, jnp.float32))
    entering = weight[...] * following
    rates = rate[...]
    band = math.gcd(rows, 64)

    def source_rows(index):
        here = pl.ds(pl.multiple_of(index * band, band), band)
        position = lax.broadcasted_iota(jnp.int32, (band, channels), 0) + index * band
        reach = (rows - position).astype(jnp.float32)
        source = inner[here]
        for mode in range(rates.shape[0]):
            source += entering[mode : mode + 1] * jnp.exp(-reach * rates[mode : mode + 1])
        late[here] = jnp.concatenate([source * value[here], source * gate[here]], axis=1).astype(
            late.dtype
        )

    loop(0, rows // band, source_rows)

    def late_tile(index):
        parts[1, span(index)] = summed(tokens[:, span(index)], late[...]).astype(parts.dtype)

    loop(0, tokens.shape[1] // tile, late_tile)
    loop(1, groups, lambda step: pair_copy(1, step).start())
    pair_copy(1, 0).start()

    def pair_sum(half, step):
        own = piece(half, member(step) * 2 + parity)[...].astype(jnp.float32)
        return own + near[half, step].astype(jnp.float32)

    for half in range(2):

        def pass_on(step):
            pair_copy(half, step).wait_recv()
            paired[half, step] = pair_sum(half, step).astype(paired.dtype)
            far_copy(half, step).start()

        loop(1, groups, pass_on)
    for half in range(2):
        pair_copy(half, 0).wait_recv()
        total[half] = pair_sum(half, 0)

        def collect(step):
            far_copy(half, step).wait_recv()
            total[half] += far[half, step].astype(jnp.float32)

        loop(1, groups, collect)

        def finish(step):
            pair_copy(half, step).wait_send()
            far_copy(half, step).wait_send()

        loop(1, groups, finish)
        pair_copy(half, 0).wait_send()
    loop(1, devices_seq, lambda step: state_copy(step).wait_send())


def reduced(state, rate, weight, inner, value, gate, early_in, early_out, tokens, grads, owned):
    devices_seq = lax.axis_size("seq")
    groups = devices_seq // 2
    rows, channels = inner.shape
    width = tokens.shape[1]
    wide = 2 * channels
    vmem, anywhere = pl.BlockSpec(memory_space=pltpu.VMEM), pl.BlockSpec(memory_space=pl.ANY)
    dma, half_type = pltpu.SemaphoreType.DMA, tokens.dtype
    return pl.pallas_call(
        functools.partial(reduce_kernel, devices_seq, math.gcd(width, 512)),
        out_shape=jax.ShapeDtypeStruct((2, owned, wide), jnp.float32),
        in_specs=[vmem] * 8 + [anywhere] * 2,
        out_specs=vmem,
        scratch_shapes=[pltpu.VMEM(tokens.shape, half_type)] * 2
        + [pltpu.VMEM((devices_seq,) + state.shape, jnp.float32)]
        + [pltpu.VMEM((rows, wide), half_type), pltpu.VMEM((2, width, wide), half_type)]
        + [pltpu.VMEM((2, groups, owned, wide), half_type)] * 3
        + [dma((2,)), dma((devices_seq,)), dma((devices_seq,))]
        + [dma((2, groups))] * 4,
        compiler_params=pltpu.CompilerParams(collective_id=1, has_side_effects=True),
        name="reduce_owned",
    )(state, rate, weight, inner, value, gate, early_in, early_out, tokens, grads)


def correlate_block(signal, residues, decay_length):
    rows, channels = signal.shape
    chunk = min(64, rows)
    chunks = rows // chunk
    per_filter = channels // residues.shape[1]
    rate = jnp.repeat(1.0 / decay_length, per_filter, axis=1)
    weight = jnp.repeat(residues, per_filter, axis=1) * jnp.sqrt(-jnp.expm1(-2.0 * rate))
    offset = jnp.arange(chunk, dtype=jnp.float32)
    exponent = rate.T[:, :, None] * offset
    grow = weight.T[:, :, None] * jnp.exp(exponent)
    fall = jnp.exp(-exponent)
    later = jnp.arange(chunk)[None, :] >= jnp.arange(chunk)[:, None]
    taps = jnp.einsum("cri,crj->cij", grow, fall, precision=precise)
    taps = jnp.where(later, taps, 0.0)
    pieces = signal.reshape(chunks, chunk, channels).transpose(2, 1, 0)
    both = jnp.einsum(
        "cij,cjn->cin", jnp.concatenate([taps, fall], axis=1), pieces, precision=precise
    )
    inner, sums = both[:, :chunk], both[:, chunk:]
    step = jnp.exp(-chunk * rate).T
    state = jnp.zeros_like(step)
    entering = []
    for index in reversed(range(chunks)):
        entering.append(step * state)
        state = sums[:, :, index] + step * state
    entering = jnp.stack(entering[::-1], axis=2)
    outer = jnp.einsum("cri,crn->cin", grow, entering, precision=precise)
    return (inner + outer).transpose(2, 1, 0).reshape(rows, channels), state.T, rate, weight


def block_kernel(
    devices_seq,
    devices_chan,
    tokens_hbm,
    grads_hbm,
    in_weight,
    out_weight,
    conv_hbm,
    residues,
    decay_length,
    grad_in,
    grad_out,
    tokens,
    grads,
    conv,
    pieces,
    weights,
    partial,
    pair_in,
    chip_sum,
    far_in,
    signal,
    consts,
    bank,
    own_state,
    states,
    flows,
    parts,
    near,
    summed,
    blocks,
    arrived,
    load_sem,
    hop_send,
    hop_recv,
    swap_send,
    swap_recv,
    keep_sem,
    twin_send,
    twin_recv,
    pair_send,
    pair_recv,
    far_send,
    far_recv,
    state_send,
    state_recv,
    flow_send,
    flow_recv,
    pass_send,
    pass_recv,
    near_send,
    near_recv,
    turn_send,
    turn_recv,
    home_send,
    home_recv,
):
    seq, chan = lax.axis_index("seq"), lax.axis_index("chan")
    planes = devices_chan
    twins = devices_seq // planes
    groups = devices_chan // 2
    plane, twin = seq // twins, seq % twins
    group, parity = chan // 2, chan % 2
    partner = (seq, chan + 1 - 2 * parity)
    channels, rows = conv.shape
    owned = out_weight.shape[1]

    def ahead(index, step, count):
        return lax.rem(index + step, count)

    def behind(index, step, count):
        return lax.rem(index - step + count, count)

    names = (
        (in_weight.at[1], out_weight),
        (in_weight.at[0], in_weight.at[2]),
    )
    weight_loads = [
        [
            pltpu.make_async_copy(names[half][j], pieces.at[half, plane, j], load_sem.at[2 * half + j])
            for j in range(2)
        ]
        for half in range(2)
    ]
    bulk_loads = [
        pltpu.make_async_copy(tokens_hbm, tokens, load_sem.at[4]),
        pltpu.make_async_copy(grads_hbm, grads, load_sem.at[5]),
        pltpu.make_async_copy(conv_hbm, conv, load_sem.at[6]),
    ]
    for half in range(2):
        for load in weight_loads[half]:
            load.start()
    for load in bulk_loads:
        load.start()

    barrier = pltpu.get_barrier_semaphore()
    for step in range(1, devices_seq):
        pl.semaphore_signal(
            barrier, inc=1, device_id=(ahead(seq, step, devices_seq), chan), device_id_type=MESH
        )
    for step in range(1, devices_chan):
        pl.semaphore_signal(
            barrier, inc=1, device_id=(seq, ahead(chan, step, devices_chan)), device_id_type=MESH
        )
    pl.semaphore_wait(barrier, devices_seq + devices_chan - 2)

    def hop(half, step):
        return remote(
            pieces.at[half, plane],
            pieces.at[half, plane],
            hop_send.at[half, step],
            hop_recv.at[half, step],
            (ahead(plane, step, planes) * twins + twin, chan),
        )

    def hop_in(half, step):
        source = behind(plane, step, planes)
        return remote(
            pieces.at[half, source],
            pieces.at[half, source],
            hop_send.at[half, step],
            hop_recv.at[half, step],
            (source * twins + twin, chan),
        )

    def swap(half, target):
        return remote(
            pieces.at[half, target],
            weights.at[half, twin, :, chan],
            swap_send.at[half, target],
            swap_recv.at[half, chan],
            (seq, target),
        )

    def swap_in(half, source):
        return remote(
            pieces.at[half, chan],
            weights.at[half, twin, :, source],
            swap_send.at[half, source],
            swap_recv.at[half, source],
            (seq, source),
        )

    def keep(half):
        return pltpu.make_async_copy(
            pieces.at[half, chan], weights.at[half, twin, :, chan], keep_sem.at[half]
        )

    def twin_copy(half, source, step):
        return remote(
            weights.at[half, twin, :, source],
            weights.at[half, twin, :, source],
            twin_send.at[half, source, step],
            twin_recv.at[half, source, step],
            (plane * twins + ahead(twin, step, twins), chan),
        )

    def twin_in(half, source, step):
        there = behind(twin, step, twins)
        return remote(
            weights.at[half, there, :, source],
            weights.at[half, there, :, source],
            twin_send.at[half, source, step],
            twin_recv.at[half, source, step],
            (plane * twins + there, chan),
        )

    def send_on(half, step):
        target = behind(plane, step, planes)
        if step:
            hop_in(half, step).wait_recv()

        @pl.when(target == chan)
        def _():
            keep(half).start()

        @pl.when(target != chan)
        def _():
            swap(half, target).start()

    def share(half):
        for index in range(1, devices_chan + 1):
            source = ahead(chan, index, devices_chan)
            if index < devices_chan:
                swap_in(half, source).wait_recv()
            else:
                keep(half).wait()
            for step in range(1, twins):
                twin_copy(half, source, step).start()

    for half in range(2):
        for load in weight_loads[half]:
            load.wait()
        for step in range(1, planes):
            hop(half, step).start()

    lanes = signal.shape[1]
    folds = lanes // channels
    groups_of_rows = 8
    span = signal.shape[0] // groups_of_rows
    modes, filters = residues.shape
    per_filter = channels // filters
    lane = lax.broadcasted_iota(jnp.int32, (filters, lanes), 1)
    which = lax.broadcasted_iota(jnp.int32, (filters, lanes), 0)
    spread = (lax.rem(lane, channels) // per_filter == which).astype(jnp.float32)
    inverse = 1.0 / decay_length[...]
    twice = 2.0 * inverse
    series = jnp.zeros_like(twice)
    for order in range(10, 0, -1):
        series = (1.0 - series) * twice / order
    loss = jnp.where(twice < 0.5, series, 1.0 - jnp.exp(-twice))
    scale = residues[...] * jnp.sqrt(loss)

    def widen(array):
        return jnp.dot(array, spread, precision=precise, preferred_element_type=jnp.float32)

    rate = widen(inverse)
    consts[0] = rate
    consts[1] = widen(scale)
    consts[2] = jnp.exp(-rate)

    def mixed(half, j):
        return grads if (half, j) == (0, 1) else tokens

    def project(half):
        for step in range(twins):
            block = ahead(twin, step, twins)
            if step:
                for source in range(devices_chan):
                    twin_in(half, source, step).wait_recv()
            columns = pl.ds(pl.multiple_of(block * owned, owned), owned)
            for j in range(2):
                product = lax.dot_general(
                    weights[half, block, j].reshape(devices_chan * channels, owned),
                    mixed(half, j)[:, columns],
                    (((1,), (1,)), ((), ())),
                    preferred_element_type=jnp.float32,
                )
                for target in range(devices_chan):
                    piece = product[target * channels : (target + 1) * channels]
                    place = (half, target % 2, target // 2, j)
                    if step:
                        piece = partial[place] + piece
                    partial[place] = piece

    def pair_copy(half, there):
        return remote(
            partial.at[half, 1 - parity, there],
            pair_in.at[half, there],
            pair_send.at[half, there],
            pair_recv.at[half, there],
            partner,
        )

    def far_copy(half, step):
        return remote(
            chip_sum.at[half, step],
            far_in.at[half, step],
            far_send.at[half, step],
            far_recv.at[half, step],
            (seq, ahead(group, step, groups) * 2 + parity),
        )

    def pair_start(half):
        for step in range(1, groups + 1):
            pair_copy(half, ahead(group, step, groups)).start()

    def far_start(half):
        for step in range(1, groups):
            there = ahead(group, step, groups)
            pair_copy(half, there).wait_recv()
            chip_sum[half, step] = partial[half, parity, there] + pair_in[half, there]
            far_copy(half, step).start()

    def far_finish(half):
        pair_copy(half, group).wait_recv()
        total = partial[half, parity, group] + pair_in[half, group]
        for step in range(1, groups):
            far_copy(half, step).wait_recv()
            total = total + far_in[half, step]
        return total

    def flow(half, step):
        return remote(
            flows.at[half, :, chan],
            flows.at[half, :, chan],
            flow_send.at[half, step],
            flow_recv.at[half, step],
            (seq, ahead(group, step, groups) * 2 + parity),
        )

    def flow_in(half, step):
        source = behind(group, step, groups) * 2 + parity
        return remote(
            flows.at[half, :, source],
            flows.at[half, :, source],
            flow_send.at[half, step],
            flow_recv.at[half, step],
            (seq, source),
        )

    def flow_pass(half, step):
        source = behind(group, step, groups) * 2 + parity
        return remote(
            flows.at[half, :, source],
            flows.at[half, :, source],
            pass_send.at[half, step],
            pass_recv.at[half, step],
            partner,
        )

    def flow_passed(half, step):
        source = behind(group, step, groups) * 2 + 1 - parity
        return remote(
            flows.at[half, :, source],
            flows.at[half, :, source],
            pass_send.at[half, step],
            pass_recv.at[half, step],
            partner,
        )

    def flow_start(half):
        for step in range(1, groups):
            flow(half, step).start()
        flow_pass(half, 0).start()

    def flow_on(half):
        for step in range(1, groups):
            flow_in(half, step).wait_recv()
            flow_pass(half, step).start()

    def flow_finish(half):
        for step in range(groups):
            flow_passed(half, step).wait_recv()

    def near_copy(half, step, target):
        return remote(
            parts.at[half, ahead(twin, step, twins), target],
            near.at[half, step, target],
            near_send.at[half, step, target],
            near_recv.at[half, step, target],
            (plane * twins + ahead(twin, step, twins), chan),
        )

    def multiply(half):
        for step in range(1, twins + 1):
            block = ahead(twin, step, twins)
            columns = pl.ds(pl.multiple_of(block * owned, owned), owned)
            for j in range(2):
                product = jnp.dot(
                    flows[half, j].reshape(devices_chan * channels, rows),
                    mixed(half, j)[:, columns],
                    preferred_element_type=jnp.float32,
                ).astype(parts.dtype)
                for target in range(devices_chan):
                    parts[half, block, target, j] = product[
                        target * channels : (target + 1) * channels
                    ]
            if step < twins:
                for index in range(1, devices_chan + 1):
                    near_copy(half, step, ahead(chan, index, devices_chan)).start()

    def turn(half, target):
        return remote(
            summed.at[half, target],
            blocks.at[half, chan],
            turn_send.at[half, target],
            turn_recv.at[half, chan],
            (seq, target),
        )

    def turn_in(half, source):
        return remote(
            summed.at[half, source],
            blocks.at[half, source],
            turn_send.at[half, source],
            turn_recv.at[half, source],
            (seq, source),
        )

    def home(half, target):
        return remote(
            blocks.at[half, target],
            arrived.at[half, plane],
            home_send.at[half, target],
            home_recv.at[half, plane],
            (target * twins + twin, chan),
        )

    def home_in(half, source):
        return remote(
            blocks.at[half, source],
            arrived.at[half, source],
            home_send.at[half, source],
            home_recv.at[half, source],
            (source * twins + twin, chan),
        )

    def turn_start(half):
        for index in range(1, devices_chan + 1):
            target = ahead(chan, index, devices_chan)
            total = parts[half, twin, target].astype(jnp.float32)
            for step in range(1, twins):
                near_copy(half, step, target).wait_recv()
                total = total + near[half, step, target].astype(jnp.float32)
            total = total.astype(blocks.dtype)
            if index < devices_chan:
                summed[half, target] = total
                turn(half, target).start()
            else:
                blocks[half, chan] = total

    def home_start(half):
        for index in range(devices_chan):
            source = behind(chan, index, devices_chan)
            if index:
                turn_in(half, source).wait_recv()

            @pl.when(source != plane)
            def _():
                home(half, source).start()

    def home_finish(half):
        total = blocks[half, plane].astype(jnp.float32)
        for step in range(1, planes):
            source = behind(plane, step, planes)
            home_in(half, source).wait_recv()
            total = total + arrived[half, source].astype(jnp.float32)
        return total

    def rowed(array):
        width = array.shape[1] // folds
        stacked = jnp.concatenate(
            [array[:, fold * width : (fold + 1) * width] for fold in range(folds)], axis=0
        )
        return stacked.T

    def unrowed(array):
        stacked = array.T
        return jnp.concatenate(
            [stacked[fold * channels : (fold + 1) * channels] for fold in range(folds)], axis=1
        )

    def mode_row(kind, mode):
        return jnp.broadcast_to(consts[kind, mode : mode + 1], (groups_of_rows, lanes))

    def line(index):
        return pl.ds(index, groups_of_rows, stride=span)

    def scan_states():
        fall = [mode_row(2, mode) for mode in range(modes)]

        def body(step, carry):
            here = signal[line(span - 1 - step)]
            return tuple(carry[mode] * fall[mode] + here for mode in range(modes))

        zero = jnp.zeros((groups_of_rows, lanes), jnp.float32)
        found = lax.fori_loop(0, span, body, (zero,) * modes)
        position = lax.broadcasted_iota(jnp.int32, (groups_of_rows, lanes), 0)
        for mode in range(modes):
            each = mode_row(0, mode) * span
            total = found[mode]
            shift = 1
            while shift < groups_of_rows:
                moved = pltpu.roll(total, groups_of_rows - shift, 0)
                moved = moved * jnp.exp(-each * shift)
                total = total + jnp.where(position < groups_of_rows - shift, moved, 0.0)
                shift *= 2
            moved = pltpu.roll(total, groups_of_rows - 1, 0)
            bank[mode] = jnp.where(position < groups_of_rows - 1, moved, 0.0)
            own_state[mode : mode + 1] = total[0:1]
        heads = own_state[...]
        reach = consts[0] * (span * groups_of_rows)
        later = pltpu.roll(heads, channels, 1)
        first = lax.broadcasted_iota(jnp.int32, (modes, lanes), 1) < channels
        consts[3] = jnp.where(first, later, 0.0)
        own_state[...] = jnp.where(first, heads + later * jnp.exp(-reach), 0.0)

    def state_copy(step):
        return remote(
            own_state,
            states.at[step],
            state_send.at[step],
            state_recv.at[step],
            (ahead(seq, step, devices_seq), chan),
        )

    def scan_source():
        rates = consts[0]
        following = jnp.zeros((modes, lanes), jnp.float32)
        for step in range(1, devices_seq):
            state_copy(step).wait_recv()
            gap = behind(seq, step, devices_seq) - seq - 1
            reach = (jnp.maximum(gap, 0) * rows).astype(jnp.float32)
            present = (gap >= 0).astype(jnp.float32)
            following = following + present * states[step] * jnp.exp(-reach * rates)
        first = lax.broadcasted_iota(jnp.int32, (modes, lanes), 1) < channels
        after = pltpu.roll(following, channels, 1)
        within = following * jnp.exp(-(rates * (span * groups_of_rows)))
        consts[3] = jnp.where(first, consts[3] + within, after)
        fall = [mode_row(2, mode) for mode in range(modes)]
        weigh = [mode_row(1, mode) for mode in range(modes)]
        position = lax.broadcasted_iota(jnp.int32, (groups_of_rows, lanes), 0)
        left = ((groups_of_rows - 1 - position) * span).astype(jnp.float32)
        start = tuple(
            bank[mode] + mode_row(3, mode) * jnp.exp(-left * mode_row(0, mode))
            for mode in range(modes)
        )

        def body(step, carry):
            here = line(span - 1 - step)
            entry = signal[here]
            following = tuple(carry[mode] * fall[mode] + entry for mode in range(modes))
            terms = [following[mode] * weigh[mode] for mode in range(modes)]
            while len(terms) > 1:
                terms = [sum(terms[at : at + 2]) for at in range(0, len(terms), 2)]
            signal[here] = terms[0]
            return following

        lax.fori_loop(0, span, body, start)

    for step in range(planes):
        send_on(0, step)
    share(0)
    send_on(1, 0)
    send_on(1, 1)
    for load in bulk_loads:
        load.wait()
    project(0)
    pair_start(0)
    for step in range(2, planes):
        send_on(1, step)
    far_start(0)
    share(1)

    early = far_finish(0)
    second = early[0].astype(flows.dtype).astype(jnp.float32)
    upstream = early[1]
    taken = conv[...].astype(jnp.float32)
    flows[0, 0, chan] = (upstream * taken).astype(flows.dtype)
    flows[0, 1, chan] = (second * taken).astype(flows.dtype)
    flow_start(0)
    signal[...] = rowed(upstream * second)
    scan_states()
    for step in range(1, devices_seq):
        state_copy(step).start()
    project(1)
    pair_start(1)
    flow_on(0)
    far_start(1)
    flow_finish(0)
    multiply(0)
    scan_source()
    source = unrowed(signal[...])
    late = far_finish(1).astype(flows.dtype).astype(jnp.float32)
    flows[1, 0, chan] = (source * late[1]).astype(flows.dtype)
    flows[1, 1, chan] = (source * late[0]).astype(flows.dtype)
    flow_start(1)
    turn_start(0)
    flow_on(1)
    flow_finish(1)
    multiply(1)
    home_start(0)
    turn_start(1)
    home_start(1)
    for half in range(2):
        total = home_finish(half)
        if half == 0:
            grad_in[1] = total[0]
            grad_out[...] = total[1]
        else:
            grad_in[0] = total[0]
            grad_in[2] = total[1]

    for half in range(2):
        for step in range(1, planes):
            hop(half, step).wait_send()
        for index in range(1, devices_chan):
            target = ahead(chan, index, devices_chan)
            swap(half, target).wait_send()
            turn(half, target).wait_send()
        for source in range(devices_chan):
            for step in range(1, twins):
                twin_copy(half, source, step).wait_send()
                near_copy(half, step, source).wait_send()
        for there in range(groups):
            pair_copy(half, there).wait_send()
        for step in range(1, groups):
            far_copy(half, step).wait_send()
            flow(half, step).wait_send()
        for step in range(groups):
            flow_pass(half, step).wait_send()
        for step in range(1, planes):
            home(half, ahead(plane, step, planes)).wait_send()
    for step in range(1, devices_seq):
        state_copy(step).wait_send()


def fits(tokens, conv_out, in_weight, residues):
    devices_seq, devices_chan = lax.axis_size("seq"), lax.axis_size("chan")
    rows, channels = conv_out.shape
    return (
        devices_chan % 2 == 0
        and devices_seq % devices_chan == 0
        and devices_seq > devices_chan
        and in_weight.shape[0] % 128 == 0
        and 2 * channels == 128
        and channels % residues.shape[1] == 0
        and rows % 256 == 0
        and tokens.shape[1] * devices_chan == in_weight.shape[0] * devices_seq
    )


def blocked(tokens, grad_out, in_weight, out_weight, conv_out, residues, decay_length):
    devices_seq, devices_chan = lax.axis_size("seq"), lax.axis_size("chan")
    planes, groups = devices_chan, devices_chan // 2
    twins = devices_seq // planes
    rows, width = tokens.shape
    channels, owned = out_weight.shape[1], out_weight.shape[0]
    modes = residues.shape[0]
    vmem, anywhere = pl.BlockSpec(memory_space=pltpu.VMEM), pl.BlockSpec(memory_space=pl.ANY)
    dma, half_type, full = pltpu.SemaphoreType.DMA, tokens.dtype, jnp.float32
    lanes = 2 * channels
    grad_in, grad_proj = pl.pallas_call(
        functools.partial(block_kernel, devices_seq, devices_chan),
        out_shape=(
            jax.ShapeDtypeStruct((3, channels, owned), full),
            jax.ShapeDtypeStruct((channels, owned), full),
        ),
        in_specs=[anywhere] * 5 + [vmem] * 2,
        out_specs=(vmem, vmem),
        scratch_shapes=[
            pltpu.VMEM((rows, width), half_type),
            pltpu.VMEM((rows, width), half_type),
            pltpu.VMEM((channels, rows), half_type),
            pltpu.VMEM((2, planes, 2, channels, owned), half_type),
            pltpu.VMEM((2, twins, 2, devices_chan, channels, owned), half_type),
            pltpu.VMEM((2, 2, groups, 2, channels, rows), full),
            pltpu.VMEM((2, groups, 2, channels, rows), full),
            pltpu.VMEM((2, groups, 2, channels, rows), full),
            pltpu.VMEM((2, groups, 2, channels, rows), full),
            pltpu.VMEM((rows * channels // lanes, lanes), full),
            pltpu.VMEM((4, modes, lanes), full),
            pltpu.VMEM((modes, 8, lanes), full),
            pltpu.VMEM((modes, lanes), full),
            pltpu.VMEM((devices_seq, modes, lanes), full),
            pltpu.VMEM((2, 2, devices_chan, channels, rows), half_type),
            pltpu.VMEM((2, twins, devices_chan, 2, channels, owned), half_type),
            pltpu.VMEM((2, twins, devices_chan, 2, channels, owned), half_type),
            pltpu.VMEM((2, devices_chan, 2, channels, owned), half_type),
            pltpu.VMEM((2, planes, 2, channels, owned), half_type),
            pltpu.VMEM((2, planes, 2, channels, owned), half_type),
            dma((7,)),
        ]
        + [dma((2, planes))] * 4
        + [dma((2,))]
        + [dma((2, devices_chan, twins))] * 2
        + [dma((2, groups))] * 4
        + [dma((devices_seq,))] * 2
        + [dma((2, groups))] * 4
        + [dma((2, twins, devices_chan))] * 2
        + [dma((2, planes))] * 4,
        compiler_params=pltpu.CompilerParams(collective_id=2, has_side_effects=True),
        name="conv_block",
    )(
        tokens,
        grad_out,
        in_weight.transpose(1, 2, 0),
        out_weight.T,
        conv_out.T,
        residues,
        decay_length,
    )
    return grad_in.transpose(2, 0, 1), grad_proj.T


def local(tokens, grad_out, in_weight, out_weight, conv_out, residues, decay_length):
    if fits(tokens, conv_out, in_weight, residues):
        return blocked(tokens, grad_out, in_weight, out_weight, conv_out, residues, decay_length)
    channels = out_weight.shape[1]
    owned_rows = in_weight.shape[0]
    weights = jnp.concatenate([in_weight.reshape(owned_rows, 3 * channels), out_weight], axis=1)
    full_tokens, full_grads, projected, upstream = gathered(tokens, grad_out, weights)
    projected = projected[:, : 3 * channels]
    upstream = upstream[:, channels:]
    streams = lax.reduce_precision(projected, exponent_bits=8, mantissa_bits=7)
    gate_first = streams[:, :channels]
    gate_second = streams[:, channels : 2 * channels]
    value_stream = streams[:, 2 * channels :]
    conv_value = conv_out.astype(jnp.float32)
    gated = (gate_second * conv_value).astype(jnp.bfloat16)
    grad_second = (upstream * conv_value).astype(jnp.bfloat16)
    grad_conv = upstream * gate_second
    inner, state, rate, weight = correlate_block(grad_conv, residues, decay_length)
    blank = jnp.zeros_like(gated)
    owned = reduced(
        state,
        rate,
        weight,
        inner,
        value_stream,
        gate_first,
        jnp.concatenate([grad_second, blank], axis=1),
        jnp.concatenate([blank, gated], axis=1),
        full_tokens,
        full_grads,
        owned_rows,
    )
    grad_in = jnp.stack(
        [owned[1, :, :channels], owned[0, :, :channels], owned[1, :, channels:]], axis=1
    )
    return (grad_in, owned[0, :, channels:])


def solution(mesh):
    return jax.shard_map(
        local,
        mesh=mesh,
        in_specs=(
            P("seq", "chan"),
            P("seq", "chan"),
            P("seq", None, "chan"),
            P("seq", "chan"),
            P("seq", "chan"),
            P(None, "chan"),
            P(None, "chan"),
        ),
        out_specs=(P("seq", None, "chan"), P("seq", "chan")),
        check_vma=False,
    )
```

```python
import functools
import math

import jax
import jax.numpy as jnp
from jax import lax
from jax.experimental import pallas as pl
from jax.experimental.pallas import tpu as pltpu
from jax.sharding import PartitionSpec as P

precise = lax.Precision.HIGHEST
MESH = pl.DeviceIdType.MESH


def remote(source, target, send_sem, recv_sem, device):
    return pltpu.make_async_remote_copy(
        src_ref=source,
        dst_ref=target,
        send_sem=send_sem,
        recv_sem=recv_sem,
        device_id=device,
        device_id_type=MESH,
    )


def greet(devices_seq, devices_chan, seq_wide):
    seq, chan = lax.axis_index("seq"), lax.axis_index("chan")
    barrier = pltpu.get_barrier_semaphore()
    count = 0
    if seq_wide == "all":

        def hello(step, carry):
            pl.semaphore_signal(
                barrier,
                inc=1,
                device_id=(lax.rem(seq + step, devices_seq), chan),
                device_id_type=MESH,
            )
            return carry

        lax.fori_loop(1, devices_seq, hello, 0)
        count += devices_seq - 1
    else:
        groups = devices_seq // 2

        def hello_group(step, carry):
            there = lax.rem(seq // 2 + step, groups) * 2 + seq % 2
            pl.semaphore_signal(barrier, inc=1, device_id=(there, chan), device_id_type=MESH)
            return carry

        lax.fori_loop(1, groups, hello_group, 0)
        pl.semaphore_signal(
            barrier, inc=1, device_id=(seq + 1 - 2 * (seq % 2), chan), device_id_type=MESH
        )
        count += groups
    if devices_chan:
        groups = devices_chan // 2
        for step in range(1, groups):
            there = lax.rem(chan // 2 + step, groups) * 2 + chan % 2
            pl.semaphore_signal(barrier, inc=1, device_id=(seq, there), device_id_type=MESH)
        pl.semaphore_signal(
            barrier, inc=1, device_id=(seq, chan + 1 - 2 * (chan % 2)), device_id_type=MESH
        )
        count += groups
    pl.semaphore_wait(barrier, count)


def gather_kernel(
    devices_seq,
    devices_chan,
    tokens,
    grads,
    weights,
    tokens_out,
    grads_out,
    projected,
    upstream,
    all_tokens,
    all_grads,
    all_weights,
    keep_sem,
    store_sem,
    chan_send,
    chan_recv,
    chan_pass,
    chan_passed,
    seq_send,
    seq_recv,
    seq_pass,
    seq_passed,
):
    seq, chan = lax.axis_index("seq"), lax.axis_index("chan")
    seq_groups, chan_groups = devices_seq // 2, devices_chan // 2
    seq_pair = (seq + 1 - 2 * (seq % 2), chan)
    chan_pair = (seq, chan + 1 - 2 * (chan % 2))
    columns = tokens.shape[1]
    rows = weights.shape[0]
    greet(devices_seq, devices_chan, "pairs")

    def block(ref, lines, index):
        return ref.at[lines, pl.ds(pl.multiple_of(index * columns, columns), columns)]

    def piece(index):
        return all_weights.at[pl.ds(pl.multiple_of(index * rows, rows), rows)]

    def chan_member(step, parity):
        return lax.rem(chan // 2 - step + chan_groups, chan_groups) * 2 + parity

    def seq_member(step, parity):
        return lax.rem(seq // 2 - step + seq_groups, seq_groups) * 2 + parity

    height = tokens.shape[0] // 2
    parts = [
        (own, whole, out, pl.ds(half * height, height))
        for own, whole, out in ((tokens, all_tokens, tokens_out), (grads, all_grads, grads_out))
        for half in range(2)
    ]

    def chan_copy(array, step):
        own, whole, _, lines = parts[array]
        there = lax.rem(chan // 2 + step, chan_groups) * 2 + chan % 2
        return remote(
            own.at[lines],
            block(whole, lines, chan),
            chan_send.at[array, step],
            chan_recv.at[array, step],
            (seq, there),
        )

    def chan_forward(array, step):
        own, whole, _, lines = parts[array]
        here = chan_member(step, chan % 2)
        return remote(
            own.at[lines] if step == 0 else block(whole, lines, here),
            block(whole, lines, here),
            chan_pass.at[array, step],
            chan_passed.at[array, step],
            chan_pair,
        )

    def seq_copy(step):
        there = lax.rem(seq // 2 + step, seq_groups) * 2 + seq % 2
        return remote(weights, piece(seq), seq_send.at[step], seq_recv.at[step], (there, chan))

    def seq_forward(step):
        here = seq_member(step, seq % 2)
        return remote(piece(here), piece(here), seq_pass.at[step], seq_passed.at[step], seq_pair)

    own_piece = remote(weights, piece(seq), seq_pass.at[0], seq_passed.at[0], seq_pair)

    def each(call):
        def body(step, carry):
            call(step)
            return carry

        lax.fori_loop(1, seq_groups, body, 0)

    def store(array):
        _, whole, out, lines = parts[array]
        return pltpu.make_async_copy(whole.at[lines], out.at[lines], store_sem.at[array])

    for array in range(4):
        for step in range(1, chan_groups):
            chan_copy(array, step).start()
    each(lambda step: seq_copy(step).start())
    own_piece.start()
    for array in range(4):
        chan_forward(array, 0).start()
    keeps = [pltpu.make_async_copy(weights, piece(seq), keep_sem.at[4])]
    for array, (own, whole, _, lines) in enumerate(parts):
        keeps.append(
            pltpu.make_async_copy(own.at[lines], block(whole, lines, chan), keep_sem.at[array])
        )
    for keep in keeps:
        keep.start()

    def pass_on(step):
        seq_copy(step).wait_recv()
        seq_forward(step).start()

    def pass_part(array):
        for step in range(1, chan_groups):
            chan_copy(array, step).wait_recv()
            chan_forward(array, step).start()

    pass_part(0)
    each(pass_on)
    for keep in keeps:
        keep.wait()
    own_piece.wait()

    def finish(step):
        seq_copy(step).wait_send()
        seq_forward(step).wait()

    each(finish)
    tile = math.gcd(height, 128)
    for array, (_, whole, _, lines) in enumerate(parts):
        if array + 1 < len(parts):
            pass_part(array + 1)
        for step in range(chan_groups):
            chan_forward(array, step).wait()
        store(array).start()
        target, first = (projected, 0) if array < 2 else (upstream, all_weights.shape[1] // 2)

        def product(index, carry):
            here = pl.ds(pl.multiple_of(array % 2 * height + index * tile, tile), tile)
            target[here] = jnp.dot(
                whole[here], all_weights[:, first:], preferred_element_type=jnp.float32
            )
            return carry

        lax.fori_loop(0, height // tile, product, 0)
    for array in range(4):
        store(array).wait()
        for step in range(1, chan_groups):
            chan_copy(array, step).wait_send()


def gathered(tokens, grads, weights):
    devices_seq, devices_chan = lax.axis_size("seq"), lax.axis_size("chan")
    dma = pltpu.SemaphoreType.DMA
    seq_groups, chan_groups = devices_seq // 2, devices_chan // 2
    vmem, anywhere = pl.BlockSpec(memory_space=pltpu.VMEM), pl.BlockSpec(memory_space=pl.ANY)
    wide = jax.ShapeDtypeStruct((tokens.shape[0], tokens.shape[1] * devices_chan), tokens.dtype)
    tall = jax.ShapeDtypeStruct((weights.shape[0] * devices_seq, weights.shape[1]), weights.dtype)
    return pl.pallas_call(
        functools.partial(gather_kernel, devices_seq, devices_chan),
        out_shape=(
            wide,
            wide,
            jax.ShapeDtypeStruct((tokens.shape[0], weights.shape[1]), jnp.float32),
            jax.ShapeDtypeStruct((tokens.shape[0], weights.shape[1] // 2), jnp.float32),
        ),
        in_specs=[vmem] * 3,
        out_specs=(anywhere, anywhere, vmem, vmem),
        scratch_shapes=[
            pltpu.VMEM(wide.shape, wide.dtype),
            pltpu.VMEM(wide.shape, wide.dtype),
            pltpu.VMEM(tall.shape, tall.dtype),
            dma((5,)),
            dma((4,)),
        ]
        + [dma((4, chan_groups))] * 4
        + [dma((seq_groups,))] * 4,
        compiler_params=pltpu.CompilerParams(collective_id=0, has_side_effects=True),
        name="gather_inputs",
    )(tokens, grads, weights)


def reduce_kernel(
    devices_seq,
    tile,
    state,
    rate,
    weight,
    inner,
    value,
    gate,
    early_in,
    early_out,
    tokens_hbm,
    grads_hbm,
    total,
    tokens,
    grads,
    states,
    late,
    parts,
    near,
    paired,
    far,
    load_sem,
    state_send,
    state_recv,
    pair_send,
    pair_recv,
    far_send,
    far_recv,
):
    seq, chan = lax.axis_index("seq"), lax.axis_index("chan")
    groups = devices_seq // 2
    group, parity = seq // 2, seq % 2
    rows, channels = inner.shape
    owned = near.shape[2]
    loads = [
        pltpu.make_async_copy(tokens_hbm, tokens, load_sem.at[0]),
        pltpu.make_async_copy(grads_hbm, grads, load_sem.at[1]),
    ]
    for load in loads:
        load.start()
    greet(devices_seq, 0, "all")

    def loop(start, stop, call):
        def body(step, carry):
            call(step)
            return carry

        lax.fori_loop(start, stop, body, 0)

    def state_copy(step):
        there = lax.rem(seq + step, devices_seq)
        return remote(
            state, states.at[step], state_send.at[step], state_recv.at[step], (there, chan)
        )

    def member(step):
        return lax.rem(group + step, groups)

    def piece(half, index):
        return parts.at[half, pl.ds(pl.multiple_of(index * owned, owned), owned)]

    def pair_copy(half, step):
        return remote(
            piece(half, member(step) * 2 + 1 - parity),
            near.at[half, step],
            pair_send.at[half, step],
            pair_recv.at[half, step],
            (group * 2 + 1 - parity, chan),
        )

    def far_copy(half, step):
        return remote(
            paired.at[half, step],
            far.at[half, step],
            far_send.at[half, step],
            far_recv.at[half, step],
            (member(step) * 2 + parity, chan),
        )

    def summed(left, right):
        return lax.dot_general(
            left, right, (((0,), (0,)), ((), ())), preferred_element_type=jnp.float32
        )

    def span(index):
        return pl.ds(pl.multiple_of(index * tile, tile), tile)

    loop(1, devices_seq, lambda step: state_copy(step).start())
    for load in loads:
        load.wait()

    def early_tile(index):
        product = summed(tokens[:, span(index)], early_in[...])
        product += summed(grads[:, span(index)], early_out[...])
        parts[0, span(index)] = product.astype(parts.dtype)

    loop(0, tokens.shape[1] // tile, early_tile)
    loop(1, groups, lambda step: pair_copy(0, step).start())
    pair_copy(0, 0).start()

    def absorb(step, following):
        state_copy(step).wait_recv()
        gap = lax.rem(seq - step + devices_seq, devices_seq) - seq - 1
        reach = (jnp.maximum(gap, 0) * rows).astype(jnp.float32)
        present = (gap >= 0).astype(jnp.float32)
        return following + present * states[step] * jnp.exp(-reach * rate[...])

    following = lax.fori_loop(1, devices_seq, absorb, jnp.zeros(rate.shape, jnp.float32))
    entering = weight[...] * following
    rates = rate[...]
    band = math.gcd(rows, 64)

    def source_rows(index):
        here = pl.ds(pl.multiple_of(index * band, band), band)
        position = lax.broadcasted_iota(jnp.int32, (band, channels), 0) + index * band
        reach = (rows - position).astype(jnp.float32)
        source = inner[here]
        for mode in range(rates.shape[0]):
            source += entering[mode : mode + 1] * jnp.exp(-reach * rates[mode : mode + 1])
        late[here] = jnp.concatenate([source * value[here], source * gate[here]], axis=1).astype(
            late.dtype
        )

    loop(0, rows // band, source_rows)

    def late_tile(index):
        parts[1, span(index)] = summed(tokens[:, span(index)], late[...]).astype(parts.dtype)

    loop(0, tokens.shape[1] // tile, late_tile)
    loop(1, groups, lambda step: pair_copy(1, step).start())
    pair_copy(1, 0).start()

    def pair_sum(half, step):
        own = piece(half, member(step) * 2 + parity)[...].astype(jnp.float32)
        return own + near[half, step].astype(jnp.float32)

    for half in range(2):

        def pass_on(step):
            pair_copy(half, step).wait_recv()
            paired[half, step] = pair_sum(half, step).astype(paired.dtype)
            far_copy(half, step).start()

        loop(1, groups, pass_on)
    for half in range(2):
        pair_copy(half, 0).wait_recv()
        total[half] = pair_sum(half, 0)

        def collect(step):
            far_copy(half, step).wait_recv()
            total[half] += far[half, step].astype(jnp.float32)

        loop(1, groups, collect)

        def finish(step):
            pair_copy(half, step).wait_send()
            far_copy(half, step).wait_send()

        loop(1, groups, finish)
        pair_copy(half, 0).wait_send()
    loop(1, devices_seq, lambda step: state_copy(step).wait_send())


def reduced(state, rate, weight, inner, value, gate, early_in, early_out, tokens, grads, owned):
    devices_seq = lax.axis_size("seq")
    groups = devices_seq // 2
    rows, channels = inner.shape
    width = tokens.shape[1]
    wide = 2 * channels
    vmem, anywhere = pl.BlockSpec(memory_space=pltpu.VMEM), pl.BlockSpec(memory_space=pl.ANY)
    dma, half_type = pltpu.SemaphoreType.DMA, tokens.dtype
    return pl.pallas_call(
        functools.partial(reduce_kernel, devices_seq, math.gcd(width, 512)),
        out_shape=jax.ShapeDtypeStruct((2, owned, wide), jnp.float32),
        in_specs=[vmem] * 8 + [anywhere] * 2,
        out_specs=vmem,
        scratch_shapes=[pltpu.VMEM(tokens.shape, half_type)] * 2
        + [pltpu.VMEM((devices_seq,) + state.shape, jnp.float32)]
        + [pltpu.VMEM((rows, wide), half_type), pltpu.VMEM((2, width, wide), half_type)]
        + [pltpu.VMEM((2, groups, owned, wide), half_type)] * 3
        + [dma((2,)), dma((devices_seq,)), dma((devices_seq,))]
        + [dma((2, groups))] * 4,
        compiler_params=pltpu.CompilerParams(collective_id=1, has_side_effects=True),
        name="reduce_owned",
    )(state, rate, weight, inner, value, gate, early_in, early_out, tokens, grads)


def correlate_block(signal, residues, decay_length):
    rows, channels = signal.shape
    chunk = min(64, rows)
    chunks = rows // chunk
    per_filter = channels // residues.shape[1]
    rate = jnp.repeat(1.0 / decay_length, per_filter, axis=1)
    weight = jnp.repeat(residues, per_filter, axis=1) * jnp.sqrt(-jnp.expm1(-2.0 * rate))
    offset = jnp.arange(chunk, dtype=jnp.float32)
    exponent = rate.T[:, :, None] * offset
    grow = weight.T[:, :, None] * jnp.exp(exponent)
    fall = jnp.exp(-exponent)
    later = jnp.arange(chunk)[None, :] >= jnp.arange(chunk)[:, None]
    taps = jnp.einsum("cri,crj->cij", grow, fall, precision=precise)
    taps = jnp.where(later, taps, 0.0)
    pieces = signal.reshape(chunks, chunk, channels).transpose(2, 1, 0)
    both = jnp.einsum(
        "cij,cjn->cin", jnp.concatenate([taps, fall], axis=1), pieces, precision=precise
    )
    inner, sums = both[:, :chunk], both[:, chunk:]
    step = jnp.exp(-chunk * rate).T
    state = jnp.zeros_like(step)
    entering = []
    for index in reversed(range(chunks)):
        entering.append(step * state)
        state = sums[:, :, index] + step * state
    entering = jnp.stack(entering[::-1], axis=2)
    outer = jnp.einsum("cri,crn->cin", grow, entering, precision=precise)
    return (inner + outer).transpose(2, 1, 0).reshape(rows, channels), state.T, rate, weight


def block_kernel(
    devices_seq,
    devices_chan,
    tokens_hbm,
    grads_hbm,
    in_weight,
    out_weight,
    conv_hbm,
    residues,
    decay_length,
    grad_in,
    grad_out,
    tokens,
    grads,
    conv,
    pieces,
    crossed,
    weights,
    partial,
    pair_in,
    chip_sum,
    far_in,
    signal,
    consts,
    bank,
    own_state,
    states,
    flows,
    parts,
    near,
    summed,
    blocks,
    arrived,
    results,
    given,
    load_sem,
    sent,
    hop_recv,
    swap_recv,
    keep_sem,
    twin_recv,
    pair_recv,
    far_recv,
    state_recv,
    flow_recv,
    pass_recv,
    near_recv,
    turn_recv,
    home_recv,
    put_sem,
):
    seq, chan = lax.axis_index("seq"), lax.axis_index("chan")
    planes = devices_chan
    twins = devices_seq // planes
    groups = devices_chan // 2
    plane, twin = seq // twins, seq % twins
    group, parity = chan // 2, chan % 2
    partner = (seq, chan + 1 - 2 * parity)
    channels, rows = conv.shape
    owned = out_weight.shape[1]

    def ahead(index, step, count):
        return lax.rem(index + step, count)

    def behind(index, step, count):
        return lax.rem(index - step + count, count)

    sources = (in_weight.at[1], out_weight, in_weight.at[0], in_weight.at[2])
    count = len(sources)
    weight_loads = [
        pltpu.make_async_copy(sources[part], pieces.at[part, plane], load_sem.at[part])
        for part in range(count)
    ]
    bulk_loads = [
        pltpu.make_async_copy(tokens_hbm, tokens, load_sem.at[count]),
        pltpu.make_async_copy(grads_hbm, grads, load_sem.at[count + 1]),
        pltpu.make_async_copy(conv_hbm, conv, load_sem.at[count + 2]),
    ]
    filter_loads = [
        pltpu.make_async_copy(residues, given.at[0], load_sem.at[count + 3]),
        pltpu.make_async_copy(decay_length, given.at[1], load_sem.at[count + 4]),
    ]
    for load in weight_loads + filter_loads + bulk_loads:
        load.start()

    barrier = pltpu.get_barrier_semaphore()
    for step in range(1, devices_seq):
        pl.semaphore_signal(
            barrier, inc=1, device_id=(ahead(seq, step, devices_seq), chan), device_id_type=MESH
        )
    for step in range(1, devices_chan):
        pl.semaphore_signal(
            barrier, inc=1, device_id=(seq, ahead(chan, step, devices_chan)), device_id_type=MESH
        )
    pl.semaphore_wait(barrier, devices_seq + devices_chan - 2)

    bits = [1 << power for power in reversed(range(planes.bit_length() - 1))]

    def flip(index, mask):
        result = index
        for bit in bits:
            if mask & bit:
                result = result + bit - 2 * bit * (index // bit % 2)
        return result

    def hop(part, bit, mask):
        here = flip(plane, mask)
        return remote(
            pieces.at[part, here],
            pieces.at[part, here],
            sent.at[0],
            hop_recv.at[part, mask ^ bit],
            (flip(plane, bit) * twins + twin, chan),
        )

    def hop_in(part, mask):
        here = flip(plane, mask)
        bit = mask & -mask
        return remote(
            pieces.at[part, here],
            pieces.at[part, here],
            sent.at[0],
            hop_recv.at[part, mask],
            (flip(plane, bit) * twins + twin, chan),
        )

    def lower(mask):
        return [bit for bit in bits if mask == 0 or bit < mask & -mask]

    def cross(part, step, mask):
        here = flip(plane, mask)
        return remote(
            pieces.at[part, here],
            crossed.at[part, step, here],
            sent.at[1],
            twin_recv.at[part, step - 1, mask],
            (plane * twins + ahead(twin, step, twins), chan),
        )

    def held(part, step, target):
        return crossed.at[part, step, target] if step else pieces.at[part, target]

    def swap(part, step, target):
        return remote(
            held(part, step, target),
            weights.at[part, behind(twin, step, twins), chan],
            sent.at[2 + min(step, 1)],
            swap_recv.at[part, step],
            (seq, target),
        )

    def swap_in(part, step):
        landed = weights.at[part, behind(twin, step, twins), pl.ds(0, devices_chan - 1)]
        return remote(landed, landed, sent.at[2 + min(step, 1)], swap_recv.at[part, step], partner)

    def keep(part, step):
        return pltpu.make_async_copy(
            held(part, step, chan),
            weights.at[part, behind(twin, step, twins), chan],
            keep_sem.at[part, step],
        )

    def deliver(part, step, mask):
        target = flip(plane, mask)

        @pl.when(target == chan)
        def _():
            keep(part, step).start()

        @pl.when(target != chan)
        def _():
            swap(part, step, target).start()

    early = count // 2

    def crosses(part, mask):
        return part < early and mask != 2

    def here(part, mask):
        if crosses(part, mask):
            for step in range(1, twins):
                cross(part, step, mask).start()
        deliver(part, 0, mask)

    def arrive(part, mask):
        hop_in(part, mask).wait_recv()
        for bit in lower(mask):
            hop(part, bit, mask).start()
        here(part, mask)

    def cross_on(part, mask):
        for step in range(1, twins):
            cross(part, step, mask).wait_recv()
            deliver(part, step, mask)

    def twin_copy(part, step):
        return remote(
            weights.at[part, twin],
            weights.at[part, twin],
            sent.at[4 + part // early],
            twin_recv.at[part, step - 1, 2],
            (plane * twins + ahead(twin, step, twins), chan),
        )

    def twin_in(part, step):
        there = behind(twin, step, twins)
        return remote(
            weights.at[part, there],
            weights.at[part, there],
            sent.at[4 + part // early],
            twin_recv.at[part, step - 1, 2],
            (plane * twins + there, chan),
        )

    def share(part, mask):
        @pl.when(flip(plane, mask) == chan)
        def _():
            swap_in(part, 0).wait_recv()
            keep(part, 0).wait()
            for step in range(1, twins):
                twin_copy(part, step).start()

    def loaded(part):
        weight_loads[part].wait()

    first, last = range(early), range(early, count)
    for part in first:
        loaded(part)
        for bit in bits:
            hop(part, bit, 0).start()
        here(part, 0)
    for part in last:
        loaded(part)

    lanes = signal.shape[1]
    folds = lanes // channels
    groups_of_rows = 8
    span = signal.shape[0] // groups_of_rows
    modes, filters = residues.shape
    per_filter = channels // filters
    lane = lax.broadcasted_iota(jnp.int32, (filters, lanes), 1)
    which = lax.broadcasted_iota(jnp.int32, (filters, lanes), 0)
    spread = (lax.rem(lane, channels) // per_filter == which).astype(jnp.float32)
    for load in filter_loads:
        load.wait()
    inverse = 1.0 / given[1]
    twice = 2.0 * inverse
    series = jnp.zeros_like(twice)
    for order in range(10, 0, -1):
        series = (1.0 - series) * twice / order
    loss = jnp.where(twice < 0.5, series, 1.0 - jnp.exp(-twice))
    scale = given[0] * jnp.sqrt(loss)

    def widen(array):
        return jnp.dot(array, spread, precision=precise, preferred_element_type=jnp.float32)

    rate = widen(inverse)
    consts[0] = rate
    consts[1] = widen(scale)
    consts[2] = jnp.exp(-rate)

    inputs = (tokens, grads, tokens, tokens)

    def ready(part, step, mask):
        @pl.when(flip(plane, mask) == chan)
        def _():
            if crosses(part, mask):
                swap_in(part, step).wait_recv()
                keep(part, step).wait()
            elif step:
                twin_in(part, step).wait_recv()

    def project(part):
        for step in range(twins):
            block = behind(twin, step, twins)
            for mask in range(planes):
                ready(part, step, mask)
            columns = pl.ds(pl.multiple_of(block * owned, owned), owned)
            product = lax.dot_general(
                weights[part, block].reshape(devices_chan * channels, owned),
                inputs[part][:, columns],
                (((1,), (1,)), ((), ())),
                preferred_element_type=jnp.float32,
            )
            for target in range(devices_chan):
                piece = product[target * channels : (target + 1) * channels]
                place = (part, target % 2, target // 2)
                if step:
                    piece = partial[place] + piece
                partial[place] = piece

    def pair_copy(part, there):
        return remote(
            partial.at[part, 1 - parity, there],
            pair_in.at[part, there],
            sent.at[6],
            pair_recv.at[part, there],
            partner,
        )

    def far_copy(part, step):
        return remote(
            chip_sum.at[part, step],
            far_in.at[part, step],
            sent.at[7],
            far_recv.at[part, step],
            (seq, ahead(group, step, groups) * 2 + parity),
        )

    def pair_start(part):
        for step in range(1, groups + 1):
            pair_copy(part, ahead(group, step, groups)).start()

    def far_start(part):
        for step in range(1, groups):
            there = ahead(group, step, groups)
            pair_copy(part, there).wait_recv()
            chip_sum[part, step] = partial[part, parity, there] + pair_in[part, there]
            far_copy(part, step).start()

    def far_finish(part):
        pair_copy(part, group).wait_recv()
        total = partial[part, parity, group] + pair_in[part, group]
        for step in range(1, groups):
            far_copy(part, step).wait_recv()
            total = total + far_in[part, step]
        return total

    def flow(part, step):
        return remote(
            flows.at[part, chan],
            flows.at[part, chan],
            sent.at[8],
            flow_recv.at[part, step],
            (seq, ahead(group, step, groups) * 2 + parity),
        )

    def flow_in(part, step):
        source = behind(group, step, groups) * 2 + parity
        return remote(
            flows.at[part, source],
            flows.at[part, source],
            sent.at[8],
            flow_recv.at[part, step],
            (seq, source),
        )

    def flow_pass(part, step):
        source = behind(group, step, groups) * 2 + parity
        return remote(
            flows.at[part, source],
            flows.at[part, source],
            sent.at[9],
            pass_recv.at[part, step],
            partner,
        )

    def flow_passed(part, step):
        source = behind(group, step, groups) * 2 + 1 - parity
        return remote(
            flows.at[part, source],
            flows.at[part, source],
            sent.at[9],
            pass_recv.at[part, step],
            partner,
        )

    def flow_start(part):
        for step in range(1, groups):
            flow(part, step).start()
        flow_pass(part, 0).start()

    def flow_on(part):
        for step in range(1, groups):
            flow_in(part, step).wait_recv()
            flow_pass(part, step).start()

    def flow_finish(part):
        for step in range(groups):
            flow_passed(part, step).wait_recv()

    def near_copy(part, step, target):
        return remote(
            parts.at[part, ahead(twin, step, twins), target],
            near.at[part, step, target],
            sent.at[10],
            near_recv.at[part, step - 1, target],
            (plane * twins + ahead(twin, step, twins), chan),
        )

    def multiply(part):
        for step in range(1, twins + 1):
            block = ahead(twin, step, twins)
            columns = pl.ds(pl.multiple_of(block * owned, owned), owned)
            product = jnp.dot(
                flows[part].reshape(devices_chan * channels, rows),
                inputs[part][:, columns],
                preferred_element_type=jnp.float32,
            ).astype(parts.dtype)
            for target in range(devices_chan):
                parts[part, block, target] = product[target * channels : (target + 1) * channels]
            if step < twins:
                for index in range(1, devices_chan + 1):
                    near_copy(part, step, ahead(chan, index, devices_chan)).start()

    def turn(part, target):
        return remote(
            summed.at[part, target],
            blocks.at[part, chan],
            sent.at[11],
            turn_recv.at[part, chan],
            (seq, target),
        )

    def turn_in(part, source):
        return remote(
            summed.at[part, source],
            blocks.at[part, source],
            sent.at[11],
            turn_recv.at[part, source],
            (seq, source),
        )

    def home(part, mask):
        return remote(
            blocks.at[part, flip(plane, mask)],
            arrived.at[part, mask],
            sent.at[12],
            home_recv.at[part, mask],
            (flip(plane, mask & -mask) * twins + twin, chan),
        )

    def turn_start(part, index):
        target = ahead(chan, index, devices_chan)
        total = parts[part, twin, target].astype(jnp.float32)
        for step in range(1, twins):
            near_copy(part, step, target).wait_recv()
            total = total + near[part, step, target].astype(jnp.float32)
        total = total.astype(blocks.dtype)
        if index < devices_chan:
            summed[part, target] = total
            turn(part, target).start()
        else:
            blocks[part, chan] = total

    def turned(part, index):
        source = behind(chan, index, devices_chan)
        if index < devices_chan:
            turn_in(part, source).wait_recv()

        for mask in range(1, planes, 2):

            @pl.when(flip(plane, mask) == source)
            def _(mask=mask):
                home(part, mask).start()

    def gathered(part, mask):
        total = blocks[part, flip(plane, mask)].astype(jnp.float32)
        for bit in reversed(bits):
            if mask == 0 or bit < mask & -mask:
                home(part, mask ^ bit).wait_recv()
                total = total + arrived[part, mask ^ bit].astype(jnp.float32)
        return total

    targets = (grad_in.at[1], grad_out, grad_in.at[0], grad_in.at[2])

    def put(part):
        return pltpu.make_async_copy(results.at[part], targets[part], put_sem.at[part])

    def finish(part):
        results[part] = gathered(part, 0)
        put(part).start()

    def home_on(part):
        for mask in range(planes - 1, 0, -1):
            if mask & -mask > 1:
                blocks[part, flip(plane, mask)] = gathered(part, mask).astype(blocks.dtype)
                home(part, mask).start()

    def rowed(array):
        width = array.shape[1] // folds
        stacked = jnp.concatenate(
            [array[:, fold * width : (fold + 1) * width] for fold in range(folds)], axis=0
        )
        return stacked.T

    def unrowed(array):
        stacked = array.T
        return jnp.concatenate(
            [stacked[fold * channels : (fold + 1) * channels] for fold in range(folds)], axis=1
        )

    def mode_row(kind, mode):
        return jnp.broadcast_to(consts[kind, mode : mode + 1], (groups_of_rows, lanes))

    def line(index):
        return pl.ds(index, groups_of_rows, stride=span)

    def scan_states():
        fall = [mode_row(2, mode) for mode in range(modes)]

        def body(step, carry):
            here = signal[line(span - 1 - step)]
            return tuple(carry[mode] * fall[mode] + here for mode in range(modes))

        zero = jnp.zeros((groups_of_rows, lanes), jnp.float32)
        found = lax.fori_loop(0, span, body, (zero,) * modes)
        position = lax.broadcasted_iota(jnp.int32, (groups_of_rows, lanes), 0)
        for mode in range(modes):
            each = mode_row(0, mode) * span
            total = found[mode]
            shift = 1
            while shift < groups_of_rows:
                moved = pltpu.roll(total, groups_of_rows - shift, 0)
                moved = moved * jnp.exp(-each * shift)
                total = total + jnp.where(position < groups_of_rows - shift, moved, 0.0)
                shift *= 2
            moved = pltpu.roll(total, groups_of_rows - 1, 0)
            bank[mode] = jnp.where(position < groups_of_rows - 1, moved, 0.0)
            own_state[mode : mode + 1] = total[0:1]
        heads = own_state[...]
        reach = consts[0] * (span * groups_of_rows)
        later = pltpu.roll(heads, channels, 1)
        first = lax.broadcasted_iota(jnp.int32, (modes, lanes), 1) < channels
        consts[3] = jnp.where(first, later, 0.0)
        own_state[...] = jnp.where(first, heads + later * jnp.exp(-reach), 0.0)

    def state_copy(step):
        return remote(
            own_state,
            states.at[step],
            sent.at[13],
            state_recv,
            (ahead(seq, step, devices_seq), chan),
        )

    def scan_source():
        rates = consts[0]
        following = jnp.zeros((modes, lanes), jnp.float32)
        landed = states.at[pl.ds(1, devices_seq - 1)]
        remote(landed, landed, sent.at[13], state_recv, partner).wait_recv()
        for step in range(1, devices_seq):
            gap = behind(seq, step, devices_seq) - seq - 1
            reach = (jnp.maximum(gap, 0) * rows).astype(jnp.float32)
            present = (gap >= 0).astype(jnp.float32)
            following = following + present * states[step] * jnp.exp(-reach * rates)
        first = lax.broadcasted_iota(jnp.int32, (modes, lanes), 1) < channels
        after = pltpu.roll(following, channels, 1)
        within = following * jnp.exp(-(rates * (span * groups_of_rows)))
        consts[3] = jnp.where(first, consts[3] + within, after)
        fall = [mode_row(2, mode) for mode in range(modes)]
        weigh = [mode_row(1, mode) for mode in range(modes)]
        position = lax.broadcasted_iota(jnp.int32, (groups_of_rows, lanes), 0)
        left = ((groups_of_rows - 1 - position) * span).astype(jnp.float32)
        start = tuple(
            bank[mode] + mode_row(3, mode) * jnp.exp(-left * mode_row(0, mode))
            for mode in range(modes)
        )

        def body(step, carry):
            here = line(span - 1 - step)
            entry = signal[here]
            following = tuple(carry[mode] * fall[mode] + entry for mode in range(modes))
            terms = [following[mode] * weigh[mode] for mode in range(modes)]
            while len(terms) > 1:
                terms = [sum(terms[at : at + 2]) for at in range(0, len(terms), 2)]
            signal[here] = terms[0]
            return following

        lax.fori_loop(0, span, body, start)

    for part in first:
        arrive(part, 1)
    for part in first:
        cross_on(part, 0)
    for part in first:
        arrive(part, 2)
    for part in last:
        for bit in bits:
            hop(part, bit, 0).start()
    for part in last:
        here(part, 0)
    for part in first:
        cross_on(part, 1)
    for part in first:
        arrive(part, 3)
    for part in first:
        share(part, 2)
    for part in last:
        arrive(part, 1)
    for part in last:
        share(part, 0)
    for part in first:
        cross_on(part, 3)
    for part in last:
        arrive(part, 2)
    for part in last:
        share(part, 1)
    for part in last:
        arrive(part, 3)
    for load in bulk_loads:
        load.wait()
    project(0)
    pair_start(0)
    project(1)
    pair_start(1)
    far_start(0)
    far_start(1)
    for part in last:
        share(part, 2)
    for part in last:
        share(part, 3)

    taken = conv[...].astype(jnp.float32)
    second = far_finish(0).astype(flows.dtype).astype(jnp.float32)
    flows[1, chan] = (second * taken).astype(flows.dtype)
    flow_start(1)
    project(2)
    pair_start(2)
    project(3)
    pair_start(3)
    upstream = far_finish(1)
    flows[0, chan] = (upstream * taken).astype(flows.dtype)
    flow_start(0)
    far_start(2)
    far_start(3)
    signal[...] = rowed(upstream * second)
    flow_on(1)
    scan_states()
    for step in range(1, devices_seq):
        state_copy(step).start()
    flow_finish(1)
    multiply(1)
    flow_on(0)
    flow_finish(0)
    multiply(0)
    turn_start(1, 1)
    turn_start(1, 2)
    scan_source()
    source = unrowed(signal[...])
    turned(1, 1)
    late = far_finish(2).astype(flows.dtype).astype(jnp.float32)
    flows[3, chan] = (source * late).astype(flows.dtype)
    flow_start(3)
    late = far_finish(3).astype(flows.dtype).astype(jnp.float32)
    flows[2, chan] = (source * late).astype(flows.dtype)
    flow_start(2)
    turn_start(1, 3)
    turn_start(1, 4)
    turned(1, 2)
    turned(1, 3)
    turned(1, 4)
    turn_start(0, 1)
    turn_start(0, 2)
    turned(0, 1)
    flow_on(3)
    flow_on(2)
    flow_finish(3)
    multiply(3)
    flow_finish(2)
    multiply(2)
    turn_start(0, 3)
    turned(0, 2)
    turn_start(0, 4)
    turned(0, 3)
    turned(0, 4)
    home_on(1)
    turn_start(3, 1)
    turn_start(3, 2)
    turned(3, 1)
    home_on(0)
    turn_start(3, 3)
    turned(3, 2)
    turn_start(3, 4)
    turned(3, 3)
    turned(3, 4)
    finish(1)
    turn_start(2, 1)
    turn_start(2, 2)
    turned(2, 1)
    home_on(3)
    turn_start(2, 3)
    turned(2, 2)
    turn_start(2, 4)
    turned(2, 3)
    turned(2, 4)
    finish(0)
    home_on(2)
    finish(3)
    finish(2)
    for part in range(count):
        put(part).wait()

    def left(kind, ref):
        remote(ref, ref, sent.at[kind], state_recv, partner).wait_send()

    fewer = pl.ds(0, planes - 1)
    others = pl.ds(1, twins - 1)
    left(0, pieces.at[:, fewer])
    left(1, crossed.at[:, others, fewer])
    left(2, pieces.at[:, fewer])

    @pl.when(flip(plane, 2) == chan)
    def _():
        left(3, crossed.at[:, others, fewer])
        left(4, weights.at[pl.ds(0, early), others])

    @pl.when(flip(plane, 2) != chan)
    def _():
        left(3, crossed.at[:, others, pl.ds(0, planes - 2)])

    left(5, weights.at[pl.ds(early, count - early), others])
    left(6, partial.at[:, 0])
    left(7, chip_sum.at[:, pl.ds(1, groups - 1)])
    left(8, flows.at[:, pl.ds(0, groups - 1)])
    left(9, flows.at[:, pl.ds(0, groups)])
    left(10, parts.at[:, others])
    left(11, summed.at[:, fewer])
    left(12, blocks.at[:, fewer])
    left(13, states.at[pl.ds(1, devices_seq - 1)])


def fits(tokens, conv_out, in_weight, residues):
    devices_seq, devices_chan = lax.axis_size("seq"), lax.axis_size("chan")
    rows, channels = conv_out.shape
    return (
        devices_chan == 4
        and devices_seq % devices_chan == 0
        and devices_seq > devices_chan
        and in_weight.shape[0] % 128 == 0
        and 2 * channels == 128
        and channels % residues.shape[1] == 0
        and rows % 256 == 0
        and tokens.shape[1] * devices_chan == in_weight.shape[0] * devices_seq
    )


def blocked(tokens, grad_out, in_weight, out_weight, conv_out, residues, decay_length):
    devices_seq, devices_chan = lax.axis_size("seq"), lax.axis_size("chan")
    planes, groups = devices_chan, devices_chan // 2
    twins = devices_seq // planes
    rows, width = tokens.shape
    channels, owned = out_weight.shape[1], out_weight.shape[0]
    modes = residues.shape[0]
    anywhere = pl.BlockSpec(memory_space=pl.ANY)
    dma, half_type, full = pltpu.SemaphoreType.DMA, tokens.dtype, jnp.float32
    lanes = 2 * channels
    grad_in, grad_proj = pl.pallas_call(
        functools.partial(block_kernel, devices_seq, devices_chan),
        out_shape=(
            jax.ShapeDtypeStruct((3, channels, owned), full),
            jax.ShapeDtypeStruct((channels, owned), full),
        ),
        in_specs=[anywhere] * 7,
        out_specs=(anywhere, anywhere),
        scratch_shapes=[
            pltpu.VMEM((rows, width), half_type),
            pltpu.VMEM((rows, width), half_type),
            pltpu.VMEM((channels, rows), half_type),
            pltpu.VMEM((4, planes, channels, owned), half_type),
            pltpu.VMEM((2, twins, planes, channels, owned), half_type),
            pltpu.VMEM((4, twins, devices_chan, channels, owned), half_type),
            pltpu.VMEM((4, 2, groups, channels, rows), full),
            pltpu.VMEM((4, groups, channels, rows), full),
            pltpu.VMEM((4, groups, channels, rows), full),
            pltpu.VMEM((4, groups, channels, rows), full),
            pltpu.VMEM((rows * channels // lanes, lanes), full),
            pltpu.VMEM((4, modes, lanes), full),
            pltpu.VMEM((modes, 8, lanes), full),
            pltpu.VMEM((modes, lanes), full),
            pltpu.VMEM((devices_seq, modes, lanes), full),
            pltpu.VMEM((4, devices_chan, channels, rows), half_type),
            pltpu.VMEM((4, twins, devices_chan, channels, owned), half_type),
            pltpu.VMEM((4, twins, devices_chan, channels, owned), half_type),
            pltpu.VMEM((4, devices_chan, channels, owned), half_type),
            pltpu.VMEM((4, planes, channels, owned), half_type),
            pltpu.VMEM((4, planes, channels, owned), half_type),
            pltpu.VMEM((4, channels, owned), full),
            pltpu.VMEM((2,) + residues.shape, full),
            dma((9,)),
            dma((14,)),
            dma((4, planes)),
            dma((4, twins)),
            dma((4, twins)),
            dma((4, twins - 1, planes)),
        ]
        + [dma((4, groups))] * 2
        + [dma]
        + [dma((4, groups))] * 2
        + [dma((4, twins - 1, planes))]
        + [dma((4, planes))] * 2
        + [dma((4,))],
        compiler_params=pltpu.CompilerParams(collective_id=2, has_side_effects=True),
        name="conv_block",
    )(
        tokens,
        grad_out,
        in_weight.transpose(1, 2, 0),
        out_weight.T,
        conv_out.T,
        residues,
        decay_length,
    )
    return grad_in.transpose(2, 0, 1), grad_proj.T


def local(tokens, grad_out, in_weight, out_weight, conv_out, residues, decay_length):
    if fits(tokens, conv_out, in_weight, residues):
        return blocked(tokens, grad_out, in_weight, out_weight, conv_out, residues, decay_length)
    channels = out_weight.shape[1]
    owned_rows = in_weight.shape[0]
    weights = jnp.concatenate([in_weight.reshape(owned_rows, 3 * channels), out_weight], axis=1)
    full_tokens, full_grads, projected, upstream = gathered(tokens, grad_out, weights)
    projected = projected[:, : 3 * channels]
    upstream = upstream[:, channels:]
    streams = lax.reduce_precision(projected, exponent_bits=8, mantissa_bits=7)
    gate_first = streams[:, :channels]
    gate_second = streams[:, channels : 2 * channels]
    value_stream = streams[:, 2 * channels :]
    conv_value = conv_out.astype(jnp.float32)
    gated = (gate_second * conv_value).astype(jnp.bfloat16)
    grad_second = (upstream * conv_value).astype(jnp.bfloat16)
    grad_conv = upstream * gate_second
    inner, state, rate, weight = correlate_block(grad_conv, residues, decay_length)
    blank = jnp.zeros_like(gated)
    owned = reduced(
        state,
        rate,
        weight,
        inner,
        value_stream,
        gate_first,
        jnp.concatenate([grad_second, blank], axis=1),
        jnp.concatenate([blank, gated], axis=1),
        full_tokens,
        full_grads,
        owned_rows,
    )
    grad_in = jnp.stack(
        [owned[1, :, :channels], owned[0, :, :channels], owned[1, :, channels:]], axis=1
    )
    return (grad_in, owned[0, :, channels:])


def solution(mesh):
    return jax.shard_map(
        local,
        mesh=mesh,
        in_specs=(
            P("seq", "chan"),
            P("seq", "chan"),
            P("seq", None, "chan"),
            P("seq", "chan"),
            P("seq", "chan"),
            P(None, "chan"),
            P(None, "chan"),
        ),
        out_specs=(P("seq", None, "chan"), P("seq", "chan")),
        check_vma=False,
    )
```

```python
import functools
import math

import jax
import jax.numpy as jnp
from jax import lax
from jax.experimental import pallas as pl
from jax.experimental.pallas import tpu as pltpu
from jax.sharding import PartitionSpec as P

precise = lax.Precision.HIGHEST
MESH = pl.DeviceIdType.MESH


def remote(source, target, send_sem, recv_sem, device):
    return pltpu.make_async_remote_copy(
        src_ref=source,
        dst_ref=target,
        send_sem=send_sem,
        recv_sem=recv_sem,
        device_id=device,
        device_id_type=MESH,
    )


def greet(devices_seq, devices_chan, seq_wide):
    seq, chan = lax.axis_index("seq"), lax.axis_index("chan")
    barrier = pltpu.get_barrier_semaphore()
    count = 0
    if seq_wide == "all":

        def hello(step, carry):
            pl.semaphore_signal(
                barrier,
                inc=1,
                device_id=(lax.rem(seq + step, devices_seq), chan),
                device_id_type=MESH,
            )
            return carry

        lax.fori_loop(1, devices_seq, hello, 0)
        count += devices_seq - 1
    else:
        groups = devices_seq // 2

        def hello_group(step, carry):
            there = lax.rem(seq // 2 + step, groups) * 2 + seq % 2
            pl.semaphore_signal(barrier, inc=1, device_id=(there, chan), device_id_type=MESH)
            return carry

        lax.fori_loop(1, groups, hello_group, 0)
        pl.semaphore_signal(
            barrier, inc=1, device_id=(seq + 1 - 2 * (seq % 2), chan), device_id_type=MESH
        )
        count += groups
    if devices_chan:
        groups = devices_chan // 2
        for step in range(1, groups):
            there = lax.rem(chan // 2 + step, groups) * 2 + chan % 2
            pl.semaphore_signal(barrier, inc=1, device_id=(seq, there), device_id_type=MESH)
        pl.semaphore_signal(
            barrier, inc=1, device_id=(seq, chan + 1 - 2 * (chan % 2)), device_id_type=MESH
        )
        count += groups
    pl.semaphore_wait(barrier, count)


def gather_kernel(
    devices_seq,
    devices_chan,
    tokens,
    grads,
    weights,
    tokens_out,
    grads_out,
    projected,
    upstream,
    all_tokens,
    all_grads,
    all_weights,
    keep_sem,
    store_sem,
    chan_send,
    chan_recv,
    chan_pass,
    chan_passed,
    seq_send,
    seq_recv,
    seq_pass,
    seq_passed,
):
    seq, chan = lax.axis_index("seq"), lax.axis_index("chan")
    seq_groups, chan_groups = devices_seq // 2, devices_chan // 2
    seq_pair = (seq + 1 - 2 * (seq % 2), chan)
    chan_pair = (seq, chan + 1 - 2 * (chan % 2))
    columns = tokens.shape[1]
    rows = weights.shape[0]
    greet(devices_seq, devices_chan, "pairs")

    def block(ref, lines, index):
        return ref.at[lines, pl.ds(pl.multiple_of(index * columns, columns), columns)]

    def piece(index):
        return all_weights.at[pl.ds(pl.multiple_of(index * rows, rows), rows)]

    def chan_member(step, parity):
        return lax.rem(chan // 2 - step + chan_groups, chan_groups) * 2 + parity

    def seq_member(step, parity):
        return lax.rem(seq // 2 - step + seq_groups, seq_groups) * 2 + parity

    height = tokens.shape[0] // 2
    parts = [
        (own, whole, out, pl.ds(half * height, height))
        for own, whole, out in ((tokens, all_tokens, tokens_out), (grads, all_grads, grads_out))
        for half in range(2)
    ]

    def chan_copy(array, step):
        own, whole, _, lines = parts[array]
        there = lax.rem(chan // 2 + step, chan_groups) * 2 + chan % 2
        return remote(
            own.at[lines],
            block(whole, lines, chan),
            chan_send.at[array, step],
            chan_recv.at[array, step],
            (seq, there),
        )

    def chan_forward(array, step):
        own, whole, _, lines = parts[array]
        here = chan_member(step, chan % 2)
        return remote(
            own.at[lines] if step == 0 else block(whole, lines, here),
            block(whole, lines, here),
            chan_pass.at[array, step],
            chan_passed.at[array, step],
            chan_pair,
        )

    def seq_copy(step):
        there = lax.rem(seq // 2 + step, seq_groups) * 2 + seq % 2
        return remote(weights, piece(seq), seq_send.at[step], seq_recv.at[step], (there, chan))

    def seq_forward(step):
        here = seq_member(step, seq % 2)
        return remote(piece(here), piece(here), seq_pass.at[step], seq_passed.at[step], seq_pair)

    own_piece = remote(weights, piece(seq), seq_pass.at[0], seq_passed.at[0], seq_pair)

    def each(call):
        def body(step, carry):
            call(step)
            return carry

        lax.fori_loop(1, seq_groups, body, 0)

    def store(array):
        _, whole, out, lines = parts[array]
        return pltpu.make_async_copy(whole.at[lines], out.at[lines], store_sem.at[array])

    for array in range(4):
        for step in range(1, chan_groups):
            chan_copy(array, step).start()
    each(lambda step: seq_copy(step).start())
    own_piece.start()
    for array in range(4):
        chan_forward(array, 0).start()
    keeps = [pltpu.make_async_copy(weights, piece(seq), keep_sem.at[4])]
    for array, (own, whole, _, lines) in enumerate(parts):
        keeps.append(
            pltpu.make_async_copy(own.at[lines], block(whole, lines, chan), keep_sem.at[array])
        )
    for keep in keeps:
        keep.start()

    def pass_on(step):
        seq_copy(step).wait_recv()
        seq_forward(step).start()

    def pass_part(array):
        for step in range(1, chan_groups):
            chan_copy(array, step).wait_recv()
            chan_forward(array, step).start()

    pass_part(0)
    each(pass_on)
    for keep in keeps:
        keep.wait()
    own_piece.wait()

    def finish(step):
        seq_copy(step).wait_send()
        seq_forward(step).wait()

    each(finish)
    tile = math.gcd(height, 128)
    for array, (_, whole, _, lines) in enumerate(parts):
        if array + 1 < len(parts):
            pass_part(array + 1)
        for step in range(chan_groups):
            chan_forward(array, step).wait()
        store(array).start()
        target, first = (projected, 0) if array < 2 else (upstream, all_weights.shape[1] // 2)

        def product(index, carry):
            here = pl.ds(pl.multiple_of(array % 2 * height + index * tile, tile), tile)
            target[here] = jnp.dot(
                whole[here], all_weights[:, first:], preferred_element_type=jnp.float32
            )
            return carry

        lax.fori_loop(0, height // tile, product, 0)
    for array in range(4):
        store(array).wait()
        for step in range(1, chan_groups):
            chan_copy(array, step).wait_send()


def gathered(tokens, grads, weights):
    devices_seq, devices_chan = lax.axis_size("seq"), lax.axis_size("chan")
    dma = pltpu.SemaphoreType.DMA
    seq_groups, chan_groups = devices_seq // 2, devices_chan // 2
    vmem, anywhere = pl.BlockSpec(memory_space=pltpu.VMEM), pl.BlockSpec(memory_space=pl.ANY)
    wide = jax.ShapeDtypeStruct((tokens.shape[0], tokens.shape[1] * devices_chan), tokens.dtype)
    tall = jax.ShapeDtypeStruct((weights.shape[0] * devices_seq, weights.shape[1]), weights.dtype)
    return pl.pallas_call(
        functools.partial(gather_kernel, devices_seq, devices_chan),
        out_shape=(
            wide,
            wide,
            jax.ShapeDtypeStruct((tokens.shape[0], weights.shape[1]), jnp.float32),
            jax.ShapeDtypeStruct((tokens.shape[0], weights.shape[1] // 2), jnp.float32),
        ),
        in_specs=[vmem] * 3,
        out_specs=(anywhere, anywhere, vmem, vmem),
        scratch_shapes=[
            pltpu.VMEM(wide.shape, wide.dtype),
            pltpu.VMEM(wide.shape, wide.dtype),
            pltpu.VMEM(tall.shape, tall.dtype),
            dma((5,)),
            dma((4,)),
        ]
        + [dma((4, chan_groups))] * 4
        + [dma((seq_groups,))] * 4,
        compiler_params=pltpu.CompilerParams(collective_id=0, has_side_effects=True),
        name="gather_inputs",
    )(tokens, grads, weights)


def reduce_kernel(
    devices_seq,
    tile,
    state,
    rate,
    weight,
    inner,
    value,
    gate,
    early_in,
    early_out,
    tokens_hbm,
    grads_hbm,
    total,
    tokens,
    grads,
    states,
    late,
    parts,
    near,
    paired,
    far,
    load_sem,
    state_send,
    state_recv,
    pair_send,
    pair_recv,
    far_send,
    far_recv,
):
    seq, chan = lax.axis_index("seq"), lax.axis_index("chan")
    groups = devices_seq // 2
    group, parity = seq // 2, seq % 2
    rows, channels = inner.shape
    owned = near.shape[2]
    loads = [
        pltpu.make_async_copy(tokens_hbm, tokens, load_sem.at[0]),
        pltpu.make_async_copy(grads_hbm, grads, load_sem.at[1]),
    ]
    for load in loads:
        load.start()
    greet(devices_seq, 0, "all")

    def loop(start, stop, call):
        def body(step, carry):
            call(step)
            return carry

        lax.fori_loop(start, stop, body, 0)

    def state_copy(step):
        there = lax.rem(seq + step, devices_seq)
        return remote(
            state, states.at[step], state_send.at[step], state_recv.at[step], (there, chan)
        )

    def member(step):
        return lax.rem(group + step, groups)

    def piece(half, index):
        return parts.at[half, pl.ds(pl.multiple_of(index * owned, owned), owned)]

    def pair_copy(half, step):
        return remote(
            piece(half, member(step) * 2 + 1 - parity),
            near.at[half, step],
            pair_send.at[half, step],
            pair_recv.at[half, step],
            (group * 2 + 1 - parity, chan),
        )

    def far_copy(half, step):
        return remote(
            paired.at[half, step],
            far.at[half, step],
            far_send.at[half, step],
            far_recv.at[half, step],
            (member(step) * 2 + parity, chan),
        )

    def summed(left, right):
        return lax.dot_general(
            left, right, (((0,), (0,)), ((), ())), preferred_element_type=jnp.float32
        )

    def span(index):
        return pl.ds(pl.multiple_of(index * tile, tile), tile)

    loop(1, devices_seq, lambda step: state_copy(step).start())
    for load in loads:
        load.wait()

    def early_tile(index):
        product = summed(tokens[:, span(index)], early_in[...])
        product += summed(grads[:, span(index)], early_out[...])
        parts[0, span(index)] = product.astype(parts.dtype)

    loop(0, tokens.shape[1] // tile, early_tile)
    loop(1, groups, lambda step: pair_copy(0, step).start())
    pair_copy(0, 0).start()

    def absorb(step, following):
        state_copy(step).wait_recv()
        gap = lax.rem(seq - step + devices_seq, devices_seq) - seq - 1
        reach = (jnp.maximum(gap, 0) * rows).astype(jnp.float32)
        present = (gap >= 0).astype(jnp.float32)
        return following + present * states[step] * jnp.exp(-reach * rate[...])

    following = lax.fori_loop(1, devices_seq, absorb, jnp.zeros(rate.shape, jnp.float32))
    entering = weight[...] * following
    rates = rate[...]
    band = math.gcd(rows, 64)

    def source_rows(index):
        here = pl.ds(pl.multiple_of(index * band, band), band)
        position = lax.broadcasted_iota(jnp.int32, (band, channels), 0) + index * band
        reach = (rows - position).astype(jnp.float32)
        source = inner[here]
        for mode in range(rates.shape[0]):
            source += entering[mode : mode + 1] * jnp.exp(-reach * rates[mode : mode + 1])
        late[here] = jnp.concatenate([source * value[here], source * gate[here]], axis=1).astype(
            late.dtype
        )

    loop(0, rows // band, source_rows)

    def late_tile(index):
        parts[1, span(index)] = summed(tokens[:, span(index)], late[...]).astype(parts.dtype)

    loop(0, tokens.shape[1] // tile, late_tile)
    loop(1, groups, lambda step: pair_copy(1, step).start())
    pair_copy(1, 0).start()

    def pair_sum(half, step):
        own = piece(half, member(step) * 2 + parity)[...].astype(jnp.float32)
        return own + near[half, step].astype(jnp.float32)

    for half in range(2):

        def pass_on(step):
            pair_copy(half, step).wait_recv()
            paired[half, step] = pair_sum(half, step).astype(paired.dtype)
            far_copy(half, step).start()

        loop(1, groups, pass_on)
    for half in range(2):
        pair_copy(half, 0).wait_recv()
        total[half] = pair_sum(half, 0)

        def collect(step):
            far_copy(half, step).wait_recv()
            total[half] += far[half, step].astype(jnp.float32)

        loop(1, groups, collect)

        def finish(step):
            pair_copy(half, step).wait_send()
            far_copy(half, step).wait_send()

        loop(1, groups, finish)
        pair_copy(half, 0).wait_send()
    loop(1, devices_seq, lambda step: state_copy(step).wait_send())


def reduced(state, rate, weight, inner, value, gate, early_in, early_out, tokens, grads, owned):
    devices_seq = lax.axis_size("seq")
    groups = devices_seq // 2
    rows, channels = inner.shape
    width = tokens.shape[1]
    wide = 2 * channels
    vmem, anywhere = pl.BlockSpec(memory_space=pltpu.VMEM), pl.BlockSpec(memory_space=pl.ANY)
    dma, half_type = pltpu.SemaphoreType.DMA, tokens.dtype
    return pl.pallas_call(
        functools.partial(reduce_kernel, devices_seq, math.gcd(width, 512)),
        out_shape=jax.ShapeDtypeStruct((2, owned, wide), jnp.float32),
        in_specs=[vmem] * 8 + [anywhere] * 2,
        out_specs=vmem,
        scratch_shapes=[pltpu.VMEM(tokens.shape, half_type)] * 2
        + [pltpu.VMEM((devices_seq,) + state.shape, jnp.float32)]
        + [pltpu.VMEM((rows, wide), half_type), pltpu.VMEM((2, width, wide), half_type)]
        + [pltpu.VMEM((2, groups, owned, wide), half_type)] * 3
        + [dma((2,)), dma((devices_seq,)), dma((devices_seq,))]
        + [dma((2, groups))] * 4,
        compiler_params=pltpu.CompilerParams(collective_id=1, has_side_effects=True),
        name="reduce_owned",
    )(state, rate, weight, inner, value, gate, early_in, early_out, tokens, grads)


def correlate_block(signal, residues, decay_length):
    rows, channels = signal.shape
    chunk = min(64, rows)
    chunks = rows // chunk
    per_filter = channels // residues.shape[1]
    rate = jnp.repeat(1.0 / decay_length, per_filter, axis=1)
    weight = jnp.repeat(residues, per_filter, axis=1) * jnp.sqrt(-jnp.expm1(-2.0 * rate))
    offset = jnp.arange(chunk, dtype=jnp.float32)
    exponent = rate.T[:, :, None] * offset
    grow = weight.T[:, :, None] * jnp.exp(exponent)
    fall = jnp.exp(-exponent)
    later = jnp.arange(chunk)[None, :] >= jnp.arange(chunk)[:, None]
    taps = jnp.einsum("cri,crj->cij", grow, fall, precision=precise)
    taps = jnp.where(later, taps, 0.0)
    pieces = signal.reshape(chunks, chunk, channels).transpose(2, 1, 0)
    both = jnp.einsum(
        "cij,cjn->cin", jnp.concatenate([taps, fall], axis=1), pieces, precision=precise
    )
    inner, sums = both[:, :chunk], both[:, chunk:]
    step = jnp.exp(-chunk * rate).T
    state = jnp.zeros_like(step)
    entering = []
    for index in reversed(range(chunks)):
        entering.append(step * state)
        state = sums[:, :, index] + step * state
    entering = jnp.stack(entering[::-1], axis=2)
    outer = jnp.einsum("cri,crn->cin", grow, entering, precision=precise)
    return (inner + outer).transpose(2, 1, 0).reshape(rows, channels), state.T, rate, weight


def block_kernel(
    devices_seq,
    devices_chan,
    tokens_hbm,
    grads_hbm,
    in_weight,
    out_weight,
    conv_hbm,
    residues,
    decay_length,
    grad_in,
    grad_out,
    tokens,
    grads,
    conv,
    pieces,
    crossed,
    weights,
    partial,
    pair_in,
    chip_sum,
    far_in,
    signal,
    consts,
    bank,
    own_state,
    states,
    flows,
    parts,
    near,
    summed,
    blocks,
    arrived,
    results,
    given,
    load_sem,
    sent,
    hop_recv,
    swap_recv,
    keep_sem,
    twin_recv,
    pair_recv,
    far_recv,
    state_recv,
    flow_recv,
    pass_recv,
    near_recv,
    turn_recv,
    home_recv,
    put_sem,
):
    seq, chan = lax.axis_index("seq"), lax.axis_index("chan")
    planes = devices_chan
    twins = devices_seq // planes
    groups = devices_chan // 2
    plane, twin = seq // twins, seq % twins
    group, parity = chan // 2, chan % 2
    partner = (seq, chan + 1 - 2 * parity)
    channels, rows = conv.shape
    owned = out_weight.shape[1]

    def ahead(index, step, count):
        return lax.rem(index + step, count)

    def behind(index, step, count):
        return lax.rem(index - step + count, count)

    sources = (in_weight.at[1], out_weight, in_weight.at[0], in_weight.at[2])
    count = len(sources)
    weight_loads = [
        pltpu.make_async_copy(sources[part], pieces.at[part, plane], load_sem.at[part])
        for part in range(count)
    ]
    bulk_loads = [
        pltpu.make_async_copy(tokens_hbm, tokens, load_sem.at[count]),
        pltpu.make_async_copy(grads_hbm, grads, load_sem.at[count + 1]),
        pltpu.make_async_copy(conv_hbm, conv, load_sem.at[count + 2]),
    ]
    filter_loads = [
        pltpu.make_async_copy(residues, given.at[0], load_sem.at[count + 3]),
        pltpu.make_async_copy(decay_length, given.at[1], load_sem.at[count + 4]),
    ]
    for load in weight_loads + filter_loads + bulk_loads:
        load.start()

    barrier = pltpu.get_barrier_semaphore()
    for step in range(1, devices_seq):
        pl.semaphore_signal(
            barrier, inc=1, device_id=(ahead(seq, step, devices_seq), chan), device_id_type=MESH
        )
    for step in range(1, devices_chan):
        pl.semaphore_signal(
            barrier, inc=1, device_id=(seq, ahead(chan, step, devices_chan)), device_id_type=MESH
        )
    pl.semaphore_wait(barrier, devices_seq + devices_chan - 2)

    bits = [1 << power for power in reversed(range(planes.bit_length() - 1))]

    def flip(index, mask):
        result = index
        for bit in bits:
            if mask & bit:
                result = result + bit - 2 * bit * (index // bit % 2)
        return result

    def hop(part, which, kind, side):
        return remote(
            pieces.at[part, which],
            pieces.at[part, which],
            sent.at[kind],
            hop_recv.at[part, which],
            ((plane + side) * twins + twin, chan),
        )

    def onward(part, which, kind, side):
        edge = planes - 1 if side > 0 else 0

        @pl.when(plane != edge)
        def _():
            hop(part, which, kind, side).start()

    def cross(part, step, mask):
        here = flip(plane, mask)
        return remote(
            pieces.at[part, here],
            crossed.at[part, step, here],
            sent.at[14 + part // early],
            twin_recv.at[part, step - 1, mask],
            (plane * twins + ahead(twin, step, twins), chan),
        )

    def held(part, step, target):
        return crossed.at[part, step, target] if step else pieces.at[part, target]

    def swap(part, step, target):
        return remote(
            held(part, step, target),
            weights.at[part, behind(twin, step, twins), chan],
            sent.at[2 + part // early if step else 1],
            swap_recv.at[part, step],
            (seq, target),
        )

    def swap_in(part, step):
        landed = weights.at[part, behind(twin, step, twins), pl.ds(0, devices_chan - 1)]
        return remote(landed, landed, sent.at[2 + part // early if step else 1], swap_recv.at[part, step], partner)

    def keep(part, step):
        return pltpu.make_async_copy(
            held(part, step, chan),
            weights.at[part, behind(twin, step, twins), chan],
            keep_sem.at[part, step],
        )

    def deliver(part, step, mask):
        target = flip(plane, mask)

        @pl.when(target == chan)
        def _():
            keep(part, step).start()

        @pl.when(target != chan)
        def _():
            swap(part, step, target).start()

    early = count // 2

    crossing = ((0, 1, 3), (3,))

    def crosses(part, mask):
        return mask in crossing[part // early]

    def here(part, mask):
        if crosses(part, mask):
            for step in range(1, twins):
                cross(part, step, mask).start()
        deliver(part, 0, mask)

    def depart(group):
        for part in group:
            for side in (1, -1):
                onward(part, plane, 0, side)

    def arrive(group, distance):
        for part in group:
            for mask in range(1, planes):
                which = flip(plane, mask)
                for side in (1, -1):

                    @pl.when(plane - which == side * distance)
                    def _(mask=mask, which=which, side=side, part=part):
                        hop(part, which, 0, side).wait_recv()
                        onward(part, which, 16, side)
                        here(part, mask)

    def cross_on(part, mask):
        for step in range(1, twins):
            cross(part, step, mask).wait_recv()
            deliver(part, step, mask)

    def twin_copy(part, step):
        return remote(
            weights.at[part, twin],
            weights.at[part, twin],
            sent.at[4 + part // early],
            twin_recv.at[part, step - 1, 2],
            (plane * twins + ahead(twin, step, twins), chan),
        )

    def twin_in(part, step):
        there = behind(twin, step, twins)
        return remote(
            weights.at[part, there],
            weights.at[part, there],
            sent.at[4 + part // early],
            twin_recv.at[part, step - 1, 2],
            (plane * twins + there, chan),
        )

    def share(part, mask):
        @pl.when(flip(plane, mask) == chan)
        def _():
            swap_in(part, 0).wait_recv()
            keep(part, 0).wait()
            for step in range(1, twins):
                twin_copy(part, step).start()

    def loaded(part):
        weight_loads[part].wait()

    first, last = range(early), range(early, count)
    for part in range(count):
        loaded(part)
    depart(first)
    for part in first:
        here(part, 0)

    lanes = signal.shape[1]
    folds = lanes // channels
    groups_of_rows = 8
    span = signal.shape[0] // groups_of_rows
    modes, filters = residues.shape
    per_filter = channels // filters
    lane = lax.broadcasted_iota(jnp.int32, (filters, lanes), 1)
    which = lax.broadcasted_iota(jnp.int32, (filters, lanes), 0)
    spread = (lax.rem(lane, channels) // per_filter == which).astype(jnp.float32)
    for load in filter_loads:
        load.wait()
    inverse = 1.0 / given[1]
    twice = 2.0 * inverse
    series = jnp.zeros_like(twice)
    for order in range(10, 0, -1):
        series = (1.0 - series) * twice / order
    loss = jnp.where(twice < 0.5, series, 1.0 - jnp.exp(-twice))
    scale = given[0] * jnp.sqrt(loss)

    def widen(array):
        return jnp.dot(array, spread, precision=precise, preferred_element_type=jnp.float32)

    rate = widen(inverse)
    consts[0] = rate
    consts[1] = widen(scale)
    consts[2] = jnp.exp(-rate)

    inputs = (tokens, grads, tokens, tokens)

    def ready(part, step, mask):
        @pl.when(flip(plane, mask) == chan)
        def _():
            if crosses(part, mask):
                swap_in(part, step).wait_recv()
                keep(part, step).wait()
            elif step:
                twin_in(part, step).wait_recv()

    def project(part):
        for step in range(twins):
            block = behind(twin, step, twins)
            for mask in range(planes):
                ready(part, step, mask)
            columns = pl.ds(pl.multiple_of(block * owned, owned), owned)
            product = lax.dot_general(
                weights[part, block].reshape(devices_chan * channels, owned),
                inputs[part][:, columns],
                (((1,), (1,)), ((), ())),
                preferred_element_type=jnp.float32,
            )
            for target in range(devices_chan):
                piece = product[target * channels : (target + 1) * channels]
                place = (part, target % 2, target // 2)
                if step:
                    piece = partial[place] + piece
                partial[place] = piece

    def pair_copy(part, there):
        return remote(
            partial.at[part, 1 - parity, there],
            pair_in.at[part, there],
            sent.at[6],
            pair_recv.at[part, there],
            partner,
        )

    def far_copy(part, step):
        return remote(
            chip_sum.at[part, step],
            far_in.at[part, step],
            sent.at[7],
            far_recv.at[part, step],
            (seq, ahead(group, step, groups) * 2 + parity),
        )

    def pair_start(part):
        for step in range(1, groups + 1):
            pair_copy(part, ahead(group, step, groups)).start()

    def far_start(part):
        for step in range(1, groups):
            there = ahead(group, step, groups)
            pair_copy(part, there).wait_recv()
            chip_sum[part, step] = partial[part, parity, there] + pair_in[part, there]
            far_copy(part, step).start()

    def far_finish(part):
        pair_copy(part, group).wait_recv()
        total = partial[part, parity, group] + pair_in[part, group]
        for step in range(1, groups):
            far_copy(part, step).wait_recv()
            total = total + far_in[part, step]
        return total

    def flow(part, step):
        return remote(
            flows.at[part, chan],
            flows.at[part, chan],
            sent.at[8],
            flow_recv.at[part, step],
            (seq, ahead(group, step, groups) * 2 + parity),
        )

    def flow_in(part, step):
        source = behind(group, step, groups) * 2 + parity
        return remote(
            flows.at[part, source],
            flows.at[part, source],
            sent.at[8],
            flow_recv.at[part, step],
            (seq, source),
        )

    def flow_pass(part, step):
        source = behind(group, step, groups) * 2 + parity
        return remote(
            flows.at[part, source],
            flows.at[part, source],
            sent.at[9],
            pass_recv.at[part, step],
            partner,
        )

    def flow_passed(part, step):
        source = behind(group, step, groups) * 2 + 1 - parity
        return remote(
            flows.at[part, source],
            flows.at[part, source],
            sent.at[9],
            pass_recv.at[part, step],
            partner,
        )

    def flow_start(part):
        for step in range(1, groups):
            flow(part, step).start()
        flow_pass(part, 0).start()

    def flow_on(part):
        for step in range(1, groups):
            flow_in(part, step).wait_recv()
            flow_pass(part, step).start()

    def flow_finish(part):
        for step in range(groups):
            flow_passed(part, step).wait_recv()

    def near_copy(part, step, target):
        return remote(
            parts.at[part, ahead(twin, step, twins), target],
            near.at[part, step, target],
            sent.at[10],
            near_recv.at[part, step - 1, target],
            (plane * twins + ahead(twin, step, twins), chan),
        )

    def multiply(part):
        for step in range(1, twins + 1):
            block = ahead(twin, step, twins)
            columns = pl.ds(pl.multiple_of(block * owned, owned), owned)
            product = jnp.dot(
                flows[part].reshape(devices_chan * channels, rows),
                inputs[part][:, columns],
                preferred_element_type=jnp.float32,
            ).astype(parts.dtype)
            for target in range(devices_chan):
                parts[part, block, target] = product[target * channels : (target + 1) * channels]
            if step < twins:
                for index in range(1, devices_chan + 1):
                    near_copy(part, step, ahead(chan, index, devices_chan)).start()

    def turn(part, target):
        return remote(
            summed.at[part, target],
            blocks.at[part, chan],
            sent.at[11],
            turn_recv.at[part, chan],
            (seq, target),
        )

    def turn_in(part, source):
        return remote(
            summed.at[part, source],
            blocks.at[part, source],
            sent.at[11],
            turn_recv.at[part, source],
            (seq, source),
        )

    straight = (0, 1, 2, 3)

    def home(part, mask):
        return remote(
            blocks.at[part, flip(plane, mask)],
            arrived.at[part, mask],
            sent.at[12],
            home_recv.at[part, mask],
            (flip(plane, mask if part in straight else mask & -mask) * twins + twin, chan),
        )

    def turn_start(part, index):
        target = ahead(chan, index, devices_chan)
        total = parts[part, twin, target].astype(jnp.float32)
        for step in range(1, twins):
            near_copy(part, step, target).wait_recv()
            total = total + near[part, step, target].astype(jnp.float32)
        total = total.astype(blocks.dtype)
        if index < devices_chan:
            summed[part, target] = total
            turn(part, target).start()
        else:
            blocks[part, chan] = total

    def turned(part, index):
        source = behind(chan, index, devices_chan)
        if index < devices_chan:
            turn_in(part, source).wait_recv()

        for mask in range(1, planes, 1 if part in straight else 2):

            @pl.when(flip(plane, mask) == source)
            def _(mask=mask):
                home(part, mask).start()

    def gathered(part, mask):
        total = blocks[part, flip(plane, mask)].astype(jnp.float32)
        for other in range(1, planes) if part in straight else reversed(bits):
            if mask == 0 or other < mask & -mask:
                home(part, mask ^ other).wait_recv()
                total = total + arrived[part, mask ^ other].astype(jnp.float32)
        return total

    targets = (grad_in.at[1], grad_out, grad_in.at[0], grad_in.at[2])

    def put(part):
        return pltpu.make_async_copy(results.at[part], targets[part], put_sem.at[part])

    def finish(part):
        results[part] = gathered(part, 0)
        put(part).start()

    def home_on(part):
        for mask in range(planes - 1, 0, -1):
            if mask & -mask > 1 and part not in straight:
                blocks[part, flip(plane, mask)] = gathered(part, mask).astype(blocks.dtype)
                home(part, mask).start()

    def rowed(array):
        width = array.shape[1] // folds
        stacked = jnp.concatenate(
            [array[:, fold * width : (fold + 1) * width] for fold in range(folds)], axis=0
        )
        return stacked.T

    def unrowed(array):
        stacked = array.T
        return jnp.concatenate(
            [stacked[fold * channels : (fold + 1) * channels] for fold in range(folds)], axis=1
        )

    def mode_row(kind, mode):
        return jnp.broadcast_to(consts[kind, mode : mode + 1], (groups_of_rows, lanes))

    def line(index):
        return pl.ds(index, groups_of_rows, stride=span)

    def scan_states():
        fall = [mode_row(2, mode) for mode in range(modes)]

        def body(step, carry):
            here = signal[line(span - 1 - step)]
            return tuple(carry[mode] * fall[mode] + here for mode in range(modes))

        zero = jnp.zeros((groups_of_rows, lanes), jnp.float32)
        found = lax.fori_loop(0, span, body, (zero,) * modes)
        position = lax.broadcasted_iota(jnp.int32, (groups_of_rows, lanes), 0)
        for mode in range(modes):
            each = mode_row(0, mode) * span
            total = found[mode]
            shift = 1
            while shift < groups_of_rows:
                moved = pltpu.roll(total, groups_of_rows - shift, 0)
                moved = moved * jnp.exp(-each * shift)
                total = total + jnp.where(position < groups_of_rows - shift, moved, 0.0)
                shift *= 2
            moved = pltpu.roll(total, groups_of_rows - 1, 0)
            bank[mode] = jnp.where(position < groups_of_rows - 1, moved, 0.0)
            own_state[mode : mode + 1] = total[0:1]
        heads = own_state[...]
        reach = consts[0] * (span * groups_of_rows)
        later = pltpu.roll(heads, channels, 1)
        first = lax.broadcasted_iota(jnp.int32, (modes, lanes), 1) < channels
        consts[3] = jnp.where(first, later, 0.0)
        own_state[...] = jnp.where(first, heads + later * jnp.exp(-reach), 0.0)

    def state_copy(step):
        return remote(
            own_state,
            states.at[step],
            sent.at[13],
            state_recv,
            (ahead(seq, step, devices_seq), chan),
        )

    def scan_source():
        rates = consts[0]
        following = jnp.zeros((modes, lanes), jnp.float32)
        landed = states.at[pl.ds(1, devices_seq - 1)]
        remote(landed, landed, sent.at[13], state_recv, partner).wait_recv()
        for step in range(1, devices_seq):
            gap = behind(seq, step, devices_seq) - seq - 1
            reach = (jnp.maximum(gap, 0) * rows).astype(jnp.float32)
            present = (gap >= 0).astype(jnp.float32)
            following = following + present * states[step] * jnp.exp(-reach * rates)
        first = lax.broadcasted_iota(jnp.int32, (modes, lanes), 1) < channels
        after = pltpu.roll(following, channels, 1)
        within = following * jnp.exp(-(rates * (span * groups_of_rows)))
        consts[3] = jnp.where(first, consts[3] + within, after)
        fall = [mode_row(2, mode) for mode in range(modes)]
        weigh = [mode_row(1, mode) for mode in range(modes)]
        position = lax.broadcasted_iota(jnp.int32, (groups_of_rows, lanes), 0)
        left = ((groups_of_rows - 1 - position) * span).astype(jnp.float32)
        start = tuple(
            bank[mode] + mode_row(3, mode) * jnp.exp(-left * mode_row(0, mode))
            for mode in range(modes)
        )

        def body(step, carry):
            here = line(span - 1 - step)
            entry = signal[here]
            following = tuple(carry[mode] * fall[mode] + entry for mode in range(modes))
            terms = [following[mode] * weigh[mode] for mode in range(modes)]
            while len(terms) > 1:
                terms = [sum(terms[at : at + 2]) for at in range(0, len(terms), 2)]
            signal[here] = terms[0]
            return following

        lax.fori_loop(0, span, body, start)

    def settle(group, mask):
        for part in group:
            if crosses(part, mask):
                cross_on(part, mask)
            else:
                share(part, mask)

    arrive(first, 1)
    settle(first, 0)
    depart(last)
    for part in last:
        here(part, 0)
    arrive(first, 2)
    settle(first, 1)
    arrive(first, 3)
    settle(first, 2)
    arrive(last, 1)
    settle(last, 0)
    settle(first, 3)
    arrive(last, 2)
    settle(last, 1)
    for load in bulk_loads:
        load.wait()
    project(0)
    pair_start(0)
    arrive(last, 3)
    project(1)
    pair_start(1)
    settle(last, 2)
    far_start(0)
    far_start(1)

    taken = conv[...].astype(jnp.float32)
    second = far_finish(0).astype(flows.dtype).astype(jnp.float32)
    flows[1, chan] = (second * taken).astype(flows.dtype)
    flow_start(1)
    settle(last, 3)
    upstream = far_finish(1)
    flows[0, chan] = (upstream * taken).astype(flows.dtype)
    flow_start(0)
    project(2)
    pair_start(2)
    signal[...] = rowed(upstream * second)
    project(3)
    pair_start(3)
    flow_on(1)
    scan_states()
    for step in range(1, devices_seq):
        state_copy(step).start()
    far_start(2)
    flow_finish(1)
    far_start(3)
    multiply(1)
    flow_on(0)
    flow_finish(0)
    multiply(0)
    turn_start(1, 1)
    turn_start(1, 2)
    scan_source()
    source = unrowed(signal[...])
    late = far_finish(2).astype(flows.dtype).astype(jnp.float32)
    flows[3, chan] = (source * late).astype(flows.dtype)
    flow_start(3)
    late = far_finish(3).astype(flows.dtype).astype(jnp.float32)
    flows[2, chan] = (source * late).astype(flows.dtype)
    flow_start(2)
    turn_start(1, 3)
    turned(1, 1)
    turn_start(1, 4)
    turned(1, 2)
    flow_on(3)
    turn_start(0, 1)
    turned(1, 3)
    flow_on(2)
    turn_start(0, 2)
    flow_finish(3)
    multiply(3)
    flow_finish(2)
    multiply(2)
    turned(1, 4)
    turn_start(0, 3)
    turned(0, 1)
    turn_start(0, 4)
    turned(0, 2)
    home_on(1)
    turned(0, 3)
    turned(0, 4)
    turn_start(3, 1)
    turn_start(3, 2)
    turn_start(3, 3)
    turned(3, 1)
    home_on(0)
    turn_start(3, 4)
    turned(3, 2)
    finish(1)
    turn_start(2, 1)
    turned(3, 3)
    turned(3, 4)
    turn_start(2, 2)
    finish(0)
    turn_start(2, 3)
    turned(2, 1)
    home_on(3)
    turn_start(2, 4)
    turned(2, 2)
    turned(2, 3)
    turned(2, 4)
    home_on(2)
    finish(3)
    finish(2)
    for part in range(count):
        put(part).wait()

    def left(kind, ref):
        remote(ref, ref, sent.at[kind], state_recv, partner).wait_send()

    fewer = pl.ds(0, planes - 1)
    others = pl.ds(1, twins - 1)
    inner = jnp.logical_and(plane > 0, plane < planes - 1)

    @pl.when(inner)
    def _():
        left(0, pieces.at[:, pl.ds(0, 2)])
        left(16, pieces.at[:, fewer])

    @pl.when(jnp.logical_not(inner))
    def _():
        left(0, pieces.at[:, pl.ds(0, 1)])

    left(1, pieces.at[:, fewer])
    for group in range(2):
        span_of = pl.ds(group * early, early)
        masks = crossing[group]
        if masks:
            left(14 + group, crossed.at[span_of, others, pl.ds(0, len(masks))])
        for mask in range(planes):

            @pl.when(flip(plane, mask) == chan)
            def _(mask=mask):
                swaps = len(masks) - (mask in masks)
                if swaps:
                    left(2 + group, crossed.at[span_of, others, pl.ds(0, swaps)])
                if mask not in masks:
                    left(4 + group, weights.at[span_of, others])

    left(6, partial.at[:, 0])
    left(7, chip_sum.at[:, pl.ds(1, groups - 1)])
    left(8, flows.at[:, pl.ds(0, groups - 1)])
    left(9, flows.at[:, pl.ds(0, groups)])
    left(10, parts.at[:, others])
    left(11, summed.at[:, fewer])
    left(12, blocks.at[:, fewer])
    left(13, states.at[pl.ds(1, devices_seq - 1)])


def fits(tokens, conv_out, in_weight, residues):
    devices_seq, devices_chan = lax.axis_size("seq"), lax.axis_size("chan")
    rows, channels = conv_out.shape
    return (
        devices_chan == 4
        and devices_seq % devices_chan == 0
        and devices_seq > devices_chan
        and in_weight.shape[0] % 128 == 0
        and 2 * channels == 128
        and channels % residues.shape[1] == 0
        and rows % 256 == 0
        and tokens.shape[1] * devices_chan == in_weight.shape[0] * devices_seq
    )


def blocked(tokens, grad_out, in_weight, out_weight, conv_out, residues, decay_length):
    devices_seq, devices_chan = lax.axis_size("seq"), lax.axis_size("chan")
    planes, groups = devices_chan, devices_chan // 2
    twins = devices_seq // planes
    rows, width = tokens.shape
    channels, owned = out_weight.shape[1], out_weight.shape[0]
    modes = residues.shape[0]
    anywhere = pl.BlockSpec(memory_space=pl.ANY)
    dma, half_type, full = pltpu.SemaphoreType.DMA, tokens.dtype, jnp.float32
    lanes = 2 * channels
    grad_in, grad_proj = pl.pallas_call(
        functools.partial(block_kernel, devices_seq, devices_chan),
        out_shape=(
            jax.ShapeDtypeStruct((3, channels, owned), full),
            jax.ShapeDtypeStruct((channels, owned), full),
        ),
        in_specs=[anywhere] * 7,
        out_specs=(anywhere, anywhere),
        scratch_shapes=[
            pltpu.VMEM((rows, width), half_type),
            pltpu.VMEM((rows, width), half_type),
            pltpu.VMEM((channels, rows), half_type),
            pltpu.VMEM((4, planes, channels, owned), half_type),
            pltpu.VMEM((4, twins, planes, channels, owned), half_type),
            pltpu.VMEM((4, twins, devices_chan, channels, owned), half_type),
            pltpu.VMEM((4, 2, groups, channels, rows), full),
            pltpu.VMEM((4, groups, channels, rows), full),
            pltpu.VMEM((4, groups, channels, rows), full),
            pltpu.VMEM((4, groups, channels, rows), full),
            pltpu.VMEM((rows * channels // lanes, lanes), full),
            pltpu.VMEM((4, modes, lanes), full),
            pltpu.VMEM((modes, 8, lanes), full),
            pltpu.VMEM((modes, lanes), full),
            pltpu.VMEM((devices_seq, modes, lanes), full),
            pltpu.VMEM((4, devices_chan, channels, rows), half_type),
            pltpu.VMEM((4, twins, devices_chan, channels, owned), half_type),
            pltpu.VMEM((4, twins, devices_chan, channels, owned), half_type),
            pltpu.VMEM((4, devices_chan, channels, owned), half_type),
            pltpu.VMEM((4, planes, channels, owned), half_type),
            pltpu.VMEM((4, planes, channels, owned), half_type),
            pltpu.VMEM((4, channels, owned), full),
            pltpu.VMEM((2,) + residues.shape, full),
            dma((9,)),
            dma((17,)),
            dma((4, planes)),
            dma((4, twins)),
            dma((4, twins)),
            dma((4, twins - 1, planes)),
        ]
        + [dma((4, groups))] * 2
        + [dma]
        + [dma((4, groups))] * 2
        + [dma((4, twins - 1, planes))]
        + [dma((4, planes))] * 2
        + [dma((4,))],
        compiler_params=pltpu.CompilerParams(collective_id=2, has_side_effects=True),
        name="conv_block",
    )(
        tokens,
        grad_out,
        in_weight.transpose(1, 2, 0),
        out_weight.T,
        conv_out.T,
        residues,
        decay_length,
    )
    return grad_in.transpose(2, 0, 1), grad_proj.T


def local(tokens, grad_out, in_weight, out_weight, conv_out, residues, decay_length):
    if fits(tokens, conv_out, in_weight, residues):
        return blocked(tokens, grad_out, in_weight, out_weight, conv_out, residues, decay_length)
    channels = out_weight.shape[1]
    owned_rows = in_weight.shape[0]
    weights = jnp.concatenate([in_weight.reshape(owned_rows, 3 * channels), out_weight], axis=1)
    full_tokens, full_grads, projected, upstream = gathered(tokens, grad_out, weights)
    projected = projected[:, : 3 * channels]
    upstream = upstream[:, channels:]
    streams = lax.reduce_precision(projected, exponent_bits=8, mantissa_bits=7)
    gate_first = streams[:, :channels]
    gate_second = streams[:, channels : 2 * channels]
    value_stream = streams[:, 2 * channels :]
    conv_value = conv_out.astype(jnp.float32)
    gated = (gate_second * conv_value).astype(jnp.bfloat16)
    grad_second = (upstream * conv_value).astype(jnp.bfloat16)
    grad_conv = upstream * gate_second
    inner, state, rate, weight = correlate_block(grad_conv, residues, decay_length)
    blank = jnp.zeros_like(gated)
    owned = reduced(
        state,
        rate,
        weight,
        inner,
        value_stream,
        gate_first,
        jnp.concatenate([grad_second, blank], axis=1),
        jnp.concatenate([blank, gated], axis=1),
        full_tokens,
        full_grads,
        owned_rows,
    )
    grad_in = jnp.stack(
        [owned[1, :, :channels], owned[0, :, :channels], owned[1, :, channels:]], axis=1
    )
    return (grad_in, owned[0, :, channels:])


def solution(mesh):
    return jax.shard_map(
        local,
        mesh=mesh,
        in_specs=(
            P("seq", "chan"),
            P("seq", "chan"),
            P("seq", None, "chan"),
            P("seq", "chan"),
            P("seq", "chan"),
            P(None, "chan"),
            P(None, "chan"),
        ),
        out_specs=(P("seq", None, "chan"), P("seq", "chan")),
        check_vma=False,
    )
```

```python
import functools
import math

import jax
import jax.numpy as jnp
from jax import lax
from jax.experimental import pallas as pl
from jax.experimental.pallas import tpu as pltpu
from jax.sharding import PartitionSpec as P

precise = lax.Precision.HIGHEST
MESH = pl.DeviceIdType.MESH


def remote(source, target, send_sem, recv_sem, device):
    return pltpu.make_async_remote_copy(
        src_ref=source,
        dst_ref=target,
        send_sem=send_sem,
        recv_sem=recv_sem,
        device_id=device,
        device_id_type=MESH,
    )


def greet(devices_seq, devices_chan, seq_wide):
    seq, chan = lax.axis_index("seq"), lax.axis_index("chan")
    barrier = pltpu.get_barrier_semaphore()
    count = 0
    if seq_wide == "all":

        def hello(step, carry):
            pl.semaphore_signal(
                barrier,
                inc=1,
                device_id=(lax.rem(seq + step, devices_seq), chan),
                device_id_type=MESH,
            )
            return carry

        lax.fori_loop(1, devices_seq, hello, 0)
        count += devices_seq - 1
    else:
        groups = devices_seq // 2

        def hello_group(step, carry):
            there = lax.rem(seq // 2 + step, groups) * 2 + seq % 2
            pl.semaphore_signal(barrier, inc=1, device_id=(there, chan), device_id_type=MESH)
            return carry

        lax.fori_loop(1, groups, hello_group, 0)
        pl.semaphore_signal(
            barrier, inc=1, device_id=(seq + 1 - 2 * (seq % 2), chan), device_id_type=MESH
        )
        count += groups
    if devices_chan:
        groups = devices_chan // 2
        for step in range(1, groups):
            there = lax.rem(chan // 2 + step, groups) * 2 + chan % 2
            pl.semaphore_signal(barrier, inc=1, device_id=(seq, there), device_id_type=MESH)
        pl.semaphore_signal(
            barrier, inc=1, device_id=(seq, chan + 1 - 2 * (chan % 2)), device_id_type=MESH
        )
        count += groups
    pl.semaphore_wait(barrier, count)


def gather_kernel(
    devices_seq,
    devices_chan,
    tokens,
    grads,
    weights,
    tokens_out,
    grads_out,
    projected,
    upstream,
    all_tokens,
    all_grads,
    all_weights,
    keep_sem,
    store_sem,
    chan_send,
    chan_recv,
    chan_pass,
    chan_passed,
    seq_send,
    seq_recv,
    seq_pass,
    seq_passed,
):
    seq, chan = lax.axis_index("seq"), lax.axis_index("chan")
    seq_groups, chan_groups = devices_seq // 2, devices_chan // 2
    seq_pair = (seq + 1 - 2 * (seq % 2), chan)
    chan_pair = (seq, chan + 1 - 2 * (chan % 2))
    columns = tokens.shape[1]
    rows = weights.shape[0]
    greet(devices_seq, devices_chan, "pairs")

    def block(ref, lines, index):
        return ref.at[lines, pl.ds(pl.multiple_of(index * columns, columns), columns)]

    def piece(index):
        return all_weights.at[pl.ds(pl.multiple_of(index * rows, rows), rows)]

    def chan_member(step, parity):
        return lax.rem(chan // 2 - step + chan_groups, chan_groups) * 2 + parity

    def seq_member(step, parity):
        return lax.rem(seq // 2 - step + seq_groups, seq_groups) * 2 + parity

    height = tokens.shape[0] // 2
    parts = [
        (own, whole, out, pl.ds(half * height, height))
        for own, whole, out in ((tokens, all_tokens, tokens_out), (grads, all_grads, grads_out))
        for half in range(2)
    ]

    def chan_copy(array, step):
        own, whole, _, lines = parts[array]
        there = lax.rem(chan // 2 + step, chan_groups) * 2 + chan % 2
        return remote(
            own.at[lines],
            block(whole, lines, chan),
            chan_send.at[array, step],
            chan_recv.at[array, step],
            (seq, there),
        )

    def chan_forward(array, step):
        own, whole, _, lines = parts[array]
        here = chan_member(step, chan % 2)
        return remote(
            own.at[lines] if step == 0 else block(whole, lines, here),
            block(whole, lines, here),
            chan_pass.at[array, step],
            chan_passed.at[array, step],
            chan_pair,
        )

    def seq_copy(step):
        there = lax.rem(seq // 2 + step, seq_groups) * 2 + seq % 2
        return remote(weights, piece(seq), seq_send.at[step], seq_recv.at[step], (there, chan))

    def seq_forward(step):
        here = seq_member(step, seq % 2)
        return remote(piece(here), piece(here), seq_pass.at[step], seq_passed.at[step], seq_pair)

    own_piece = remote(weights, piece(seq), seq_pass.at[0], seq_passed.at[0], seq_pair)

    def each(call):
        def body(step, carry):
            call(step)
            return carry

        lax.fori_loop(1, seq_groups, body, 0)

    def store(array):
        _, whole, out, lines = parts[array]
        return pltpu.make_async_copy(whole.at[lines], out.at[lines], store_sem.at[array])

    for array in range(4):
        for step in range(1, chan_groups):
            chan_copy(array, step).start()
    each(lambda step: seq_copy(step).start())
    own_piece.start()
    for array in range(4):
        chan_forward(array, 0).start()
    keeps = [pltpu.make_async_copy(weights, piece(seq), keep_sem.at[4])]
    for array, (own, whole, _, lines) in enumerate(parts):
        keeps.append(
            pltpu.make_async_copy(own.at[lines], block(whole, lines, chan), keep_sem.at[array])
        )
    for keep in keeps:
        keep.start()

    def pass_on(step):
        seq_copy(step).wait_recv()
        seq_forward(step).start()

    def pass_part(array):
        for step in range(1, chan_groups):
            chan_copy(array, step).wait_recv()
            chan_forward(array, step).start()

    pass_part(0)
    each(pass_on)
    for keep in keeps:
        keep.wait()
    own_piece.wait()

    def finish(step):
        seq_copy(step).wait_send()
        seq_forward(step).wait()

    each(finish)
    tile = math.gcd(height, 128)
    for array, (_, whole, _, lines) in enumerate(parts):
        if array + 1 < len(parts):
            pass_part(array + 1)
        for step in range(chan_groups):
            chan_forward(array, step).wait()
        store(array).start()
        target, first = (projected, 0) if array < 2 else (upstream, all_weights.shape[1] // 2)

        def product(index, carry):
            here = pl.ds(pl.multiple_of(array % 2 * height + index * tile, tile), tile)
            target[here] = jnp.dot(
                whole[here], all_weights[:, first:], preferred_element_type=jnp.float32
            )
            return carry

        lax.fori_loop(0, height // tile, product, 0)
    for array in range(4):
        store(array).wait()
        for step in range(1, chan_groups):
            chan_copy(array, step).wait_send()


def gathered(tokens, grads, weights):
    devices_seq, devices_chan = lax.axis_size("seq"), lax.axis_size("chan")
    dma = pltpu.SemaphoreType.DMA
    seq_groups, chan_groups = devices_seq // 2, devices_chan // 2
    vmem, anywhere = pl.BlockSpec(memory_space=pltpu.VMEM), pl.BlockSpec(memory_space=pl.ANY)
    wide = jax.ShapeDtypeStruct((tokens.shape[0], tokens.shape[1] * devices_chan), tokens.dtype)
    tall = jax.ShapeDtypeStruct((weights.shape[0] * devices_seq, weights.shape[1]), weights.dtype)
    return pl.pallas_call(
        functools.partial(gather_kernel, devices_seq, devices_chan),
        out_shape=(
            wide,
            wide,
            jax.ShapeDtypeStruct((tokens.shape[0], weights.shape[1]), jnp.float32),
            jax.ShapeDtypeStruct((tokens.shape[0], weights.shape[1] // 2), jnp.float32),
        ),
        in_specs=[vmem] * 3,
        out_specs=(anywhere, anywhere, vmem, vmem),
        scratch_shapes=[
            pltpu.VMEM(wide.shape, wide.dtype),
            pltpu.VMEM(wide.shape, wide.dtype),
            pltpu.VMEM(tall.shape, tall.dtype),
            dma((5,)),
            dma((4,)),
        ]
        + [dma((4, chan_groups))] * 4
        + [dma((seq_groups,))] * 4,
        compiler_params=pltpu.CompilerParams(collective_id=0, has_side_effects=True),
        name="gather_inputs",
    )(tokens, grads, weights)


def reduce_kernel(
    devices_seq,
    tile,
    state,
    rate,
    weight,
    inner,
    value,
    gate,
    early_in,
    early_out,
    tokens_hbm,
    grads_hbm,
    total,
    tokens,
    grads,
    states,
    late,
    parts,
    near,
    paired,
    far,
    load_sem,
    state_send,
    state_recv,
    pair_send,
    pair_recv,
    far_send,
    far_recv,
):
    seq, chan = lax.axis_index("seq"), lax.axis_index("chan")
    groups = devices_seq // 2
    group, parity = seq // 2, seq % 2
    rows, channels = inner.shape
    owned = near.shape[2]
    loads = [
        pltpu.make_async_copy(tokens_hbm, tokens, load_sem.at[0]),
        pltpu.make_async_copy(grads_hbm, grads, load_sem.at[1]),
    ]
    for load in loads:
        load.start()
    greet(devices_seq, 0, "all")

    def loop(start, stop, call):
        def body(step, carry):
            call(step)
            return carry

        lax.fori_loop(start, stop, body, 0)

    def state_copy(step):
        there = lax.rem(seq + step, devices_seq)
        return remote(
            state, states.at[step], state_send.at[step], state_recv.at[step], (there, chan)
        )

    def member(step):
        return lax.rem(group + step, groups)

    def piece(half, index):
        return parts.at[half, pl.ds(pl.multiple_of(index * owned, owned), owned)]

    def pair_copy(half, step):
        return remote(
            piece(half, member(step) * 2 + 1 - parity),
            near.at[half, step],
            pair_send.at[half, step],
            pair_recv.at[half, step],
            (group * 2 + 1 - parity, chan),
        )

    def far_copy(half, step):
        return remote(
            paired.at[half, step],
            far.at[half, step],
            far_send.at[half, step],
            far_recv.at[half, step],
            (member(step) * 2 + parity, chan),
        )

    def summed(left, right):
        return lax.dot_general(
            left, right, (((0,), (0,)), ((), ())), preferred_element_type=jnp.float32
        )

    def span(index):
        return pl.ds(pl.multiple_of(index * tile, tile), tile)

    loop(1, devices_seq, lambda step: state_copy(step).start())
    for load in loads:
        load.wait()

    def early_tile(index):
        product = summed(tokens[:, span(index)], early_in[...])
        product += summed(grads[:, span(index)], early_out[...])
        parts[0, span(index)] = product.astype(parts.dtype)

    loop(0, tokens.shape[1] // tile, early_tile)
    loop(1, groups, lambda step: pair_copy(0, step).start())
    pair_copy(0, 0).start()

    def absorb(step, following):
        state_copy(step).wait_recv()
        gap = lax.rem(seq - step + devices_seq, devices_seq) - seq - 1
        reach = (jnp.maximum(gap, 0) * rows).astype(jnp.float32)
        present = (gap >= 0).astype(jnp.float32)
        return following + present * states[step] * jnp.exp(-reach * rate[...])

    following = lax.fori_loop(1, devices_seq, absorb, jnp.zeros(rate.shape, jnp.float32))
    entering = weight[...] * following
    rates = rate[...]
    band = math.gcd(rows, 64)

    def source_rows(index):
        here = pl.ds(pl.multiple_of(index * band, band), band)
        position = lax.broadcasted_iota(jnp.int32, (band, channels), 0) + index * band
        reach = (rows - position).astype(jnp.float32)
        source = inner[here]
        for mode in range(rates.shape[0]):
            source += entering[mode : mode + 1] * jnp.exp(-reach * rates[mode : mode + 1])
        late[here] = jnp.concatenate([source * value[here], source * gate[here]], axis=1).astype(
            late.dtype
        )

    loop(0, rows // band, source_rows)

    def late_tile(index):
        parts[1, span(index)] = summed(tokens[:, span(index)], late[...]).astype(parts.dtype)

    loop(0, tokens.shape[1] // tile, late_tile)
    loop(1, groups, lambda step: pair_copy(1, step).start())
    pair_copy(1, 0).start()

    def pair_sum(half, step):
        own = piece(half, member(step) * 2 + parity)[...].astype(jnp.float32)
        return own + near[half, step].astype(jnp.float32)

    for half in range(2):

        def pass_on(step):
            pair_copy(half, step).wait_recv()
            paired[half, step] = pair_sum(half, step).astype(paired.dtype)
            far_copy(half, step).start()

        loop(1, groups, pass_on)
    for half in range(2):
        pair_copy(half, 0).wait_recv()
        total[half] = pair_sum(half, 0)

        def collect(step):
            far_copy(half, step).wait_recv()
            total[half] += far[half, step].astype(jnp.float32)

        loop(1, groups, collect)

        def finish(step):
            pair_copy(half, step).wait_send()
            far_copy(half, step).wait_send()

        loop(1, groups, finish)
        pair_copy(half, 0).wait_send()
    loop(1, devices_seq, lambda step: state_copy(step).wait_send())


def reduced(state, rate, weight, inner, value, gate, early_in, early_out, tokens, grads, owned):
    devices_seq = lax.axis_size("seq")
    groups = devices_seq // 2
    rows, channels = inner.shape
    width = tokens.shape[1]
    wide = 2 * channels
    vmem, anywhere = pl.BlockSpec(memory_space=pltpu.VMEM), pl.BlockSpec(memory_space=pl.ANY)
    dma, half_type = pltpu.SemaphoreType.DMA, tokens.dtype
    return pl.pallas_call(
        functools.partial(reduce_kernel, devices_seq, math.gcd(width, 512)),
        out_shape=jax.ShapeDtypeStruct((2, owned, wide), jnp.float32),
        in_specs=[vmem] * 8 + [anywhere] * 2,
        out_specs=vmem,
        scratch_shapes=[pltpu.VMEM(tokens.shape, half_type)] * 2
        + [pltpu.VMEM((devices_seq,) + state.shape, jnp.float32)]
        + [pltpu.VMEM((rows, wide), half_type), pltpu.VMEM((2, width, wide), half_type)]
        + [pltpu.VMEM((2, groups, owned, wide), half_type)] * 3
        + [dma((2,)), dma((devices_seq,)), dma((devices_seq,))]
        + [dma((2, groups))] * 4,
        compiler_params=pltpu.CompilerParams(collective_id=1, has_side_effects=True),
        name="reduce_owned",
    )(state, rate, weight, inner, value, gate, early_in, early_out, tokens, grads)


def correlate_block(signal, residues, decay_length):
    rows, channels = signal.shape
    chunk = min(64, rows)
    chunks = rows // chunk
    per_filter = channels // residues.shape[1]
    rate = jnp.repeat(1.0 / decay_length, per_filter, axis=1)
    weight = jnp.repeat(residues, per_filter, axis=1) * jnp.sqrt(-jnp.expm1(-2.0 * rate))
    offset = jnp.arange(chunk, dtype=jnp.float32)
    exponent = rate.T[:, :, None] * offset
    grow = weight.T[:, :, None] * jnp.exp(exponent)
    fall = jnp.exp(-exponent)
    later = jnp.arange(chunk)[None, :] >= jnp.arange(chunk)[:, None]
    taps = jnp.einsum("cri,crj->cij", grow, fall, precision=precise)
    taps = jnp.where(later, taps, 0.0)
    pieces = signal.reshape(chunks, chunk, channels).transpose(2, 1, 0)
    both = jnp.einsum(
        "cij,cjn->cin", jnp.concatenate([taps, fall], axis=1), pieces, precision=precise
    )
    inner, sums = both[:, :chunk], both[:, chunk:]
    step = jnp.exp(-chunk * rate).T
    state = jnp.zeros_like(step)
    entering = []
    for index in reversed(range(chunks)):
        entering.append(step * state)
        state = sums[:, :, index] + step * state
    entering = jnp.stack(entering[::-1], axis=2)
    outer = jnp.einsum("cri,crn->cin", grow, entering, precision=precise)
    return (inner + outer).transpose(2, 1, 0).reshape(rows, channels), state.T, rate, weight


def block_kernel(
    devices_seq,
    devices_chan,
    tokens_hbm,
    grads_hbm,
    in_weight,
    out_weight,
    conv_hbm,
    residues,
    decay_length,
    grad_in,
    grad_out,
    tokens,
    grads,
    conv,
    pieces,
    crossed,
    weights,
    partial,
    pair_in,
    chip_sum,
    far_in,
    signal,
    consts,
    bank,
    own_state,
    states,
    flows,
    parts,
    near,
    summed,
    blocks,
    arrived,
    results,
    given,
    load_sem,
    sent,
    hop_recv,
    swap_recv,
    keep_sem,
    twin_recv,
    pair_recv,
    far_recv,
    state_recv,
    flow_recv,
    pass_recv,
    near_recv,
    turn_recv,
    home_recv,
    put_sem,
):
    seq, chan = lax.axis_index("seq"), lax.axis_index("chan")
    planes = devices_chan
    twins = devices_seq // planes
    groups = devices_chan // 2
    plane, twin = seq // twins, seq % twins
    group, parity = chan // 2, chan % 2
    partner = (seq, chan + 1 - 2 * parity)
    channels, rows = conv.shape
    owned = out_weight.shape[1]

    def ahead(index, step, count):
        return lax.rem(index + step, count)

    def behind(index, step, count):
        return lax.rem(index - step + count, count)

    sources = (in_weight.at[1], out_weight, in_weight.at[0], in_weight.at[2])
    count = len(sources)
    weight_loads = [
        pltpu.make_async_copy(sources[part], pieces.at[part, plane], load_sem.at[part])
        for part in range(count)
    ]
    bulk_loads = [
        pltpu.make_async_copy(tokens_hbm, tokens, load_sem.at[count]),
        pltpu.make_async_copy(grads_hbm, grads, load_sem.at[count + 1]),
        pltpu.make_async_copy(conv_hbm, conv, load_sem.at[count + 2]),
    ]
    filter_loads = [
        pltpu.make_async_copy(residues, given.at[0], load_sem.at[count + 3]),
        pltpu.make_async_copy(decay_length, given.at[1], load_sem.at[count + 4]),
    ]
    for load in weight_loads + filter_loads + bulk_loads:
        load.start()

    barrier = pltpu.get_barrier_semaphore()
    for step in range(1, devices_seq):
        pl.semaphore_signal(
            barrier, inc=1, device_id=(ahead(seq, step, devices_seq), chan), device_id_type=MESH
        )
    for step in range(1, devices_chan):
        pl.semaphore_signal(
            barrier, inc=1, device_id=(seq, ahead(chan, step, devices_chan)), device_id_type=MESH
        )
    pl.semaphore_wait(barrier, devices_seq + devices_chan - 2)

    bits = [1 << power for power in reversed(range(planes.bit_length() - 1))]

    def flip(index, mask):
        result = index
        for bit in bits:
            if mask & bit:
                result = result + bit - 2 * bit * (index // bit % 2)
        return result

    def hop(part, which, kind, side):
        return remote(
            pieces.at[part, which],
            pieces.at[part, which],
            sent.at[kind],
            hop_recv.at[part, which],
            ((plane + side) * twins + twin, chan),
        )

    def onward(part, which, kind, side):
        edge = planes - 1 if side > 0 else 0

        @pl.when(plane != edge)
        def _():
            hop(part, which, kind, side).start()

    def cross(part, step, mask):
        here = flip(plane, mask)
        return remote(
            pieces.at[part, here],
            crossed.at[part, step, here],
            sent.at[14 + part // early],
            twin_recv.at[part, step - 1, mask],
            (plane * twins + ahead(twin, step, twins), chan),
        )

    def held(part, step, target):
        return crossed.at[part, step, target] if step else pieces.at[part, target]

    def swap(part, step, target):
        return remote(
            held(part, step, target),
            weights.at[part, behind(twin, step, twins), chan],
            sent.at[2 + part // early if step else 1],
            swap_recv.at[part, step],
            (seq, target),
        )

    def swap_in(part, step):
        landed = weights.at[part, behind(twin, step, twins), pl.ds(0, devices_chan - 1)]
        return remote(landed, landed, sent.at[2 + part // early if step else 1], swap_recv.at[part, step], partner)

    def keep(part, step):
        return pltpu.make_async_copy(
            held(part, step, chan),
            weights.at[part, behind(twin, step, twins), chan],
            keep_sem.at[part, step],
        )

    def deliver(part, step, mask):
        target = flip(plane, mask)

        @pl.when(target == chan)
        def _():
            keep(part, step).start()

        @pl.when(target != chan)
        def _():
            swap(part, step, target).start()

    early = count // 2

    crossing = ((0, 1, 3), (3,))

    def crosses(part, mask):
        return mask in crossing[part // early]

    def here(part, mask):
        if crosses(part, mask):
            for step in range(1, twins):
                cross(part, step, mask).start()
        deliver(part, 0, mask)

    def depart(group):
        for part in group:
            for side in (1, -1):
                onward(part, plane, 0, side)

    def arrive(group, distance):
        for part in group:
            for mask in range(1, planes):
                which = flip(plane, mask)
                for side in (1, -1):

                    @pl.when(plane - which == side * distance)
                    def _(mask=mask, which=which, side=side, part=part):
                        hop(part, which, 0, side).wait_recv()
                        onward(part, which, 16, side)
                        here(part, mask)

    def cross_on(part, mask):
        for step in range(1, twins):
            cross(part, step, mask).wait_recv()
            deliver(part, step, mask)

    def twin_copy(part, step):
        return remote(
            weights.at[part, twin],
            weights.at[part, twin],
            sent.at[4 + part // early],
            twin_recv.at[part, step - 1, 2],
            (plane * twins + ahead(twin, step, twins), chan),
        )

    def twin_in(part, step):
        there = behind(twin, step, twins)
        return remote(
            weights.at[part, there],
            weights.at[part, there],
            sent.at[4 + part // early],
            twin_recv.at[part, step - 1, 2],
            (plane * twins + there, chan),
        )

    def share(part, mask):
        @pl.when(flip(plane, mask) == chan)
        def _():
            swap_in(part, 0).wait_recv()
            keep(part, 0).wait()
            for step in range(1, twins):
                twin_copy(part, step).start()

    def loaded(part):
        weight_loads[part].wait()

    first, last = range(early), range(early, count)
    for part in range(count):
        loaded(part)
    depart(first)
    for part in first:
        here(part, 0)

    lanes = signal.shape[1]
    folds = lanes // channels
    groups_of_rows = 8
    span = signal.shape[0] // groups_of_rows
    modes, filters = residues.shape
    per_filter = channels // filters
    lane = lax.broadcasted_iota(jnp.int32, (filters, lanes), 1)
    which = lax.broadcasted_iota(jnp.int32, (filters, lanes), 0)
    spread = (lax.rem(lane, channels) // per_filter == which).astype(jnp.float32)
    for load in filter_loads:
        load.wait()
    inverse = 1.0 / given[1]
    twice = 2.0 * inverse
    series = jnp.zeros_like(twice)
    for order in range(10, 0, -1):
        series = (1.0 - series) * twice / order
    loss = jnp.where(twice < 0.5, series, 1.0 - jnp.exp(-twice))
    scale = given[0] * jnp.sqrt(loss)

    def widen(array):
        return jnp.dot(array, spread, precision=precise, preferred_element_type=jnp.float32)

    rate = widen(inverse)
    consts[0] = rate
    consts[1] = widen(scale)
    consts[2] = jnp.exp(-rate)

    inputs = (tokens, grads, tokens, tokens)

    def ready(part, step, mask):
        @pl.when(flip(plane, mask) == chan)
        def _():
            if crosses(part, mask):
                swap_in(part, step).wait_recv()
                keep(part, step).wait()
            elif step:
                twin_in(part, step).wait_recv()

    def project(part):
        for step in range(twins):
            block = behind(twin, step, twins)
            for mask in range(planes):
                ready(part, step, mask)
            columns = pl.ds(pl.multiple_of(block * owned, owned), owned)
            product = lax.dot_general(
                weights[part, block].reshape(devices_chan * channels, owned),
                inputs[part][:, columns],
                (((1,), (1,)), ((), ())),
                preferred_element_type=jnp.float32,
            )
            for target in range(devices_chan):
                piece = product[target * channels : (target + 1) * channels]
                place = (part, target % 2, target // 2)
                if step:
                    piece = partial[place] + piece
                partial[place] = piece

    def pair_copy(part, there):
        return remote(
            partial.at[part, 1 - parity, there],
            pair_in.at[part, there],
            sent.at[6],
            pair_recv.at[part, there],
            partner,
        )

    def far_copy(part, step):
        return remote(
            chip_sum.at[part, step],
            far_in.at[part, step],
            sent.at[7],
            far_recv.at[part, step],
            (seq, ahead(group, step, groups) * 2 + parity),
        )

    def pair_start(part):
        for step in range(1, groups + 1):
            pair_copy(part, ahead(group, step, groups)).start()

    def far_start(part):
        for step in range(1, groups):
            there = ahead(group, step, groups)
            pair_copy(part, there).wait_recv()
            chip_sum[part, step] = partial[part, parity, there] + pair_in[part, there]
            far_copy(part, step).start()

    def far_finish(part):
        pair_copy(part, group).wait_recv()
        total = partial[part, parity, group] + pair_in[part, group]
        for step in range(1, groups):
            far_copy(part, step).wait_recv()
            total = total + far_in[part, step]
        return total

    def flow(part, step):
        return remote(
            flows.at[part, chan],
            flows.at[part, chan],
            sent.at[8],
            flow_recv.at[part, step],
            (seq, ahead(group, step, groups) * 2 + parity),
        )

    def flow_in(part, step):
        source = behind(group, step, groups) * 2 + parity
        return remote(
            flows.at[part, source],
            flows.at[part, source],
            sent.at[8],
            flow_recv.at[part, step],
            (seq, source),
        )

    def flow_pass(part, step):
        source = behind(group, step, groups) * 2 + parity
        return remote(
            flows.at[part, source],
            flows.at[part, source],
            sent.at[9],
            pass_recv.at[part, step],
            partner,
        )

    def flow_passed(part, step):
        source = behind(group, step, groups) * 2 + 1 - parity
        return remote(
            flows.at[part, source],
            flows.at[part, source],
            sent.at[9],
            pass_recv.at[part, step],
            partner,
        )

    def flow_start(part):
        for step in range(1, groups):
            flow(part, step).start()
        flow_pass(part, 0).start()

    def flow_on(part):
        for step in range(1, groups):
            flow_in(part, step).wait_recv()
            flow_pass(part, step).start()

    def flow_finish(part):
        for step in range(groups):
            flow_passed(part, step).wait_recv()

    def near_copy(part, step, target):
        return remote(
            parts.at[part, ahead(twin, step, twins), target],
            near.at[part, step, target],
            sent.at[10],
            near_recv.at[part, step - 1, target],
            (plane * twins + ahead(twin, step, twins), chan),
        )

    def multiply(part):
        for step in range(1, twins + 1):
            block = ahead(twin, step, twins)
            columns = pl.ds(pl.multiple_of(block * owned, owned), owned)
            product = jnp.dot(
                flows[part].reshape(devices_chan * channels, rows),
                inputs[part][:, columns],
                preferred_element_type=jnp.float32,
            ).astype(parts.dtype)
            for target in range(devices_chan):
                parts[part, block, target] = product[target * channels : (target + 1) * channels]
            if step < twins:
                for index in range(1, devices_chan + 1):
                    near_copy(part, step, ahead(chan, index, devices_chan)).start()

    def turn(part, target):
        return remote(
            summed.at[part, target],
            blocks.at[part, chan],
            sent.at[11],
            turn_recv.at[part, chan],
            (seq, target),
        )

    def turn_in(part, source):
        return remote(
            summed.at[part, source],
            blocks.at[part, source],
            sent.at[11],
            turn_recv.at[part, source],
            (seq, source),
        )

    straight = (0, 1, 2, 3)

    def home(part, mask):
        return remote(
            blocks.at[part, flip(plane, mask)],
            arrived.at[part, mask],
            sent.at[12],
            home_recv.at[part, mask],
            (flip(plane, mask if part in straight else mask & -mask) * twins + twin, chan),
        )

    def turn_start(part, index):
        target = ahead(chan, index, devices_chan)
        total = parts[part, twin, target].astype(jnp.float32)
        for step in range(1, twins):
            near_copy(part, step, target).wait_recv()
            total = total + near[part, step, target].astype(jnp.float32)
        total = total.astype(blocks.dtype)
        if index < devices_chan:
            summed[part, target] = total
            turn(part, target).start()
        else:
            blocks[part, chan] = total

    def turned(part, index):
        source = behind(chan, index, devices_chan)
        if index < devices_chan:
            turn_in(part, source).wait_recv()

        for mask in range(1, planes, 1 if part in straight else 2):

            @pl.when(flip(plane, mask) == source)
            def _(mask=mask):
                home(part, mask).start()

    def gathered(part, mask):
        total = blocks[part, flip(plane, mask)].astype(jnp.float32)
        for other in range(1, planes) if part in straight else reversed(bits):
            if mask == 0 or other < mask & -mask:
                home(part, mask ^ other).wait_recv()
                total = total + arrived[part, mask ^ other].astype(jnp.float32)
        return total

    targets = (grad_in.at[1], grad_out, grad_in.at[0], grad_in.at[2])

    def put(part):
        return pltpu.make_async_copy(results.at[part], targets[part], put_sem.at[part])

    def finish(part):
        results[part] = gathered(part, 0)
        put(part).start()

    def home_on(part):
        for mask in range(planes - 1, 0, -1):
            if mask & -mask > 1 and part not in straight:
                blocks[part, flip(plane, mask)] = gathered(part, mask).astype(blocks.dtype)
                home(part, mask).start()

    def rowed(array):
        width = array.shape[1] // folds
        stacked = jnp.concatenate(
            [array[:, fold * width : (fold + 1) * width] for fold in range(folds)], axis=0
        )
        return stacked.T

    def unrowed(array):
        stacked = array.T
        return jnp.concatenate(
            [stacked[fold * channels : (fold + 1) * channels] for fold in range(folds)], axis=1
        )

    def mode_row(kind, mode):
        return jnp.broadcast_to(consts[kind, mode : mode + 1], (groups_of_rows, lanes))

    def line(index):
        return pl.ds(index, groups_of_rows, stride=span)

    def scan_states():
        fall = [mode_row(2, mode) for mode in range(modes)]

        def body(step, carry):
            here = signal[line(span - 1 - step)]
            return tuple(carry[mode] * fall[mode] + here for mode in range(modes))

        zero = jnp.zeros((groups_of_rows, lanes), jnp.float32)
        found = lax.fori_loop(0, span, body, (zero,) * modes)
        position = lax.broadcasted_iota(jnp.int32, (groups_of_rows, lanes), 0)
        for mode in range(modes):
            each = mode_row(0, mode) * span
            total = found[mode]
            shift = 1
            while shift < groups_of_rows:
                moved = pltpu.roll(total, groups_of_rows - shift, 0)
                moved = moved * jnp.exp(-each * shift)
                total = total + jnp.where(position < groups_of_rows - shift, moved, 0.0)
                shift *= 2
            moved = pltpu.roll(total, groups_of_rows - 1, 0)
            bank[mode] = jnp.where(position < groups_of_rows - 1, moved, 0.0)
            own_state[mode : mode + 1] = total[0:1]
        heads = own_state[...]
        reach = consts[0] * (span * groups_of_rows)
        later = pltpu.roll(heads, channels, 1)
        first = lax.broadcasted_iota(jnp.int32, (modes, lanes), 1) < channels
        consts[3] = jnp.where(first, later, 0.0)
        own_state[...] = jnp.where(first, heads + later * jnp.exp(-reach), 0.0)

    def state_copy(step):
        return remote(
            own_state,
            states.at[step],
            sent.at[13],
            state_recv,
            (ahead(seq, step, devices_seq), chan),
        )

    def scan_source():
        rates = consts[0]
        following = jnp.zeros((modes, lanes), jnp.float32)
        landed = states.at[pl.ds(1, devices_seq - 1)]
        remote(landed, landed, sent.at[13], state_recv, partner).wait_recv()
        for step in range(1, devices_seq):
            gap = behind(seq, step, devices_seq) - seq - 1
            reach = (jnp.maximum(gap, 0) * rows).astype(jnp.float32)
            present = (gap >= 0).astype(jnp.float32)
            following = following + present * states[step] * jnp.exp(-reach * rates)
        first = lax.broadcasted_iota(jnp.int32, (modes, lanes), 1) < channels
        after = pltpu.roll(following, channels, 1)
        within = following * jnp.exp(-(rates * (span * groups_of_rows)))
        consts[3] = jnp.where(first, consts[3] + within, after)
        fall = [mode_row(2, mode) for mode in range(modes)]
        weigh = [mode_row(1, mode) for mode in range(modes)]
        position = lax.broadcasted_iota(jnp.int32, (groups_of_rows, lanes), 0)
        left = ((groups_of_rows - 1 - position) * span).astype(jnp.float32)
        start = tuple(
            bank[mode] + mode_row(3, mode) * jnp.exp(-left * mode_row(0, mode))
            for mode in range(modes)
        )

        def body(step, carry):
            here = line(span - 1 - step)
            entry = signal[here]
            following = tuple(carry[mode] * fall[mode] + entry for mode in range(modes))
            terms = [following[mode] * weigh[mode] for mode in range(modes)]
            while len(terms) > 1:
                terms = [sum(terms[at : at + 2]) for at in range(0, len(terms), 2)]
            signal[here] = terms[0]
            return following

        lax.fori_loop(0, span, body, start)

    def settle(group, mask):
        for part in group:
            if crosses(part, mask):
                cross_on(part, mask)
            else:
                share(part, mask)

    arrive(first, 1)
    settle(first, 0)
    arrive(first, 2)
    depart(last)
    for part in last:
        here(part, 0)
    settle(first, 1)
    arrive(first, 3)
    settle(first, 2)
    arrive(last, 1)
    settle(last, 0)
    settle(first, 3)
    arrive(last, 2)
    settle(last, 1)
    for load in bulk_loads:
        load.wait()
    project(0)
    pair_start(0)
    arrive(last, 3)
    project(1)
    pair_start(1)
    settle(last, 2)
    far_start(0)
    far_start(1)

    taken = conv[...].astype(jnp.float32)
    second = far_finish(0).astype(flows.dtype).astype(jnp.float32)
    flows[1, chan] = (second * taken).astype(flows.dtype)
    flow_start(1)
    settle(last, 3)
    upstream = far_finish(1)
    flows[0, chan] = (upstream * taken).astype(flows.dtype)
    flow_start(0)
    project(2)
    pair_start(2)
    signal[...] = rowed(upstream * second)
    project(3)
    pair_start(3)
    flow_on(1)
    scan_states()
    for step in range(1, devices_seq):
        state_copy(step).start()
    far_start(2)
    flow_finish(1)
    far_start(3)
    multiply(1)
    flow_on(0)
    flow_finish(0)
    multiply(0)
    turn_start(1, 1)
    turn_start(1, 2)
    scan_source()
    source = unrowed(signal[...])
    late = far_finish(2).astype(flows.dtype).astype(jnp.float32)
    flows[3, chan] = (source * late).astype(flows.dtype)
    flow_start(3)
    late = far_finish(3).astype(flows.dtype).astype(jnp.float32)
    flows[2, chan] = (source * late).astype(flows.dtype)
    flow_start(2)
    turn_start(1, 3)
    turned(1, 1)
    turn_start(1, 4)
    turned(1, 2)
    flow_on(3)
    turn_start(0, 1)
    turned(1, 3)
    flow_on(2)
    turn_start(0, 2)
    flow_finish(3)
    multiply(3)
    flow_finish(2)
    multiply(2)
    turned(1, 4)
    turn_start(0, 3)
    turned(0, 1)
    turn_start(0, 4)
    turned(0, 2)
    home_on(1)
    turned(0, 3)
    turned(0, 4)
    turn_start(3, 1)
    turn_start(3, 2)
    turn_start(3, 3)
    turned(3, 1)
    home_on(0)
    turn_start(3, 4)
    turned(3, 2)
    finish(1)
    turn_start(2, 1)
    turned(3, 3)
    turned(3, 4)
    turn_start(2, 2)
    finish(0)
    turn_start(2, 3)
    turned(2, 1)
    home_on(3)
    turn_start(2, 4)
    turned(2, 2)
    turned(2, 3)
    turned(2, 4)
    home_on(2)
    finish(3)
    finish(2)
    for part in range(count):
        put(part).wait()

    def left(kind, ref):
        remote(ref, ref, sent.at[kind], state_recv, partner).wait_send()

    fewer = pl.ds(0, planes - 1)
    others = pl.ds(1, twins - 1)
    inner = jnp.logical_and(plane > 0, plane < planes - 1)

    @pl.when(inner)
    def _():
        left(0, pieces.at[:, pl.ds(0, 2)])
        left(16, pieces.at[:, fewer])

    @pl.when(jnp.logical_not(inner))
    def _():
        left(0, pieces.at[:, pl.ds(0, 1)])

    left(1, pieces.at[:, fewer])
    for group in range(2):
        span_of = pl.ds(group * early, early)
        masks = crossing[group]
        if masks:
            left(14 + group, crossed.at[span_of, others, pl.ds(0, len(masks))])
        for mask in range(planes):

            @pl.when(flip(plane, mask) == chan)
            def _(mask=mask):
                swaps = len(masks) - (mask in masks)
                if swaps:
                    left(2 + group, crossed.at[span_of, others, pl.ds(0, swaps)])
                if mask not in masks:
                    left(4 + group, weights.at[span_of, others])

    left(6, partial.at[:, 0])
    left(7, chip_sum.at[:, pl.ds(1, groups - 1)])
    left(8, flows.at[:, pl.ds(0, groups - 1)])
    left(9, flows.at[:, pl.ds(0, groups)])
    left(10, parts.at[:, others])
    left(11, summed.at[:, fewer])
    left(12, blocks.at[:, fewer])
    left(13, states.at[pl.ds(1, devices_seq - 1)])


def place_kernel(grad_in, grad_proj, out_in, out_proj, held, take_sem, give_sem):
    streams = grad_in.shape[0]
    ends = [(grad_in.at[at], out_in.at[at]) for at in range(streams)] + [(grad_proj, out_proj)]
    takes = [
        pltpu.make_async_copy(source, held.at[at], take_sem.at[at])
        for at, (source, _) in enumerate(ends)
    ]
    gives = [
        pltpu.make_async_copy(held.at[at], target, give_sem.at[at])
        for at, (_, target) in enumerate(ends)
    ]
    for take in takes:
        take.start()
    for take, give in zip(takes, gives):
        take.wait()
        give.start()
    for give in gives:
        give.wait()


def placed(grad_in, grad_proj):
    anywhere, dma = pl.BlockSpec(memory_space=pl.ANY), pltpu.SemaphoreType.DMA
    count = grad_in.shape[0] + 1
    return pl.pallas_call(
        place_kernel,
        out_shape=tuple(jax.ShapeDtypeStruct(a.shape, a.dtype) for a in (grad_in, grad_proj)),
        in_specs=[anywhere] * 2,
        out_specs=(anywhere, anywhere),
        scratch_shapes=[
            pltpu.VMEM((count,) + grad_proj.shape, grad_proj.dtype),
            dma((count,)),
            dma((count,)),
        ],
        name="place_outputs",
    )(grad_in, grad_proj)


def fits(tokens, conv_out, in_weight, residues):
    devices_seq, devices_chan = lax.axis_size("seq"), lax.axis_size("chan")
    rows, channels = conv_out.shape
    return (
        devices_chan == 4
        and devices_seq % devices_chan == 0
        and devices_seq > devices_chan
        and in_weight.shape[0] % 128 == 0
        and 2 * channels == 128
        and channels % residues.shape[1] == 0
        and rows % 256 == 0
        and tokens.shape[1] * devices_chan == in_weight.shape[0] * devices_seq
    )


def blocked(tokens, grad_out, in_weight, out_weight, conv_out, residues, decay_length):
    devices_seq, devices_chan = lax.axis_size("seq"), lax.axis_size("chan")
    planes, groups = devices_chan, devices_chan // 2
    twins = devices_seq // planes
    rows, width = tokens.shape
    channels, owned = out_weight.shape[1], out_weight.shape[0]
    modes = residues.shape[0]
    anywhere = pl.BlockSpec(memory_space=pl.ANY)
    dma, half_type, full = pltpu.SemaphoreType.DMA, tokens.dtype, jnp.float32
    lanes = 2 * channels
    grad_in, grad_proj = pl.pallas_call(
        functools.partial(block_kernel, devices_seq, devices_chan),
        out_shape=(
            jax.ShapeDtypeStruct((3, channels, owned), full),
            jax.ShapeDtypeStruct((channels, owned), full),
        ),
        in_specs=[anywhere] * 7,
        out_specs=(anywhere, anywhere),
        scratch_shapes=[
            pltpu.VMEM((rows, width), half_type),
            pltpu.VMEM((rows, width), half_type),
            pltpu.VMEM((channels, rows), half_type),
            pltpu.VMEM((4, planes, channels, owned), half_type),
            pltpu.VMEM((4, twins, planes, channels, owned), half_type),
            pltpu.VMEM((4, twins, devices_chan, channels, owned), half_type),
            pltpu.VMEM((4, 2, groups, channels, rows), full),
            pltpu.VMEM((4, groups, channels, rows), full),
            pltpu.VMEM((4, groups, channels, rows), full),
            pltpu.VMEM((4, groups, channels, rows), full),
            pltpu.VMEM((rows * channels // lanes, lanes), full),
            pltpu.VMEM((4, modes, lanes), full),
            pltpu.VMEM((modes, 8, lanes), full),
            pltpu.VMEM((modes, lanes), full),
            pltpu.VMEM((devices_seq, modes, lanes), full),
            pltpu.VMEM((4, devices_chan, channels, rows), half_type),
            pltpu.VMEM((4, twins, devices_chan, channels, owned), half_type),
            pltpu.VMEM((4, twins, devices_chan, channels, owned), half_type),
            pltpu.VMEM((4, devices_chan, channels, owned), half_type),
            pltpu.VMEM((4, planes, channels, owned), half_type),
            pltpu.VMEM((4, planes, channels, owned), half_type),
            pltpu.VMEM((4, channels, owned), full),
            pltpu.VMEM((2,) + residues.shape, full),
            dma((9,)),
            dma((17,)),
            dma((4, planes)),
            dma((4, twins)),
            dma((4, twins)),
            dma((4, twins - 1, planes)),
        ]
        + [dma((4, groups))] * 2
        + [dma]
        + [dma((4, groups))] * 2
        + [dma((4, twins - 1, planes))]
        + [dma((4, planes))] * 2
        + [dma((4,))],
        compiler_params=pltpu.CompilerParams(collective_id=2, has_side_effects=True),
        name="conv_block",
    )(
        tokens,
        grad_out,
        in_weight.transpose(1, 2, 0),
        out_weight.T,
        conv_out.T,
        residues,
        decay_length,
    )
    grad_in, grad_proj = placed(grad_in, grad_proj)
    return grad_in.transpose(2, 0, 1), grad_proj.T


def local(tokens, grad_out, in_weight, out_weight, conv_out, residues, decay_length):
    if fits(tokens, conv_out, in_weight, residues):
        return blocked(tokens, grad_out, in_weight, out_weight, conv_out, residues, decay_length)
    channels = out_weight.shape[1]
    owned_rows = in_weight.shape[0]
    weights = jnp.concatenate([in_weight.reshape(owned_rows, 3 * channels), out_weight], axis=1)
    full_tokens, full_grads, projected, upstream = gathered(tokens, grad_out, weights)
    projected = projected[:, : 3 * channels]
    upstream = upstream[:, channels:]
    streams = lax.reduce_precision(projected, exponent_bits=8, mantissa_bits=7)
    gate_first = streams[:, :channels]
    gate_second = streams[:, channels : 2 * channels]
    value_stream = streams[:, 2 * channels :]
    conv_value = conv_out.astype(jnp.float32)
    gated = (gate_second * conv_value).astype(jnp.bfloat16)
    grad_second = (upstream * conv_value).astype(jnp.bfloat16)
    grad_conv = upstream * gate_second
    inner, state, rate, weight = correlate_block(grad_conv, residues, decay_length)
    blank = jnp.zeros_like(gated)
    owned = reduced(
        state,
        rate,
        weight,
        inner,
        value_stream,
        gate_first,
        jnp.concatenate([grad_second, blank], axis=1),
        jnp.concatenate([blank, gated], axis=1),
        full_tokens,
        full_grads,
        owned_rows,
    )
    grad_in = jnp.stack(
        [owned[1, :, :channels], owned[0, :, :channels], owned[1, :, channels:]], axis=1
    )
    return (grad_in, owned[0, :, channels:])


def solution(mesh):
    return jax.shard_map(
        local,
        mesh=mesh,
        in_specs=(
            P("seq", "chan"),
            P("seq", "chan"),
            P("seq", None, "chan"),
            P("seq", "chan"),
            P("seq", "chan"),
            P(None, "chan"),
            P(None, "chan"),
        ),
        out_specs=(P("seq", None, "chan"), P("seq", "chan")),
        check_vma=False,
    )
```

```python
import functools
import math

import jax
import jax.numpy as jnp
from jax import lax
from jax.experimental import pallas as pl
from jax.experimental.pallas import tpu as pltpu
from jax.sharding import PartitionSpec as P

precise = lax.Precision.HIGHEST
MESH = pl.DeviceIdType.MESH


def remote(source, target, send_sem, recv_sem, device):
    return pltpu.make_async_remote_copy(
        src_ref=source,
        dst_ref=target,
        send_sem=send_sem,
        recv_sem=recv_sem,
        device_id=device,
        device_id_type=MESH,
    )


def greet(devices_seq, devices_chan, seq_wide):
    seq, chan = lax.axis_index("seq"), lax.axis_index("chan")
    barrier = pltpu.get_barrier_semaphore()
    count = 0
    if seq_wide == "all":

        def hello(step, carry):
            pl.semaphore_signal(
                barrier,
                inc=1,
                device_id=(lax.rem(seq + step, devices_seq), chan),
                device_id_type=MESH,
            )
            return carry

        lax.fori_loop(1, devices_seq, hello, 0)
        count += devices_seq - 1
    else:
        groups = devices_seq // 2

        def hello_group(step, carry):
            there = lax.rem(seq // 2 + step, groups) * 2 + seq % 2
            pl.semaphore_signal(barrier, inc=1, device_id=(there, chan), device_id_type=MESH)
            return carry

        lax.fori_loop(1, groups, hello_group, 0)
        pl.semaphore_signal(
            barrier, inc=1, device_id=(seq + 1 - 2 * (seq % 2), chan), device_id_type=MESH
        )
        count += groups
    if devices_chan:
        groups = devices_chan // 2
        for step in range(1, groups):
            there = lax.rem(chan // 2 + step, groups) * 2 + chan % 2
            pl.semaphore_signal(barrier, inc=1, device_id=(seq, there), device_id_type=MESH)
        pl.semaphore_signal(
            barrier, inc=1, device_id=(seq, chan + 1 - 2 * (chan % 2)), device_id_type=MESH
        )
        count += groups
    pl.semaphore_wait(barrier, count)


def gather_kernel(
    devices_seq,
    devices_chan,
    tokens,
    grads,
    weights,
    tokens_out,
    grads_out,
    projected,
    upstream,
    all_tokens,
    all_grads,
    all_weights,
    keep_sem,
    store_sem,
    chan_send,
    chan_recv,
    chan_pass,
    chan_passed,
    seq_send,
    seq_recv,
    seq_pass,
    seq_passed,
):
    seq, chan = lax.axis_index("seq"), lax.axis_index("chan")
    seq_groups, chan_groups = devices_seq // 2, devices_chan // 2
    seq_pair = (seq + 1 - 2 * (seq % 2), chan)
    chan_pair = (seq, chan + 1 - 2 * (chan % 2))
    columns = tokens.shape[1]
    rows = weights.shape[0]
    greet(devices_seq, devices_chan, "pairs")

    def block(ref, lines, index):
        return ref.at[lines, pl.ds(pl.multiple_of(index * columns, columns), columns)]

    def piece(index):
        return all_weights.at[pl.ds(pl.multiple_of(index * rows, rows), rows)]

    def chan_member(step, parity):
        return lax.rem(chan // 2 - step + chan_groups, chan_groups) * 2 + parity

    def seq_member(step, parity):
        return lax.rem(seq // 2 - step + seq_groups, seq_groups) * 2 + parity

    height = tokens.shape[0] // 2
    parts = [
        (own, whole, out, pl.ds(half * height, height))
        for own, whole, out in ((tokens, all_tokens, tokens_out), (grads, all_grads, grads_out))
        for half in range(2)
    ]

    def chan_copy(array, step):
        own, whole, _, lines = parts[array]
        there = lax.rem(chan // 2 + step, chan_groups) * 2 + chan % 2
        return remote(
            own.at[lines],
            block(whole, lines, chan),
            chan_send.at[array, step],
            chan_recv.at[array, step],
            (seq, there),
        )

    def chan_forward(array, step):
        own, whole, _, lines = parts[array]
        here = chan_member(step, chan % 2)
        return remote(
            own.at[lines] if step == 0 else block(whole, lines, here),
            block(whole, lines, here),
            chan_pass.at[array, step],
            chan_passed.at[array, step],
            chan_pair,
        )

    def seq_copy(step):
        there = lax.rem(seq // 2 + step, seq_groups) * 2 + seq % 2
        return remote(weights, piece(seq), seq_send.at[step], seq_recv.at[step], (there, chan))

    def seq_forward(step):
        here = seq_member(step, seq % 2)
        return remote(piece(here), piece(here), seq_pass.at[step], seq_passed.at[step], seq_pair)

    own_piece = remote(weights, piece(seq), seq_pass.at[0], seq_passed.at[0], seq_pair)

    def each(call):
        def body(step, carry):
            call(step)
            return carry

        lax.fori_loop(1, seq_groups, body, 0)

    def store(array):
        _, whole, out, lines = parts[array]
        return pltpu.make_async_copy(whole.at[lines], out.at[lines], store_sem.at[array])

    for array in range(4):
        for step in range(1, chan_groups):
            chan_copy(array, step).start()
    each(lambda step: seq_copy(step).start())
    own_piece.start()
    for array in range(4):
        chan_forward(array, 0).start()
    keeps = [pltpu.make_async_copy(weights, piece(seq), keep_sem.at[4])]
    for array, (own, whole, _, lines) in enumerate(parts):
        keeps.append(
            pltpu.make_async_copy(own.at[lines], block(whole, lines, chan), keep_sem.at[array])
        )
    for keep in keeps:
        keep.start()

    def pass_on(step):
        seq_copy(step).wait_recv()
        seq_forward(step).start()

    def pass_part(array):
        for step in range(1, chan_groups):
            chan_copy(array, step).wait_recv()
            chan_forward(array, step).start()

    pass_part(0)
    each(pass_on)
    for keep in keeps:
        keep.wait()
    own_piece.wait()

    def finish(step):
        seq_copy(step).wait_send()
        seq_forward(step).wait()

    each(finish)
    tile = math.gcd(height, 128)
    for array, (_, whole, _, lines) in enumerate(parts):
        if array + 1 < len(parts):
            pass_part(array + 1)
        for step in range(chan_groups):
            chan_forward(array, step).wait()
        store(array).start()
        target, first = (projected, 0) if array < 2 else (upstream, all_weights.shape[1] // 2)

        def product(index, carry):
            here = pl.ds(pl.multiple_of(array % 2 * height + index * tile, tile), tile)
            target[here] = jnp.dot(
                whole[here], all_weights[:, first:], preferred_element_type=jnp.float32
            )
            return carry

        lax.fori_loop(0, height // tile, product, 0)
    for array in range(4):
        store(array).wait()
        for step in range(1, chan_groups):
            chan_copy(array, step).wait_send()


def gathered(tokens, grads, weights):
    devices_seq, devices_chan = lax.axis_size("seq"), lax.axis_size("chan")
    dma = pltpu.SemaphoreType.DMA
    seq_groups, chan_groups = devices_seq // 2, devices_chan // 2
    vmem, anywhere = pl.BlockSpec(memory_space=pltpu.VMEM), pl.BlockSpec(memory_space=pl.ANY)
    wide = jax.ShapeDtypeStruct((tokens.shape[0], tokens.shape[1] * devices_chan), tokens.dtype)
    tall = jax.ShapeDtypeStruct((weights.shape[0] * devices_seq, weights.shape[1]), weights.dtype)
    return pl.pallas_call(
        functools.partial(gather_kernel, devices_seq, devices_chan),
        out_shape=(
            wide,
            wide,
            jax.ShapeDtypeStruct((tokens.shape[0], weights.shape[1]), jnp.float32),
            jax.ShapeDtypeStruct((tokens.shape[0], weights.shape[1] // 2), jnp.float32),
        ),
        in_specs=[vmem] * 3,
        out_specs=(anywhere, anywhere, vmem, vmem),
        scratch_shapes=[
            pltpu.VMEM(wide.shape, wide.dtype),
            pltpu.VMEM(wide.shape, wide.dtype),
            pltpu.VMEM(tall.shape, tall.dtype),
            dma((5,)),
            dma((4,)),
        ]
        + [dma((4, chan_groups))] * 4
        + [dma((seq_groups,))] * 4,
        compiler_params=pltpu.CompilerParams(collective_id=0, has_side_effects=True),
        name="gather_inputs",
    )(tokens, grads, weights)


def reduce_kernel(
    devices_seq,
    tile,
    state,
    rate,
    weight,
    inner,
    value,
    gate,
    early_in,
    early_out,
    tokens_hbm,
    grads_hbm,
    total,
    tokens,
    grads,
    states,
    late,
    parts,
    near,
    paired,
    far,
    load_sem,
    state_send,
    state_recv,
    pair_send,
    pair_recv,
    far_send,
    far_recv,
):
    seq, chan = lax.axis_index("seq"), lax.axis_index("chan")
    groups = devices_seq // 2
    group, parity = seq // 2, seq % 2
    rows, channels = inner.shape
    owned = near.shape[2]
    loads = [
        pltpu.make_async_copy(tokens_hbm, tokens, load_sem.at[0]),
        pltpu.make_async_copy(grads_hbm, grads, load_sem.at[1]),
    ]
    for load in loads:
        load.start()
    greet(devices_seq, 0, "all")

    def loop(start, stop, call):
        def body(step, carry):
            call(step)
            return carry

        lax.fori_loop(start, stop, body, 0)

    def state_copy(step):
        there = lax.rem(seq + step, devices_seq)
        return remote(
            state, states.at[step], state_send.at[step], state_recv.at[step], (there, chan)
        )

    def member(step):
        return lax.rem(group + step, groups)

    def piece(half, index):
        return parts.at[half, pl.ds(pl.multiple_of(index * owned, owned), owned)]

    def pair_copy(half, step):
        return remote(
            piece(half, member(step) * 2 + 1 - parity),
            near.at[half, step],
            pair_send.at[half, step],
            pair_recv.at[half, step],
            (group * 2 + 1 - parity, chan),
        )

    def far_copy(half, step):
        return remote(
            paired.at[half, step],
            far.at[half, step],
            far_send.at[half, step],
            far_recv.at[half, step],
            (member(step) * 2 + parity, chan),
        )

    def summed(left, right):
        return lax.dot_general(
            left, right, (((0,), (0,)), ((), ())), preferred_element_type=jnp.float32
        )

    def span(index):
        return pl.ds(pl.multiple_of(index * tile, tile), tile)

    loop(1, devices_seq, lambda step: state_copy(step).start())
    for load in loads:
        load.wait()

    def early_tile(index):
        product = summed(tokens[:, span(index)], early_in[...])
        product += summed(grads[:, span(index)], early_out[...])
        parts[0, span(index)] = product.astype(parts.dtype)

    loop(0, tokens.shape[1] // tile, early_tile)
    loop(1, groups, lambda step: pair_copy(0, step).start())
    pair_copy(0, 0).start()

    def absorb(step, following):
        state_copy(step).wait_recv()
        gap = lax.rem(seq - step + devices_seq, devices_seq) - seq - 1
        reach = (jnp.maximum(gap, 0) * rows).astype(jnp.float32)
        present = (gap >= 0).astype(jnp.float32)
        return following + present * states[step] * jnp.exp(-reach * rate[...])

    following = lax.fori_loop(1, devices_seq, absorb, jnp.zeros(rate.shape, jnp.float32))
    entering = weight[...] * following
    rates = rate[...]
    band = math.gcd(rows, 64)

    def source_rows(index):
        here = pl.ds(pl.multiple_of(index * band, band), band)
        position = lax.broadcasted_iota(jnp.int32, (band, channels), 0) + index * band
        reach = (rows - position).astype(jnp.float32)
        source = inner[here]
        for mode in range(rates.shape[0]):
            source += entering[mode : mode + 1] * jnp.exp(-reach * rates[mode : mode + 1])
        late[here] = jnp.concatenate([source * value[here], source * gate[here]], axis=1).astype(
            late.dtype
        )

    loop(0, rows // band, source_rows)

    def late_tile(index):
        parts[1, span(index)] = summed(tokens[:, span(index)], late[...]).astype(parts.dtype)

    loop(0, tokens.shape[1] // tile, late_tile)
    loop(1, groups, lambda step: pair_copy(1, step).start())
    pair_copy(1, 0).start()

    def pair_sum(half, step):
        own = piece(half, member(step) * 2 + parity)[...].astype(jnp.float32)
        return own + near[half, step].astype(jnp.float32)

    for half in range(2):

        def pass_on(step):
            pair_copy(half, step).wait_recv()
            paired[half, step] = pair_sum(half, step).astype(paired.dtype)
            far_copy(half, step).start()

        loop(1, groups, pass_on)
    for half in range(2):
        pair_copy(half, 0).wait_recv()
        total[half] = pair_sum(half, 0)

        def collect(step):
            far_copy(half, step).wait_recv()
            total[half] += far[half, step].astype(jnp.float32)

        loop(1, groups, collect)

        def finish(step):
            pair_copy(half, step).wait_send()
            far_copy(half, step).wait_send()

        loop(1, groups, finish)
        pair_copy(half, 0).wait_send()
    loop(1, devices_seq, lambda step: state_copy(step).wait_send())


def reduced(state, rate, weight, inner, value, gate, early_in, early_out, tokens, grads, owned):
    devices_seq = lax.axis_size("seq")
    groups = devices_seq // 2
    rows, channels = inner.shape
    width = tokens.shape[1]
    wide = 2 * channels
    vmem, anywhere = pl.BlockSpec(memory_space=pltpu.VMEM), pl.BlockSpec(memory_space=pl.ANY)
    dma, half_type = pltpu.SemaphoreType.DMA, tokens.dtype
    return pl.pallas_call(
        functools.partial(reduce_kernel, devices_seq, math.gcd(width, 512)),
        out_shape=jax.ShapeDtypeStruct((2, owned, wide), jnp.float32),
        in_specs=[vmem] * 8 + [anywhere] * 2,
        out_specs=vmem,
        scratch_shapes=[pltpu.VMEM(tokens.shape, half_type)] * 2
        + [pltpu.VMEM((devices_seq,) + state.shape, jnp.float32)]
        + [pltpu.VMEM((rows, wide), half_type), pltpu.VMEM((2, width, wide), half_type)]
        + [pltpu.VMEM((2, groups, owned, wide), half_type)] * 3
        + [dma((2,)), dma((devices_seq,)), dma((devices_seq,))]
        + [dma((2, groups))] * 4,
        compiler_params=pltpu.CompilerParams(collective_id=1, has_side_effects=True),
        name="reduce_owned",
    )(state, rate, weight, inner, value, gate, early_in, early_out, tokens, grads)


def correlate_block(signal, residues, decay_length):
    rows, channels = signal.shape
    chunk = min(64, rows)
    chunks = rows // chunk
    per_filter = channels // residues.shape[1]
    rate = jnp.repeat(1.0 / decay_length, per_filter, axis=1)
    weight = jnp.repeat(residues, per_filter, axis=1) * jnp.sqrt(-jnp.expm1(-2.0 * rate))
    offset = jnp.arange(chunk, dtype=jnp.float32)
    exponent = rate.T[:, :, None] * offset
    grow = weight.T[:, :, None] * jnp.exp(exponent)
    fall = jnp.exp(-exponent)
    later = jnp.arange(chunk)[None, :] >= jnp.arange(chunk)[:, None]
    taps = jnp.einsum("cri,crj->cij", grow, fall, precision=precise)
    taps = jnp.where(later, taps, 0.0)
    pieces = signal.reshape(chunks, chunk, channels).transpose(2, 1, 0)
    both = jnp.einsum(
        "cij,cjn->cin", jnp.concatenate([taps, fall], axis=1), pieces, precision=precise
    )
    inner, sums = both[:, :chunk], both[:, chunk:]
    step = jnp.exp(-chunk * rate).T
    state = jnp.zeros_like(step)
    entering = []
    for index in reversed(range(chunks)):
        entering.append(step * state)
        state = sums[:, :, index] + step * state
    entering = jnp.stack(entering[::-1], axis=2)
    outer = jnp.einsum("cri,crn->cin", grow, entering, precision=precise)
    return (inner + outer).transpose(2, 1, 0).reshape(rows, channels), state.T, rate, weight


def block_kernel(
    devices_seq,
    devices_chan,
    tokens_hbm,
    grads_hbm,
    in_weight,
    out_weight,
    conv_hbm,
    residues,
    decay_length,
    grad_in,
    grad_out,
    tokens,
    grads,
    conv,
    pieces,
    crossed,
    weights,
    partial,
    pair_in,
    chip_sum,
    far_in,
    signal,
    consts,
    bank,
    own_state,
    states,
    flows,
    parts,
    kept,
    near,
    summed,
    blocks,
    arrived,
    results,
    given,
    load_sem,
    sent,
    hop_recv,
    swap_recv,
    keep_sem,
    twin_recv,
    pair_recv,
    far_recv,
    state_recv,
    flow_recv,
    pass_recv,
    near_recv,
    turn_recv,
    home_recv,
    put_sem,
):
    seq, chan = lax.axis_index("seq"), lax.axis_index("chan")
    planes = devices_chan
    twins = devices_seq // planes
    groups = devices_chan // 2
    plane, twin = seq // twins, seq % twins
    group, parity = chan // 2, chan % 2
    partner = (seq, chan + 1 - 2 * parity)
    channels, rows = conv.shape
    owned = out_weight.shape[1]

    def ahead(index, step, count):
        return lax.rem(index + step, count)

    def behind(index, step, count):
        return lax.rem(index - step + count, count)

    sources = (in_weight.at[1], out_weight, in_weight.at[0], in_weight.at[2])
    count = len(sources)
    weight_loads = [
        pltpu.make_async_copy(sources[part], pieces.at[part, plane], load_sem.at[part])
        for part in range(count)
    ]
    bulk_loads = [
        pltpu.make_async_copy(tokens_hbm, tokens, load_sem.at[count]),
        pltpu.make_async_copy(grads_hbm, grads, load_sem.at[count + 1]),
        pltpu.make_async_copy(conv_hbm, conv, load_sem.at[count + 2]),
    ]
    filter_loads = [
        pltpu.make_async_copy(residues, given.at[0], load_sem.at[count + 3]),
        pltpu.make_async_copy(decay_length, given.at[1], load_sem.at[count + 4]),
    ]
    for load in weight_loads + filter_loads + bulk_loads:
        load.start()

    barrier = pltpu.get_barrier_semaphore()
    for step in range(1, devices_seq):
        pl.semaphore_signal(
            barrier, inc=1, device_id=(ahead(seq, step, devices_seq), chan), device_id_type=MESH
        )
    for step in range(1, devices_chan):
        pl.semaphore_signal(
            barrier, inc=1, device_id=(seq, ahead(chan, step, devices_chan)), device_id_type=MESH
        )
    pl.semaphore_wait(barrier, devices_seq + devices_chan - 2)

    bits = [1 << power for power in reversed(range(planes.bit_length() - 1))]

    def flip(index, mask):
        result = index
        for bit in bits:
            if mask & bit:
                result = result + bit - 2 * bit * (index // bit % 2)
        return result

    def hop(part, which, kind, side):
        return remote(
            pieces.at[part, which],
            pieces.at[part, which],
            sent.at[kind],
            hop_recv.at[part, which],
            ((plane + side) * twins + twin, chan),
        )

    def onward(part, which, kind, side):
        edge = planes - 1 if side > 0 else 0

        @pl.when(plane != edge)
        def _():
            hop(part, which, kind, side).start()

    def cross(part, step, mask):
        here = flip(plane, mask)
        return remote(
            pieces.at[part, here],
            crossed.at[part, step, here],
            sent.at[14 + part // early],
            twin_recv.at[part, step - 1, mask],
            (plane * twins + ahead(twin, step, twins), chan),
        )

    def held(part, step, target):
        return crossed.at[part, step, target] if step else pieces.at[part, target]

    def swap(part, step, target):
        return remote(
            held(part, step, target),
            weights.at[part, behind(twin, step, twins), chan],
            sent.at[2 + part // early if step else 1],
            swap_recv.at[part, step],
            (seq, target),
        )

    def swap_in(part, step):
        landed = weights.at[part, behind(twin, step, twins), pl.ds(0, devices_chan - 1)]
        return remote(landed, landed, sent.at[2 + part // early if step else 1], swap_recv.at[part, step], partner)

    def keep(part, step):
        return pltpu.make_async_copy(
            held(part, step, chan),
            weights.at[part, behind(twin, step, twins), chan],
            keep_sem.at[part, step],
        )

    def deliver(part, step, mask):
        target = flip(plane, mask)

        @pl.when(target == chan)
        def _():
            keep(part, step).start()

        @pl.when(target != chan)
        def _():
            swap(part, step, target).start()

    early = count // 2

    crossing = ((0, 1, 3), (3,))

    def crosses(part, mask):
        return mask in crossing[part // early]

    def here(part, mask):
        if crosses(part, mask):
            for step in range(1, twins):
                cross(part, step, mask).start()
        deliver(part, 0, mask)

    def depart(group):
        for part in group:
            for side in (1, -1):
                onward(part, plane, 0, side)

    def arrive(group, distance):
        for part in group:
            for mask in range(1, planes):
                which = flip(plane, mask)
                for side in (1, -1):

                    @pl.when(plane - which == side * distance)
                    def _(mask=mask, which=which, side=side, part=part):
                        hop(part, which, 0, side).wait_recv()
                        onward(part, which, 16, side)
                        here(part, mask)

    def cross_on(part, mask):
        for step in range(1, twins):
            cross(part, step, mask).wait_recv()
            deliver(part, step, mask)

    def twin_copy(part, step):
        return remote(
            weights.at[part, twin],
            weights.at[part, twin],
            sent.at[4 + part // early],
            twin_recv.at[part, step - 1, 2],
            (plane * twins + ahead(twin, step, twins), chan),
        )

    def twin_in(part, step):
        there = behind(twin, step, twins)
        return remote(
            weights.at[part, there],
            weights.at[part, there],
            sent.at[4 + part // early],
            twin_recv.at[part, step - 1, 2],
            (plane * twins + there, chan),
        )

    def share(part, mask):
        @pl.when(flip(plane, mask) == chan)
        def _():
            swap_in(part, 0).wait_recv()
            keep(part, 0).wait()
            for step in range(1, twins):
                twin_copy(part, step).start()

    def loaded(part):
        weight_loads[part].wait()

    first, last = range(early), range(early, count)
    for part in range(count):
        loaded(part)
    depart(first)
    for part in first:
        here(part, 0)

    lanes = signal.shape[1]
    folds = lanes // channels
    groups_of_rows = 8
    span = signal.shape[0] // groups_of_rows
    modes, filters = residues.shape
    per_filter = channels // filters
    lane = lax.broadcasted_iota(jnp.int32, (filters, lanes), 1)
    which = lax.broadcasted_iota(jnp.int32, (filters, lanes), 0)
    spread = (lax.rem(lane, channels) // per_filter == which).astype(jnp.float32)
    for load in filter_loads:
        load.wait()
    inverse = 1.0 / given[1]
    twice = 2.0 * inverse
    series = jnp.zeros_like(twice)
    for order in range(10, 0, -1):
        series = (1.0 - series) * twice / order
    loss = jnp.where(twice < 0.5, series, 1.0 - jnp.exp(-twice))
    scale = given[0] * jnp.sqrt(loss)

    def widen(array):
        return jnp.dot(array, spread, precision=precise, preferred_element_type=jnp.float32)

    rate = widen(inverse)
    consts[0] = rate
    consts[1] = widen(scale)
    consts[2] = jnp.exp(-rate)

    inputs = (tokens, grads, tokens, tokens)

    def ready(part, step, mask):
        @pl.when(flip(plane, mask) == chan)
        def _():
            if crosses(part, mask):
                swap_in(part, step).wait_recv()
                keep(part, step).wait()
            elif step:
                twin_in(part, step).wait_recv()

    def project(part):
        for step in range(twins):
            block = behind(twin, step, twins)
            for mask in range(planes):
                ready(part, step, mask)
            columns = pl.ds(pl.multiple_of(block * owned, owned), owned)
            product = lax.dot_general(
                weights[part, block].reshape(devices_chan * channels, owned),
                inputs[part][:, columns],
                (((1,), (1,)), ((), ())),
                preferred_element_type=jnp.float32,
            )
            for target in range(devices_chan):
                piece = product[target * channels : (target + 1) * channels]
                place = (part, target % 2, target // 2)
                if step:
                    piece = partial[place] + piece
                partial[place] = piece

    def pair_copy(part, there):
        return remote(
            partial.at[part, 1 - parity, there],
            pair_in.at[part, there],
            sent.at[6],
            pair_recv.at[part, there],
            partner,
        )

    def far_copy(part, step):
        return remote(
            chip_sum.at[part, step],
            far_in.at[part, step],
            sent.at[7],
            far_recv.at[part, step - 1],
            (seq, ahead(group, step, groups) * 2 + parity),
        )

    def pair_start(part):
        for step in range(1, groups + 1):
            pair_copy(part, ahead(group, step, groups)).start()

    def far_start(part):
        for step in range(1, groups):
            there = ahead(group, step, groups)
            pair_copy(part, there).wait_recv()
            chip_sum[part, step] = partial[part, parity, there] + pair_in[part, there]
            far_copy(part, step).start()

    def far_finish(part):
        pair_copy(part, group).wait_recv()
        total = partial[part, parity, group] + pair_in[part, group]
        for step in range(1, groups):
            far_copy(part, step).wait_recv()
            total = total + far_in[part, step]
        return total

    def flow(part, step):
        return remote(
            flows.at[part, chan],
            flows.at[part, chan],
            sent.at[8],
            flow_recv.at[part, step - 1],
            (seq, ahead(group, step, groups) * 2 + parity),
        )

    def flow_in(part, step):
        source = behind(group, step, groups) * 2 + parity
        return remote(
            flows.at[part, source],
            flows.at[part, source],
            sent.at[8],
            flow_recv.at[part, step - 1],
            (seq, source),
        )

    def flow_pass(part, step):
        source = behind(group, step, groups) * 2 + parity
        return remote(
            flows.at[part, source],
            flows.at[part, source],
            sent.at[9],
            pass_recv.at[part, step],
            partner,
        )

    def flow_passed(part, step):
        source = behind(group, step, groups) * 2 + 1 - parity
        return remote(
            flows.at[part, source],
            flows.at[part, source],
            sent.at[9],
            pass_recv.at[part, step],
            partner,
        )

    def flow_start(part):
        for step in range(1, groups):
            flow(part, step).start()
        flow_pass(part, 0).start()

    def flow_on(part):
        for step in range(1, groups):
            flow_in(part, step).wait_recv()
            flow_pass(part, step).start()

    def flow_finish(part):
        for step in range(groups):
            flow_passed(part, step).wait_recv()

    def near_copy(part, step, target):
        return remote(
            parts.at[part, step - 1, target],
            near.at[part, step - 1, target],
            sent.at[10],
            near_recv.at[part, step - 1, target],
            (plane * twins + ahead(twin, step, twins), chan),
        )

    def multiply(part):
        for step in range(1, twins + 1):
            block = ahead(twin, step, twins)
            columns = pl.ds(pl.multiple_of(block * owned, owned), owned)
            product = jnp.dot(
                flows[part].reshape(devices_chan * channels, rows),
                inputs[part][:, columns],
                preferred_element_type=jnp.float32,
            )
            for target in range(devices_chan):
                piece = product[target * channels : (target + 1) * channels]
                if step < twins:
                    parts[part, step - 1, target] = piece.astype(parts.dtype)
                else:
                    kept[part, target] = piece
            if step < twins:
                for index in range(1, devices_chan + 1):
                    near_copy(part, step, ahead(chan, index, devices_chan)).start()

    def turn(part, target):
        return remote(
            summed.at[part, target],
            blocks.at[part, chan],
            sent.at[11],
            turn_recv.at[part, chan],
            (seq, target),
        )

    def turn_in(part, source):
        return remote(
            summed.at[part, source],
            blocks.at[part, source],
            sent.at[11],
            turn_recv.at[part, source],
            (seq, source),
        )

    straight = (0, 1, 2, 3)

    def home(part, mask):
        return remote(
            blocks.at[part, flip(plane, mask)],
            arrived.at[part, mask],
            sent.at[12],
            home_recv.at[part, mask - 1],
            (flip(plane, mask if part in straight else mask & -mask) * twins + twin, chan),
        )

    def turn_start(part, index):
        target = ahead(chan, index, devices_chan)
        total = kept[part, target]
        for step in range(1, twins):
            near_copy(part, step, target).wait_recv()
            total = total + near[part, step - 1, target].astype(jnp.float32)
        total = total.astype(blocks.dtype)
        if index < devices_chan:
            summed[part, target] = total
            turn(part, target).start()
        else:
            blocks[part, chan] = total

    def turned(part, index):
        source = behind(chan, index, devices_chan)
        if index < devices_chan:
            turn_in(part, source).wait_recv()

        for mask in range(1, planes, 1 if part in straight else 2):

            @pl.when(flip(plane, mask) == source)
            def _(mask=mask):
                home(part, mask).start()

    def gathered(part, mask):
        total = blocks[part, flip(plane, mask)].astype(jnp.float32)
        for other in range(1, planes) if part in straight else reversed(bits):
            if mask == 0 or other < mask & -mask:
                home(part, mask ^ other).wait_recv()
                total = total + arrived[part, mask ^ other].astype(jnp.float32)
        return total

    targets = (grad_in.at[1], grad_out, grad_in.at[0], grad_in.at[2])

    def put(part):
        return pltpu.make_async_copy(results.at[part], targets[part], put_sem.at[part])

    def finish(part):
        results[part] = gathered(part, 0)
        put(part).start()

    def home_on(part):
        for mask in range(planes - 1, 0, -1):
            if mask & -mask > 1 and part not in straight:
                blocks[part, flip(plane, mask)] = gathered(part, mask).astype(blocks.dtype)
                home(part, mask).start()

    def rowed(array):
        width = array.shape[1] // folds
        stacked = jnp.concatenate(
            [array[:, fold * width : (fold + 1) * width] for fold in range(folds)], axis=0
        )
        return stacked.T

    def unrowed(array):
        stacked = array.T
        return jnp.concatenate(
            [stacked[fold * channels : (fold + 1) * channels] for fold in range(folds)], axis=1
        )

    def mode_row(kind, mode):
        return jnp.broadcast_to(consts[kind, mode : mode + 1], (groups_of_rows, lanes))

    def line(index):
        return pl.ds(index, groups_of_rows, stride=span)

    def scan_states():
        fall = [mode_row(2, mode) for mode in range(modes)]

        def body(step, carry):
            here = signal[line(span - 1 - step)]
            return tuple(carry[mode] * fall[mode] + here for mode in range(modes))

        zero = jnp.zeros((groups_of_rows, lanes), jnp.float32)
        found = lax.fori_loop(0, span, body, (zero,) * modes)
        position = lax.broadcasted_iota(jnp.int32, (groups_of_rows, lanes), 0)
        for mode in range(modes):
            each = mode_row(0, mode) * span
            total = found[mode]
            shift = 1
            while shift < groups_of_rows:
                moved = pltpu.roll(total, groups_of_rows - shift, 0)
                moved = moved * jnp.exp(-each * shift)
                total = total + jnp.where(position < groups_of_rows - shift, moved, 0.0)
                shift *= 2
            moved = pltpu.roll(total, groups_of_rows - 1, 0)
            bank[mode] = jnp.where(position < groups_of_rows - 1, moved, 0.0)
            own_state[mode : mode + 1] = total[0:1]
        heads = own_state[...]
        reach = consts[0] * (span * groups_of_rows)
        later = pltpu.roll(heads, channels, 1)
        first = lax.broadcasted_iota(jnp.int32, (modes, lanes), 1) < channels
        consts[3] = jnp.where(first, later, 0.0)
        own_state[...] = jnp.where(first, heads + later * jnp.exp(-reach), 0.0)

    def state_copy(step):
        return remote(
            own_state,
            states.at[step],
            sent.at[13],
            state_recv,
            (ahead(seq, step, devices_seq), chan),
        )

    def scan_source():
        rates = consts[0]
        following = jnp.zeros((modes, lanes), jnp.float32)
        landed = states.at[pl.ds(1, devices_seq - 1)]
        remote(landed, landed, sent.at[13], state_recv, partner).wait_recv()
        for step in range(1, devices_seq):
            gap = behind(seq, step, devices_seq) - seq - 1
            reach = (jnp.maximum(gap, 0) * rows).astype(jnp.float32)
            present = (gap >= 0).astype(jnp.float32)
            following = following + present * states[step] * jnp.exp(-reach * rates)
        first = lax.broadcasted_iota(jnp.int32, (modes, lanes), 1) < channels
        after = pltpu.roll(following, channels, 1)
        within = following * jnp.exp(-(rates * (span * groups_of_rows)))
        consts[3] = jnp.where(first, consts[3] + within, after)
        fall = [mode_row(2, mode) for mode in range(modes)]
        weigh = [mode_row(1, mode) for mode in range(modes)]
        position = lax.broadcasted_iota(jnp.int32, (groups_of_rows, lanes), 0)
        left = ((groups_of_rows - 1 - position) * span).astype(jnp.float32)
        start = tuple(
            bank[mode] + mode_row(3, mode) * jnp.exp(-left * mode_row(0, mode))
            for mode in range(modes)
        )

        def body(step, carry):
            here = line(span - 1 - step)
            entry = signal[here]
            following = tuple(carry[mode] * fall[mode] + entry for mode in range(modes))
            terms = [following[mode] * weigh[mode] for mode in range(modes)]
            while len(terms) > 1:
                terms = [sum(terms[at : at + 2]) for at in range(0, len(terms), 2)]
            signal[here] = terms[0]
            return following

        lax.fori_loop(0, span, body, start)

    def settle(group, mask):
        for part in group:
            if crosses(part, mask):
                cross_on(part, mask)
            else:
                share(part, mask)

    arrive(first, 1)
    settle(first, 0)
    arrive(first, 2)
    depart(last)
    for part in last:
        here(part, 0)
    settle(first, 1)
    arrive(first, 3)
    settle(first, 2)
    arrive(last, 1)
    settle(last, 0)
    settle(first, 3)
    arrive(last, 2)
    settle(last, 1)
    for load in bulk_loads:
        load.wait()
    project(0)
    pair_start(0)
    project(1)
    pair_start(1)
    arrive(last, 3)
    settle(last, 2)
    far_start(0)
    far_start(1)
    taken = conv[...].astype(jnp.float32)
    second = far_finish(0).astype(flows.dtype).astype(jnp.float32)
    flows[1, chan] = (second * taken).astype(flows.dtype)
    flow_start(1)
    settle(last, 3)
    upstream = far_finish(1)
    flows[0, chan] = (upstream * taken).astype(flows.dtype)
    flow_start(0)
    signal[...] = rowed(upstream * second)
    flow_on(1)
    scan_states()
    for step in range(1, devices_seq):
        state_copy(step).start()
    project(2)
    pair_start(2)
    flow_finish(1)
    multiply(1)
    project(3)
    pair_start(3)
    far_start(2)
    far_start(3)
    flow_on(0)
    flow_finish(0)
    multiply(0)
    turn_start(1, 1)
    scan_source()
    source = unrowed(signal[...])
    turn_start(1, 2)
    late = far_finish(2).astype(flows.dtype).astype(jnp.float32)
    flows[3, chan] = (source * late).astype(flows.dtype)
    flow_start(3)
    late = far_finish(3).astype(flows.dtype).astype(jnp.float32)
    flows[2, chan] = (source * late).astype(flows.dtype)
    flow_start(2)
    turn_start(1, 3)
    turned(1, 1)
    turn_start(1, 4)
    turned(1, 2)
    flow_on(3)
    turn_start(0, 1)
    turned(1, 3)
    flow_on(2)
    turn_start(0, 2)
    flow_finish(3)
    multiply(3)
    flow_finish(2)
    multiply(2)
    turned(1, 4)
    turn_start(0, 3)
    turned(0, 1)
    turn_start(0, 4)
    turned(0, 2)
    turned(0, 3)
    turned(0, 4)
    turn_start(3, 1)
    turn_start(3, 2)
    turn_start(3, 3)
    turned(3, 1)
    turn_start(3, 4)
    turned(3, 2)
    turn_start(2, 1)
    turned(3, 3)
    turn_start(2, 2)
    turned(3, 4)
    turn_start(2, 3)
    turned(2, 1)
    turn_start(2, 4)
    turned(2, 2)
    turned(2, 3)
    turned(2, 4)
    finish(1)
    finish(0)
    finish(3)
    finish(2)
    for part in range(count):
        put(part).wait()

    def left(kind, ref):
        remote(ref, ref, sent.at[kind], state_recv, partner).wait_send()

    fewer = pl.ds(0, planes - 1)
    others = pl.ds(1, twins - 1)
    inner = jnp.logical_and(plane > 0, plane < planes - 1)

    @pl.when(inner)
    def _():
        left(0, pieces.at[:, pl.ds(0, 2)])
        left(16, pieces.at[:, fewer])

    @pl.when(jnp.logical_not(inner))
    def _():
        left(0, pieces.at[:, pl.ds(0, 1)])

    left(1, pieces.at[:, fewer])
    for group in range(2):
        span_of = pl.ds(group * early, early)
        masks = crossing[group]
        if masks:
            left(14 + group, crossed.at[span_of, others, pl.ds(0, len(masks))])
        for mask in range(planes):

            @pl.when(flip(plane, mask) == chan)
            def _(mask=mask):
                swaps = len(masks) - (mask in masks)
                if swaps:
                    left(2 + group, crossed.at[span_of, others, pl.ds(0, swaps)])
                if mask not in masks:
                    left(4 + group, weights.at[span_of, others])

    left(6, partial.at[:, 0])
    left(7, chip_sum.at[:, pl.ds(1, groups - 1)])
    left(8, flows.at[:, pl.ds(0, groups - 1)])
    left(9, flows.at[:, pl.ds(0, groups)])
    left(10, parts)
    left(11, summed.at[:, fewer])
    left(12, blocks.at[:, fewer])
    left(13, states.at[pl.ds(1, devices_seq - 1)])


def place_kernel(grad_in, grad_proj, out_in, out_proj, held, take_sem, give_sem):
    streams = grad_in.shape[0]
    ends = [(grad_in.at[at], out_in.at[at]) for at in range(streams)] + [(grad_proj, out_proj)]
    takes = [
        pltpu.make_async_copy(source, held.at[at], take_sem.at[at])
        for at, (source, _) in enumerate(ends)
    ]
    gives = [
        pltpu.make_async_copy(held.at[at], target, give_sem.at[at])
        for at, (_, target) in enumerate(ends)
    ]
    for take in takes:
        take.start()
    for take, give in zip(takes, gives):
        take.wait()
        give.start()
    for give in gives:
        give.wait()


def placed(grad_in, grad_proj):
    anywhere, dma = pl.BlockSpec(memory_space=pl.ANY), pltpu.SemaphoreType.DMA
    count = grad_in.shape[0] + 1
    return pl.pallas_call(
        place_kernel,
        out_shape=tuple(jax.ShapeDtypeStruct(a.shape, a.dtype) for a in (grad_in, grad_proj)),
        in_specs=[anywhere] * 2,
        out_specs=(anywhere, anywhere),
        scratch_shapes=[
            pltpu.VMEM((count,) + grad_proj.shape, grad_proj.dtype),
            dma((count,)),
            dma((count,)),
        ],
        name="place_outputs",
    )(grad_in, grad_proj)


def fits(tokens, conv_out, in_weight, residues):
    devices_seq, devices_chan = lax.axis_size("seq"), lax.axis_size("chan")
    rows, channels = conv_out.shape
    return (
        devices_chan == 4
        and devices_seq % devices_chan == 0
        and devices_seq > devices_chan
        and in_weight.shape[0] % 128 == 0
        and 2 * channels == 128
        and channels % residues.shape[1] == 0
        and rows % 256 == 0
        and tokens.shape[1] * devices_chan == in_weight.shape[0] * devices_seq
    )


def blocked(tokens, grad_out, in_weight, out_weight, conv_out, residues, decay_length):
    devices_seq, devices_chan = lax.axis_size("seq"), lax.axis_size("chan")
    planes, groups = devices_chan, devices_chan // 2
    twins = devices_seq // planes
    rows, width = tokens.shape
    channels, owned = out_weight.shape[1], out_weight.shape[0]
    modes = residues.shape[0]
    anywhere = pl.BlockSpec(memory_space=pl.ANY)
    dma, half_type, full = pltpu.SemaphoreType.DMA, tokens.dtype, jnp.float32
    lanes = 2 * channels
    grad_in, grad_proj = pl.pallas_call(
        functools.partial(block_kernel, devices_seq, devices_chan),
        out_shape=(
            jax.ShapeDtypeStruct((3, channels, owned), full),
            jax.ShapeDtypeStruct((channels, owned), full),
        ),
        in_specs=[anywhere] * 7,
        out_specs=(anywhere, anywhere),
        scratch_shapes=[
            pltpu.VMEM((rows, width), half_type),
            pltpu.VMEM((rows, width), half_type),
            pltpu.VMEM((channels, rows), half_type),
            pltpu.VMEM((4, planes, channels, owned), half_type),
            pltpu.VMEM((4, twins, planes, channels, owned), half_type),
            pltpu.VMEM((4, twins, devices_chan, channels, owned), half_type),
            pltpu.VMEM((4, 2, groups, channels, rows), full),
            pltpu.VMEM((4, groups, channels, rows), full),
            pltpu.VMEM((4, groups, channels, rows), full),
            pltpu.VMEM((4, groups, channels, rows), full),
            pltpu.VMEM((rows * channels // lanes, lanes), full),
            pltpu.VMEM((4, modes, lanes), full),
            pltpu.VMEM((modes, 8, lanes), full),
            pltpu.VMEM((modes, lanes), full),
            pltpu.VMEM((devices_seq, modes, lanes), full),
            pltpu.VMEM((4, devices_chan, channels, rows), half_type),
            pltpu.VMEM((4, twins - 1, devices_chan, channels, owned), half_type),
            pltpu.VMEM((4, devices_chan, channels, owned), full),
            pltpu.VMEM((4, twins - 1, devices_chan, channels, owned), half_type),
            pltpu.VMEM((4, devices_chan, channels, owned), half_type),
            pltpu.VMEM((4, planes, channels, owned), half_type),
            pltpu.VMEM((4, planes, channels, owned), half_type),
            pltpu.VMEM((4, channels, owned), full),
            pltpu.VMEM((2,) + residues.shape, full),
            dma((9,)),
            dma((17,)),
            dma((4, planes)),
            dma((4, twins)),
            dma((4, twins)),
            dma((4, twins - 1, planes)),
        ]
        + [dma((4, groups)), dma((4, groups - 1)), dma, dma((4, groups - 1)), dma((4, groups))]
        + [dma((4, twins - 1, planes))]
        + [dma((4, planes)), dma((4, planes - 1)), dma((4,))],
        compiler_params=pltpu.CompilerParams(collective_id=2, has_side_effects=True),
        name="conv_block",
    )(
        tokens,
        grad_out,
        in_weight.transpose(1, 2, 0),
        out_weight.T,
        conv_out.T,
        residues,
        decay_length,
    )
    grad_in, grad_proj = placed(grad_in, grad_proj)
    return grad_in.transpose(2, 0, 1), grad_proj.T


def local(tokens, grad_out, in_weight, out_weight, conv_out, residues, decay_length):
    if fits(tokens, conv_out, in_weight, residues):
        return blocked(tokens, grad_out, in_weight, out_weight, conv_out, residues, decay_length)
    channels = out_weight.shape[1]
    owned_rows = in_weight.shape[0]
    weights = jnp.concatenate([in_weight.reshape(owned_rows, 3 * channels), out_weight], axis=1)
    full_tokens, full_grads, projected, upstream = gathered(tokens, grad_out, weights)
    projected = projected[:, : 3 * channels]
    upstream = upstream[:, channels:]
    streams = lax.reduce_precision(projected, exponent_bits=8, mantissa_bits=7)
    gate_first = streams[:, :channels]
    gate_second = streams[:, channels : 2 * channels]
    value_stream = streams[:, 2 * channels :]
    conv_value = conv_out.astype(jnp.float32)
    gated = (gate_second * conv_value).astype(jnp.bfloat16)
    grad_second = (upstream * conv_value).astype(jnp.bfloat16)
    grad_conv = upstream * gate_second
    inner, state, rate, weight = correlate_block(grad_conv, residues, decay_length)
    blank = jnp.zeros_like(gated)
    owned = reduced(
        state,
        rate,
        weight,
        inner,
        value_stream,
        gate_first,
        jnp.concatenate([grad_second, blank], axis=1),
        jnp.concatenate([blank, gated], axis=1),
        full_tokens,
        full_grads,
        owned_rows,
    )
    grad_in = jnp.stack(
        [owned[1, :, :channels], owned[0, :, :channels], owned[1, :, channels:]], axis=1
    )
    return (grad_in, owned[0, :, channels:])


def solution(mesh):
    return jax.shard_map(
        local,
        mesh=mesh,
        in_specs=(
            P("seq", "chan"),
            P("seq", "chan"),
            P("seq", None, "chan"),
            P("seq", "chan"),
            P("seq", "chan"),
            P(None, "chan"),
            P(None, "chan"),
        ),
        out_specs=(P("seq", None, "chan"), P("seq", "chan")),
        check_vma=False,
    )
```

```python
import functools
import math

import jax
import jax.numpy as jnp
from jax import lax
from jax.experimental import pallas as pl
from jax.experimental.pallas import tpu as pltpu
from jax.sharding import PartitionSpec as P

precise = lax.Precision.HIGHEST
MESH = pl.DeviceIdType.MESH


def remote(source, target, send_sem, recv_sem, device):
    return pltpu.make_async_remote_copy(
        src_ref=source,
        dst_ref=target,
        send_sem=send_sem,
        recv_sem=recv_sem,
        device_id=device,
        device_id_type=MESH,
    )


def greet(devices_seq, devices_chan, seq_wide):
    seq, chan = lax.axis_index("seq"), lax.axis_index("chan")
    barrier = pltpu.get_barrier_semaphore()
    count = 0
    if seq_wide == "all":

        def hello(step, carry):
            pl.semaphore_signal(
                barrier,
                inc=1,
                device_id=(lax.rem(seq + step, devices_seq), chan),
                device_id_type=MESH,
            )
            return carry

        lax.fori_loop(1, devices_seq, hello, 0)
        count += devices_seq - 1
    else:
        groups = devices_seq // 2

        def hello_group(step, carry):
            there = lax.rem(seq // 2 + step, groups) * 2 + seq % 2
            pl.semaphore_signal(barrier, inc=1, device_id=(there, chan), device_id_type=MESH)
            return carry

        lax.fori_loop(1, groups, hello_group, 0)
        pl.semaphore_signal(
            barrier, inc=1, device_id=(seq + 1 - 2 * (seq % 2), chan), device_id_type=MESH
        )
        count += groups
    if devices_chan:
        groups = devices_chan // 2
        for step in range(1, groups):
            there = lax.rem(chan // 2 + step, groups) * 2 + chan % 2
            pl.semaphore_signal(barrier, inc=1, device_id=(seq, there), device_id_type=MESH)
        pl.semaphore_signal(
            barrier, inc=1, device_id=(seq, chan + 1 - 2 * (chan % 2)), device_id_type=MESH
        )
        count += groups
    pl.semaphore_wait(barrier, count)


def gather_kernel(
    devices_seq,
    devices_chan,
    tokens,
    grads,
    weights,
    tokens_out,
    grads_out,
    projected,
    upstream,
    all_tokens,
    all_grads,
    all_weights,
    keep_sem,
    store_sem,
    chan_send,
    chan_recv,
    chan_pass,
    chan_passed,
    seq_send,
    seq_recv,
    seq_pass,
    seq_passed,
):
    seq, chan = lax.axis_index("seq"), lax.axis_index("chan")
    seq_groups, chan_groups = devices_seq // 2, devices_chan // 2
    seq_pair = (seq + 1 - 2 * (seq % 2), chan)
    chan_pair = (seq, chan + 1 - 2 * (chan % 2))
    columns = tokens.shape[1]
    rows = weights.shape[0]
    greet(devices_seq, devices_chan, "pairs")

    def block(ref, lines, index):
        return ref.at[lines, pl.ds(pl.multiple_of(index * columns, columns), columns)]

    def piece(index):
        return all_weights.at[pl.ds(pl.multiple_of(index * rows, rows), rows)]

    def chan_member(step, parity):
        return lax.rem(chan // 2 - step + chan_groups, chan_groups) * 2 + parity

    def seq_member(step, parity):
        return lax.rem(seq // 2 - step + seq_groups, seq_groups) * 2 + parity

    height = tokens.shape[0] // 2
    parts = [
        (own, whole, out, pl.ds(half * height, height))
        for own, whole, out in ((tokens, all_tokens, tokens_out), (grads, all_grads, grads_out))
        for half in range(2)
    ]

    def chan_copy(array, step):
        own, whole, _, lines = parts[array]
        there = lax.rem(chan // 2 + step, chan_groups) * 2 + chan % 2
        return remote(
            own.at[lines],
            block(whole, lines, chan),
            chan_send.at[array, step],
            chan_recv.at[array, step],
            (seq, there),
        )

    def chan_forward(array, step):
        own, whole, _, lines = parts[array]
        here = chan_member(step, chan % 2)
        return remote(
            own.at[lines] if step == 0 else block(whole, lines, here),
            block(whole, lines, here),
            chan_pass.at[array, step],
            chan_passed.at[array, step],
            chan_pair,
        )

    def seq_copy(step):
        there = lax.rem(seq // 2 + step, seq_groups) * 2 + seq % 2
        return remote(weights, piece(seq), seq_send.at[step], seq_recv.at[step], (there, chan))

    def seq_forward(step):
        here = seq_member(step, seq % 2)
        return remote(piece(here), piece(here), seq_pass.at[step], seq_passed.at[step], seq_pair)

    own_piece = remote(weights, piece(seq), seq_pass.at[0], seq_passed.at[0], seq_pair)

    def each(call):
        def body(step, carry):
            call(step)
            return carry

        lax.fori_loop(1, seq_groups, body, 0)

    def store(array):
        _, whole, out, lines = parts[array]
        return pltpu.make_async_copy(whole.at[lines], out.at[lines], store_sem.at[array])

    for array in range(4):
        for step in range(1, chan_groups):
            chan_copy(array, step).start()
    each(lambda step: seq_copy(step).start())
    own_piece.start()
    for array in range(4):
        chan_forward(array, 0).start()
    keeps = [pltpu.make_async_copy(weights, piece(seq), keep_sem.at[4])]
    for array, (own, whole, _, lines) in enumerate(parts):
        keeps.append(
            pltpu.make_async_copy(own.at[lines], block(whole, lines, chan), keep_sem.at[array])
        )
    for keep in keeps:
        keep.start()

    def pass_on(step):
        seq_copy(step).wait_recv()
        seq_forward(step).start()

    def pass_part(array):
        for step in range(1, chan_groups):
            chan_copy(array, step).wait_recv()
            chan_forward(array, step).start()

    pass_part(0)
    each(pass_on)
    for keep in keeps:
        keep.wait()
    own_piece.wait()

    def finish(step):
        seq_copy(step).wait_send()
        seq_forward(step).wait()

    each(finish)
    tile = math.gcd(height, 128)
    for array, (_, whole, _, lines) in enumerate(parts):
        if array + 1 < len(parts):
            pass_part(array + 1)
        for step in range(chan_groups):
            chan_forward(array, step).wait()
        store(array).start()
        target, first = (projected, 0) if array < 2 else (upstream, all_weights.shape[1] // 2)

        def product(index, carry):
            here = pl.ds(pl.multiple_of(array % 2 * height + index * tile, tile), tile)
            target[here] = jnp.dot(
                whole[here], all_weights[:, first:], preferred_element_type=jnp.float32
            )
            return carry

        lax.fori_loop(0, height // tile, product, 0)
    for array in range(4):
        store(array).wait()
        for step in range(1, chan_groups):
            chan_copy(array, step).wait_send()


def gathered(tokens, grads, weights):
    devices_seq, devices_chan = lax.axis_size("seq"), lax.axis_size("chan")
    dma = pltpu.SemaphoreType.DMA
    seq_groups, chan_groups = devices_seq // 2, devices_chan // 2
    vmem, anywhere = pl.BlockSpec(memory_space=pltpu.VMEM), pl.BlockSpec(memory_space=pl.ANY)
    wide = jax.ShapeDtypeStruct((tokens.shape[0], tokens.shape[1] * devices_chan), tokens.dtype)
    tall = jax.ShapeDtypeStruct((weights.shape[0] * devices_seq, weights.shape[1]), weights.dtype)
    return pl.pallas_call(
        functools.partial(gather_kernel, devices_seq, devices_chan),
        out_shape=(
            wide,
            wide,
            jax.ShapeDtypeStruct((tokens.shape[0], weights.shape[1]), jnp.float32),
            jax.ShapeDtypeStruct((tokens.shape[0], weights.shape[1] // 2), jnp.float32),
        ),
        in_specs=[vmem] * 3,
        out_specs=(anywhere, anywhere, vmem, vmem),
        scratch_shapes=[
            pltpu.VMEM(wide.shape, wide.dtype),
            pltpu.VMEM(wide.shape, wide.dtype),
            pltpu.VMEM(tall.shape, tall.dtype),
            dma((5,)),
            dma((4,)),
        ]
        + [dma((4, chan_groups))] * 4
        + [dma((seq_groups,))] * 4,
        compiler_params=pltpu.CompilerParams(collective_id=0, has_side_effects=True),
        name="gather_inputs",
    )(tokens, grads, weights)


def reduce_kernel(
    devices_seq,
    tile,
    state,
    rate,
    weight,
    inner,
    value,
    gate,
    early_in,
    early_out,
    tokens_hbm,
    grads_hbm,
    total,
    tokens,
    grads,
    states,
    late,
    parts,
    near,
    paired,
    far,
    load_sem,
    state_send,
    state_recv,
    pair_send,
    pair_recv,
    far_send,
    far_recv,
):
    seq, chan = lax.axis_index("seq"), lax.axis_index("chan")
    groups = devices_seq // 2
    group, parity = seq // 2, seq % 2
    rows, channels = inner.shape
    owned = near.shape[2]
    loads = [
        pltpu.make_async_copy(tokens_hbm, tokens, load_sem.at[0]),
        pltpu.make_async_copy(grads_hbm, grads, load_sem.at[1]),
    ]
    for load in loads:
        load.start()
    greet(devices_seq, 0, "all")

    def loop(start, stop, call):
        def body(step, carry):
            call(step)
            return carry

        lax.fori_loop(start, stop, body, 0)

    def state_copy(step):
        there = lax.rem(seq + step, devices_seq)
        return remote(
            state, states.at[step], state_send.at[step], state_recv.at[step], (there, chan)
        )

    def member(step):
        return lax.rem(group + step, groups)

    def piece(half, index):
        return parts.at[half, pl.ds(pl.multiple_of(index * owned, owned), owned)]

    def pair_copy(half, step):
        return remote(
            piece(half, member(step) * 2 + 1 - parity),
            near.at[half, step],
            pair_send.at[half, step],
            pair_recv.at[half, step],
            (group * 2 + 1 - parity, chan),
        )

    def far_copy(half, step):
        return remote(
            paired.at[half, step],
            far.at[half, step],
            far_send.at[half, step],
            far_recv.at[half, step],
            (member(step) * 2 + parity, chan),
        )

    def summed(left, right):
        return lax.dot_general(
            left, right, (((0,), (0,)), ((), ())), preferred_element_type=jnp.float32
        )

    def span(index):
        return pl.ds(pl.multiple_of(index * tile, tile), tile)

    loop(1, devices_seq, lambda step: state_copy(step).start())
    for load in loads:
        load.wait()

    def early_tile(index):
        product = summed(tokens[:, span(index)], early_in[...])
        product += summed(grads[:, span(index)], early_out[...])
        parts[0, span(index)] = product.astype(parts.dtype)

    loop(0, tokens.shape[1] // tile, early_tile)
    loop(1, groups, lambda step: pair_copy(0, step).start())
    pair_copy(0, 0).start()

    def absorb(step, following):
        state_copy(step).wait_recv()
        gap = lax.rem(seq - step + devices_seq, devices_seq) - seq - 1
        reach = (jnp.maximum(gap, 0) * rows).astype(jnp.float32)
        present = (gap >= 0).astype(jnp.float32)
        return following + present * states[step] * jnp.exp(-reach * rate[...])

    following = lax.fori_loop(1, devices_seq, absorb, jnp.zeros(rate.shape, jnp.float32))
    entering = weight[...] * following
    rates = rate[...]
    band = math.gcd(rows, 64)

    def source_rows(index):
        here = pl.ds(pl.multiple_of(index * band, band), band)
        position = lax.broadcasted_iota(jnp.int32, (band, channels), 0) + index * band
        reach = (rows - position).astype(jnp.float32)
        source = inner[here]
        for mode in range(rates.shape[0]):
            source += entering[mode : mode + 1] * jnp.exp(-reach * rates[mode : mode + 1])
        late[here] = jnp.concatenate([source * value[here], source * gate[here]], axis=1).astype(
            late.dtype
        )

    loop(0, rows // band, source_rows)

    def late_tile(index):
        parts[1, span(index)] = summed(tokens[:, span(index)], late[...]).astype(parts.dtype)

    loop(0, tokens.shape[1] // tile, late_tile)
    loop(1, groups, lambda step: pair_copy(1, step).start())
    pair_copy(1, 0).start()

    def pair_sum(half, step):
        own = piece(half, member(step) * 2 + parity)[...].astype(jnp.float32)
        return own + near[half, step].astype(jnp.float32)

    for half in range(2):

        def pass_on(step):
            pair_copy(half, step).wait_recv()
            paired[half, step] = pair_sum(half, step).astype(paired.dtype)
            far_copy(half, step).start()

        loop(1, groups, pass_on)
    for half in range(2):
        pair_copy(half, 0).wait_recv()
        total[half] = pair_sum(half, 0)

        def collect(step):
            far_copy(half, step).wait_recv()
            total[half] += far[half, step].astype(jnp.float32)

        loop(1, groups, collect)

        def finish(step):
            pair_copy(half, step).wait_send()
            far_copy(half, step).wait_send()

        loop(1, groups, finish)
        pair_copy(half, 0).wait_send()
    loop(1, devices_seq, lambda step: state_copy(step).wait_send())


def reduced(state, rate, weight, inner, value, gate, early_in, early_out, tokens, grads, owned):
    devices_seq = lax.axis_size("seq")
    groups = devices_seq // 2
    rows, channels = inner.shape
    width = tokens.shape[1]
    wide = 2 * channels
    vmem, anywhere = pl.BlockSpec(memory_space=pltpu.VMEM), pl.BlockSpec(memory_space=pl.ANY)
    dma, half_type = pltpu.SemaphoreType.DMA, tokens.dtype
    return pl.pallas_call(
        functools.partial(reduce_kernel, devices_seq, math.gcd(width, 512)),
        out_shape=jax.ShapeDtypeStruct((2, owned, wide), jnp.float32),
        in_specs=[vmem] * 8 + [anywhere] * 2,
        out_specs=vmem,
        scratch_shapes=[pltpu.VMEM(tokens.shape, half_type)] * 2
        + [pltpu.VMEM((devices_seq,) + state.shape, jnp.float32)]
        + [pltpu.VMEM((rows, wide), half_type), pltpu.VMEM((2, width, wide), half_type)]
        + [pltpu.VMEM((2, groups, owned, wide), half_type)] * 3
        + [dma((2,)), dma((devices_seq,)), dma((devices_seq,))]
        + [dma((2, groups))] * 4,
        compiler_params=pltpu.CompilerParams(collective_id=1, has_side_effects=True),
        name="reduce_owned",
    )(state, rate, weight, inner, value, gate, early_in, early_out, tokens, grads)


def correlate_block(signal, residues, decay_length):
    rows, channels = signal.shape
    chunk = min(64, rows)
    chunks = rows // chunk
    per_filter = channels // residues.shape[1]
    rate = jnp.repeat(1.0 / decay_length, per_filter, axis=1)
    weight = jnp.repeat(residues, per_filter, axis=1) * jnp.sqrt(-jnp.expm1(-2.0 * rate))
    offset = jnp.arange(chunk, dtype=jnp.float32)
    exponent = rate.T[:, :, None] * offset
    grow = weight.T[:, :, None] * jnp.exp(exponent)
    fall = jnp.exp(-exponent)
    later = jnp.arange(chunk)[None, :] >= jnp.arange(chunk)[:, None]
    taps = jnp.einsum("cri,crj->cij", grow, fall, precision=precise)
    taps = jnp.where(later, taps, 0.0)
    pieces = signal.reshape(chunks, chunk, channels).transpose(2, 1, 0)
    both = jnp.einsum(
        "cij,cjn->cin", jnp.concatenate([taps, fall], axis=1), pieces, precision=precise
    )
    inner, sums = both[:, :chunk], both[:, chunk:]
    step = jnp.exp(-chunk * rate).T
    state = jnp.zeros_like(step)
    entering = []
    for index in reversed(range(chunks)):
        entering.append(step * state)
        state = sums[:, :, index] + step * state
    entering = jnp.stack(entering[::-1], axis=2)
    outer = jnp.einsum("cri,crn->cin", grow, entering, precision=precise)
    return (inner + outer).transpose(2, 1, 0).reshape(rows, channels), state.T, rate, weight


def block_kernel(
    devices_seq,
    devices_chan,
    tokens_hbm,
    grads_hbm,
    in_weight,
    out_weight,
    conv_hbm,
    residues,
    decay_length,
    grad_in,
    grad_out,
    tokens,
    grads,
    conv,
    pieces,
    crossed,
    weights,
    partial,
    pair_in,
    chip_sum,
    far_in,
    late_sum,
    late_in,
    signal,
    consts,
    bank,
    own_state,
    states,
    flows,
    parts,
    kept,
    near,
    summed,
    blocks,
    arrived,
    results,
    given,
    load_sem,
    sent,
    hop_recv,
    swap_recv,
    keep_sem,
    twin_recv,
    pair_recv,
    far_recv,
    state_recv,
    flow_recv,
    pass_recv,
    near_recv,
    turn_recv,
    home_recv,
    put_sem,
):
    seq, chan = lax.axis_index("seq"), lax.axis_index("chan")
    planes = devices_chan
    twins = devices_seq // planes
    groups = devices_chan // 2
    plane, twin = seq // twins, seq % twins
    group, parity = chan // 2, chan % 2
    partner = (seq, chan + 1 - 2 * parity)
    channels, rows = conv.shape
    owned = out_weight.shape[1]

    def ahead(index, step, count):
        return lax.rem(index + step, count)

    def behind(index, step, count):
        return lax.rem(index - step + count, count)

    sources = (in_weight.at[1], out_weight, in_weight.at[0], in_weight.at[2])
    count = len(sources)
    weight_loads = [
        pltpu.make_async_copy(sources[part], pieces.at[part, plane], load_sem.at[part])
        for part in range(count)
    ]
    bulk_loads = [
        pltpu.make_async_copy(tokens_hbm, tokens, load_sem.at[count]),
        pltpu.make_async_copy(grads_hbm, grads, load_sem.at[count + 1]),
        pltpu.make_async_copy(conv_hbm, conv, load_sem.at[count + 2]),
    ]
    filter_loads = [
        pltpu.make_async_copy(residues, given.at[0], load_sem.at[count + 3]),
        pltpu.make_async_copy(decay_length, given.at[1], load_sem.at[count + 4]),
    ]
    for load in weight_loads + filter_loads + bulk_loads:
        load.start()

    barrier = pltpu.get_barrier_semaphore()
    for step in range(1, devices_seq):
        pl.semaphore_signal(
            barrier, inc=1, device_id=(ahead(seq, step, devices_seq), chan), device_id_type=MESH
        )
    for step in range(1, devices_chan):
        pl.semaphore_signal(
            barrier, inc=1, device_id=(seq, ahead(chan, step, devices_chan)), device_id_type=MESH
        )
    pl.semaphore_wait(barrier, devices_seq + devices_chan - 2)

    bits = [1 << power for power in reversed(range(planes.bit_length() - 1))]

    def flip(index, mask):
        result = index
        for bit in bits:
            if mask & bit:
                result = result + bit - 2 * bit * (index // bit % 2)
        return result

    def hop(part, which, kind, side):
        return remote(
            pieces.at[part, which],
            pieces.at[part, which],
            sent.at[kind],
            hop_recv.at[part, which],
            ((plane + side) * twins + twin, chan),
        )

    def onward(part, which, kind, side):
        edge = planes - 1 if side > 0 else 0

        @pl.when(plane != edge)
        def _():
            hop(part, which, kind, side).start()

    def cross(part, step, mask):
        here = flip(plane, mask)
        return remote(
            pieces.at[part, here],
            crossed.at[part, step, here],
            sent.at[14 + part // early],
            twin_recv.at[part, step - 1, mask],
            (plane * twins + ahead(twin, step, twins), chan),
        )

    def held(part, step, target):
        return crossed.at[part, step, target] if step else pieces.at[part, target]

    def swap(part, step, target):
        return remote(
            held(part, step, target),
            weights.at[part, behind(twin, step, twins), chan],
            sent.at[2 + part // early if step else 1],
            swap_recv.at[part, step],
            (seq, target),
        )

    def swap_in(part, step):
        landed = weights.at[part, behind(twin, step, twins), pl.ds(0, devices_chan - 1)]
        return remote(landed, landed, sent.at[2 + part // early if step else 1], swap_recv.at[part, step], partner)

    def keep(part, step):
        return pltpu.make_async_copy(
            held(part, step, chan),
            weights.at[part, behind(twin, step, twins), chan],
            keep_sem.at[part, step],
        )

    def deliver(part, step, mask):
        target = flip(plane, mask)

        @pl.when(target == chan)
        def _():
            keep(part, step).start()

        @pl.when(target != chan)
        def _():
            swap(part, step, target).start()

    early = count // 2

    crossing = ((0, 1, 3), (3,))

    def crosses(part, mask):
        return mask in crossing[part // early]

    def here(part, mask):
        if crosses(part, mask):
            for step in range(1, twins):
                cross(part, step, mask).start()
        deliver(part, 0, mask)

    def depart(group):
        for part in group:
            for side in (1, -1):
                onward(part, plane, 0, side)

    def arrive(group, distance):
        for part in group:
            for mask in range(1, planes):
                which = flip(plane, mask)
                for side in (1, -1):

                    @pl.when(plane - which == side * distance)
                    def _(mask=mask, which=which, side=side, part=part):
                        hop(part, which, 0, side).wait_recv()
                        onward(part, which, 16, side)
                        here(part, mask)

    def cross_on(part, mask):
        for step in range(1, twins):
            cross(part, step, mask).wait_recv()
            deliver(part, step, mask)

    def twin_copy(part, step):
        return remote(
            weights.at[part, twin],
            weights.at[part, twin],
            sent.at[4 + part // early],
            twin_recv.at[part, step - 1, 2],
            (plane * twins + ahead(twin, step, twins), chan),
        )

    def twin_in(part, step):
        there = behind(twin, step, twins)
        return remote(
            weights.at[part, there],
            weights.at[part, there],
            sent.at[4 + part // early],
            twin_recv.at[part, step - 1, 2],
            (plane * twins + there, chan),
        )

    def share(part, mask):
        @pl.when(flip(plane, mask) == chan)
        def _():
            swap_in(part, 0).wait_recv()
            keep(part, 0).wait()
            for step in range(1, twins):
                twin_copy(part, step).start()

    def loaded(part):
        weight_loads[part].wait()

    first, last = range(early), range(early, count)
    for part in range(count):
        loaded(part)
    depart(first)
    for part in first:
        here(part, 0)

    lanes = signal.shape[1]
    folds = lanes // channels
    groups_of_rows = 8
    span = signal.shape[0] // groups_of_rows
    modes, filters = residues.shape
    per_filter = channels // filters
    lane = lax.broadcasted_iota(jnp.int32, (filters, lanes), 1)
    which = lax.broadcasted_iota(jnp.int32, (filters, lanes), 0)
    spread = (lax.rem(lane, channels) // per_filter == which).astype(jnp.float32)
    for load in filter_loads:
        load.wait()
    inverse = 1.0 / given[1]
    twice = 2.0 * inverse
    series = jnp.zeros_like(twice)
    for order in range(10, 0, -1):
        series = (1.0 - series) * twice / order
    loss = jnp.where(twice < 0.5, series, 1.0 - jnp.exp(-twice))
    scale = given[0] * jnp.sqrt(loss)

    def widen(array):
        return jnp.dot(array, spread, precision=precise, preferred_element_type=jnp.float32)

    rate = widen(inverse)
    consts[0] = rate
    consts[1] = widen(scale)
    consts[2] = jnp.exp(-rate)

    inputs = (tokens, grads, tokens, tokens)

    def ready(part, step, mask):
        @pl.when(flip(plane, mask) == chan)
        def _():
            if crosses(part, mask):
                swap_in(part, step).wait_recv()
                keep(part, step).wait()
            elif step:
                twin_in(part, step).wait_recv()

    def project(part):
        for step in range(twins):
            block = behind(twin, step, twins)
            for mask in range(planes):
                ready(part, step, mask)
            columns = pl.ds(pl.multiple_of(block * owned, owned), owned)
            product = lax.dot_general(
                weights[part, block].reshape(devices_chan * channels, owned),
                inputs[part][:, columns],
                (((1,), (1,)), ((), ())),
                preferred_element_type=jnp.float32,
            )
            for target in range(devices_chan):
                piece = product[target * channels : (target + 1) * channels]
                place = (part, target % 2, target // 2)
                if step:
                    piece = partial[place] + piece
                partial[place] = piece

    def pair_copy(part, there):
        return remote(
            partial.at[part, 1 - parity, there],
            pair_in.at[part, there],
            sent.at[6],
            pair_recv.at[part, there],
            partner,
        )

    def far_copy(part, step):
        return remote(
            (chip_sum, late_sum)[part // early].at[part % early, step - 1],
            (far_in, late_in)[part // early].at[part % early, step - 1],
            sent.at[7 if part < early else 17],
            far_recv.at[part, step - 1],
            (seq, ahead(group, step, groups) * 2 + parity),
        )

    def pair_start(part):
        for step in range(1, groups + 1):
            pair_copy(part, ahead(group, step, groups)).start()

    def far_start(part):
        for step in range(1, groups):
            there = ahead(group, step, groups)
            pair_copy(part, there).wait_recv()
            total = partial[part, parity, there] + pair_in[part, there]
            if part < early:
                chip_sum[part, step - 1] = total
            else:
                late_sum[part - early, step - 1] = total.astype(late_sum.dtype)
            far_copy(part, step).start()

    def far_finish(part):
        pair_copy(part, group).wait_recv()
        total = partial[part, parity, group] + pair_in[part, group]
        for step in range(1, groups):
            far_copy(part, step).wait_recv()
            arriving = (far_in, late_in)[part // early]
            total = total + arriving[part % early, step - 1].astype(jnp.float32)
        return total

    def flow(part, step):
        return remote(
            flows.at[part, chan],
            flows.at[part, chan],
            sent.at[8],
            flow_recv.at[part, step - 1],
            (seq, ahead(group, step, groups) * 2 + parity),
        )

    def flow_in(part, step):
        source = behind(group, step, groups) * 2 + parity
        return remote(
            flows.at[part, source],
            flows.at[part, source],
            sent.at[8],
            flow_recv.at[part, step - 1],
            (seq, source),
        )

    def flow_pass(part, step):
        source = behind(group, step, groups) * 2 + parity
        return remote(
            flows.at[part, source],
            flows.at[part, source],
            sent.at[9],
            pass_recv.at[part, step],
            partner,
        )

    def flow_passed(part, step):
        source = behind(group, step, groups) * 2 + 1 - parity
        return remote(
            flows.at[part, source],
            flows.at[part, source],
            sent.at[9],
            pass_recv.at[part, step],
            partner,
        )

    def flow_start(part):
        for step in range(1, groups):
            flow(part, step).start()
        flow_pass(part, 0).start()

    def flow_on(part):
        for step in range(1, groups):
            flow_in(part, step).wait_recv()
            flow_pass(part, step).start()

    def flow_finish(part):
        for step in range(groups):
            flow_passed(part, step).wait_recv()

    def near_copy(part, step, target):
        return remote(
            parts.at[part, step - 1, target],
            near.at[part, step - 1, target],
            sent.at[10],
            near_recv.at[part, step - 1, target],
            (plane * twins + ahead(twin, step, twins), chan),
        )

    def multiply(part):
        for step in range(1, twins + 1):
            block = ahead(twin, step, twins)
            columns = pl.ds(pl.multiple_of(block * owned, owned), owned)
            product = jnp.dot(
                flows[part].reshape(devices_chan * channels, rows),
                inputs[part][:, columns],
                preferred_element_type=jnp.float32,
            )
            for target in range(devices_chan):
                piece = product[target * channels : (target + 1) * channels]
                if step < twins:
                    parts[part, step - 1, target] = piece.astype(parts.dtype)
                else:
                    kept[part, target] = piece
            if step < twins:
                for index in range(1, devices_chan + 1):
                    near_copy(part, step, ahead(chan, index, devices_chan)).start()

    def turn(part, target):
        return remote(
            summed.at[part, target],
            blocks.at[part, chan],
            sent.at[11],
            turn_recv.at[part, chan],
            (seq, target),
        )

    def turn_in(part, source):
        return remote(
            summed.at[part, source],
            blocks.at[part, source],
            sent.at[11],
            turn_recv.at[part, source],
            (seq, source),
        )

    straight = (0, 1, 2, 3)

    def home(part, mask):
        return remote(
            blocks.at[part, flip(plane, mask)],
            arrived.at[part, mask],
            sent.at[12],
            home_recv.at[part, mask - 1],
            (flip(plane, mask if part in straight else mask & -mask) * twins + twin, chan),
        )

    def turn_start(part, index):
        target = ahead(chan, index, devices_chan)
        total = kept[part, target]
        for step in range(1, twins):
            near_copy(part, step, target).wait_recv()
            total = total + near[part, step - 1, target].astype(jnp.float32)
        total = total.astype(blocks.dtype)
        if index < devices_chan:
            summed[part, target] = total
            turn(part, target).start()
        else:
            blocks[part, chan] = total

    def turned(part, index):
        source = behind(chan, index, devices_chan)
        if index < devices_chan:
            turn_in(part, source).wait_recv()

        for mask in range(1, planes, 1 if part in straight else 2):

            @pl.when(flip(plane, mask) == source)
            def _(mask=mask):
                home(part, mask).start()

    def gathered(part, mask):
        total = blocks[part, flip(plane, mask)].astype(jnp.float32)
        for other in range(1, planes) if part in straight else reversed(bits):
            if mask == 0 or other < mask & -mask:
                home(part, mask ^ other).wait_recv()
                total = total + arrived[part, mask ^ other].astype(jnp.float32)
        return total

    targets = (grad_in.at[1], grad_out, grad_in.at[0], grad_in.at[2])

    def put(part):
        return pltpu.make_async_copy(results.at[part], targets[part], put_sem.at[part])

    def finish(part):
        results[part] = gathered(part, 0)
        put(part).start()

    def home_on(part):
        for mask in range(planes - 1, 0, -1):
            if mask & -mask > 1 and part not in straight:
                blocks[part, flip(plane, mask)] = gathered(part, mask).astype(blocks.dtype)
                home(part, mask).start()

    def rowed(array):
        width = array.shape[1] // folds
        stacked = jnp.concatenate(
            [array[:, fold * width : (fold + 1) * width] for fold in range(folds)], axis=0
        )
        return stacked.T

    def unrowed(array):
        stacked = array.T
        return jnp.concatenate(
            [stacked[fold * channels : (fold + 1) * channels] for fold in range(folds)], axis=1
        )

    def mode_row(kind, mode):
        return jnp.broadcast_to(consts[kind, mode : mode + 1], (groups_of_rows, lanes))

    def line(index):
        return pl.ds(index, groups_of_rows, stride=span)

    def scan_states():
        fall = [mode_row(2, mode) for mode in range(modes)]

        def body(step, carry):
            here = signal[line(span - 1 - step)]
            return tuple(carry[mode] * fall[mode] + here for mode in range(modes))

        zero = jnp.zeros((groups_of_rows, lanes), jnp.float32)
        found = lax.fori_loop(0, span, body, (zero,) * modes)
        position = lax.broadcasted_iota(jnp.int32, (groups_of_rows, lanes), 0)
        for mode in range(modes):
            each = mode_row(0, mode) * span
            total = found[mode]
            shift = 1
            while shift < groups_of_rows:
                moved = pltpu.roll(total, groups_of_rows - shift, 0)
                moved = moved * jnp.exp(-each * shift)
                total = total + jnp.where(position < groups_of_rows - shift, moved, 0.0)
                shift *= 2
            moved = pltpu.roll(total, groups_of_rows - 1, 0)
            bank[mode] = jnp.where(position < groups_of_rows - 1, moved, 0.0)
            own_state[mode : mode + 1] = total[0:1]
        heads = own_state[...]
        reach = consts[0] * (span * groups_of_rows)
        later = pltpu.roll(heads, channels, 1)
        first = lax.broadcasted_iota(jnp.int32, (modes, lanes), 1) < channels
        consts[3] = jnp.where(first, later, 0.0)
        own_state[...] = jnp.where(first, heads + later * jnp.exp(-reach), 0.0)

    def state_copy(step):
        return remote(
            own_state,
            states.at[step],
            sent.at[13],
            state_recv,
            (ahead(seq, step, devices_seq), chan),
        )

    def scan_source():
        rates = consts[0]
        following = jnp.zeros((modes, lanes), jnp.float32)
        landed = states.at[pl.ds(1, devices_seq - 1)]
        remote(landed, landed, sent.at[13], state_recv, partner).wait_recv()
        for step in range(1, devices_seq):
            gap = behind(seq, step, devices_seq) - seq - 1
            reach = (jnp.maximum(gap, 0) * rows).astype(jnp.float32)
            present = (gap >= 0).astype(jnp.float32)
            following = following + present * states[step] * jnp.exp(-reach * rates)
        first = lax.broadcasted_iota(jnp.int32, (modes, lanes), 1) < channels
        after = pltpu.roll(following, channels, 1)
        within = following * jnp.exp(-(rates * (span * groups_of_rows)))
        consts[3] = jnp.where(first, consts[3] + within, after)
        fall = [mode_row(2, mode) for mode in range(modes)]
        weigh = [mode_row(1, mode) for mode in range(modes)]
        position = lax.broadcasted_iota(jnp.int32, (groups_of_rows, lanes), 0)
        left = ((groups_of_rows - 1 - position) * span).astype(jnp.float32)
        start = tuple(
            bank[mode] + mode_row(3, mode) * jnp.exp(-left * mode_row(0, mode))
            for mode in range(modes)
        )

        def body(step, carry):
            here = line(span - 1 - step)
            entry = signal[here]
            following = tuple(carry[mode] * fall[mode] + entry for mode in range(modes))
            terms = [following[mode] * weigh[mode] for mode in range(modes)]
            while len(terms) > 1:
                terms = [sum(terms[at : at + 2]) for at in range(0, len(terms), 2)]
            signal[here] = terms[0]
            return following

        lax.fori_loop(0, span, body, start)

    def settle(group, mask):
        for part in group:
            if crosses(part, mask):
                cross_on(part, mask)
            else:
                share(part, mask)

    arrive(first, 1)
    settle(first, 0)
    arrive(first, 2)
    depart(last)
    for part in last:
        here(part, 0)
    settle(first, 1)
    arrive(first, 3)
    settle(first, 2)
    arrive(last, 1)
    settle(last, 0)
    settle(first, 3)
    arrive(last, 2)
    settle(last, 1)
    for load in bulk_loads:
        load.wait()
    project(0)
    pair_start(0)
    project(1)
    pair_start(1)
    arrive(last, 3)
    settle(last, 2)
    far_start(0)
    far_start(1)
    taken = conv[...].astype(jnp.float32)
    second = far_finish(0).astype(flows.dtype).astype(jnp.float32)
    flows[1, chan] = (second * taken).astype(flows.dtype)
    flow_start(1)
    settle(last, 3)
    upstream = far_finish(1)
    flows[0, chan] = (upstream * taken).astype(flows.dtype)
    flow_start(0)
    signal[...] = rowed(upstream * second)
    flow_on(1)
    scan_states()
    for step in range(1, devices_seq):
        state_copy(step).start()
    project(2)
    pair_start(2)
    flow_finish(1)
    multiply(1)
    project(3)
    pair_start(3)
    far_start(2)
    far_start(3)
    flow_on(0)
    flow_finish(0)
    multiply(0)
    turn_start(1, 1)
    scan_source()
    source = unrowed(signal[...])
    turn_start(1, 2)
    late = far_finish(2).astype(flows.dtype).astype(jnp.float32)
    flows[3, chan] = (source * late).astype(flows.dtype)
    flow_start(3)
    late = far_finish(3).astype(flows.dtype).astype(jnp.float32)
    flows[2, chan] = (source * late).astype(flows.dtype)
    flow_start(2)
    turn_start(1, 3)
    turned(1, 1)
    turn_start(1, 4)
    turned(1, 2)
    flow_on(3)
    turn_start(0, 1)
    turned(1, 3)
    flow_on(2)
    turn_start(0, 2)
    flow_finish(3)
    multiply(3)
    flow_finish(2)
    multiply(2)
    turned(1, 4)
    turn_start(0, 3)
    turned(0, 1)
    turn_start(0, 4)
    turned(0, 2)
    turned(0, 3)
    turned(0, 4)
    turn_start(3, 1)
    turn_start(3, 2)
    turn_start(3, 3)
    turned(3, 1)
    turn_start(3, 4)
    turned(3, 2)
    turn_start(2, 1)
    turned(3, 3)
    turn_start(2, 2)
    turned(3, 4)
    turn_start(2, 3)
    turned(2, 1)
    turn_start(2, 4)
    turned(2, 2)
    turned(2, 3)
    turned(2, 4)
    finish(1)
    finish(0)
    finish(3)
    finish(2)
    for part in range(count):
        put(part).wait()

    def left(kind, ref):
        remote(ref, ref, sent.at[kind], state_recv, partner).wait_send()

    fewer = pl.ds(0, planes - 1)
    others = pl.ds(1, twins - 1)
    inner = jnp.logical_and(plane > 0, plane < planes - 1)

    @pl.when(inner)
    def _():
        left(0, pieces.at[:, pl.ds(0, 2)])
        left(16, pieces.at[:, fewer])

    @pl.when(jnp.logical_not(inner))
    def _():
        left(0, pieces.at[:, pl.ds(0, 1)])

    left(1, pieces.at[:, fewer])
    for group in range(2):
        span_of = pl.ds(group * early, early)
        masks = crossing[group]
        if masks:
            left(14 + group, crossed.at[span_of, others, pl.ds(0, len(masks))])
        for mask in range(planes):

            @pl.when(flip(plane, mask) == chan)
            def _(mask=mask):
                swaps = len(masks) - (mask in masks)
                if swaps:
                    left(2 + group, crossed.at[span_of, others, pl.ds(0, swaps)])
                if mask not in masks:
                    left(4 + group, weights.at[span_of, others])

    left(6, partial.at[:, 0])
    left(7, chip_sum)
    left(17, late_sum)
    left(8, flows.at[:, pl.ds(0, groups - 1)])
    left(9, flows.at[:, pl.ds(0, groups)])
    left(10, parts)
    left(11, summed.at[:, fewer])
    left(12, blocks.at[:, fewer])
    left(13, states.at[pl.ds(1, devices_seq - 1)])


def place_kernel(grad_in, grad_proj, out_in, out_proj, held, take_sem, give_sem):
    streams = grad_in.shape[0]
    ends = [(grad_in.at[at], out_in.at[at]) for at in range(streams)] + [(grad_proj, out_proj)]
    takes = [
        pltpu.make_async_copy(source, held.at[at], take_sem.at[at])
        for at, (source, _) in enumerate(ends)
    ]
    gives = [
        pltpu.make_async_copy(held.at[at], target, give_sem.at[at])
        for at, (_, target) in enumerate(ends)
    ]
    for take in takes:
        take.start()
    for take, give in zip(takes, gives):
        take.wait()
        give.start()
    for give in gives:
        give.wait()


def placed(grad_in, grad_proj):
    anywhere, dma = pl.BlockSpec(memory_space=pl.ANY), pltpu.SemaphoreType.DMA
    count = grad_in.shape[0] + 1
    return pl.pallas_call(
        place_kernel,
        out_shape=tuple(jax.ShapeDtypeStruct(a.shape, a.dtype) for a in (grad_in, grad_proj)),
        in_specs=[anywhere] * 2,
        out_specs=(anywhere, anywhere),
        scratch_shapes=[
            pltpu.VMEM((count,) + grad_proj.shape, grad_proj.dtype),
            dma((count,)),
            dma((count,)),
        ],
        name="place_outputs",
    )(grad_in, grad_proj)


def fits(tokens, conv_out, in_weight, residues):
    devices_seq, devices_chan = lax.axis_size("seq"), lax.axis_size("chan")
    rows, channels = conv_out.shape
    return (
        devices_chan == 4
        and devices_seq % devices_chan == 0
        and devices_seq > devices_chan
        and in_weight.shape[0] % 128 == 0
        and 2 * channels == 128
        and channels % residues.shape[1] == 0
        and rows % 256 == 0
        and tokens.shape[1] * devices_chan == in_weight.shape[0] * devices_seq
    )


def blocked(tokens, grad_out, in_weight, out_weight, conv_out, residues, decay_length):
    devices_seq, devices_chan = lax.axis_size("seq"), lax.axis_size("chan")
    planes, groups = devices_chan, devices_chan // 2
    twins = devices_seq // planes
    rows, width = tokens.shape
    channels, owned = out_weight.shape[1], out_weight.shape[0]
    modes = residues.shape[0]
    anywhere = pl.BlockSpec(memory_space=pl.ANY)
    dma, half_type, full = pltpu.SemaphoreType.DMA, tokens.dtype, jnp.float32
    lanes = 2 * channels
    grad_in, grad_proj = pl.pallas_call(
        functools.partial(block_kernel, devices_seq, devices_chan),
        out_shape=(
            jax.ShapeDtypeStruct((3, channels, owned), full),
            jax.ShapeDtypeStruct((channels, owned), full),
        ),
        in_specs=[anywhere] * 7,
        out_specs=(anywhere, anywhere),
        scratch_shapes=[
            pltpu.VMEM((rows, width), half_type),
            pltpu.VMEM((rows, width), half_type),
            pltpu.VMEM((channels, rows), half_type),
            pltpu.VMEM((4, planes, channels, owned), half_type),
            pltpu.VMEM((4, twins, planes, channels, owned), half_type),
            pltpu.VMEM((4, twins, devices_chan, channels, owned), half_type),
            pltpu.VMEM((4, 2, groups, channels, rows), full),
            pltpu.VMEM((4, groups, channels, rows), full),
            pltpu.VMEM((2, groups - 1, channels, rows), full),
            pltpu.VMEM((2, groups - 1, channels, rows), full),
            pltpu.VMEM((2, groups - 1, channels, rows), half_type),
            pltpu.VMEM((2, groups - 1, channels, rows), half_type),
            pltpu.VMEM((rows * channels // lanes, lanes), full),
            pltpu.VMEM((4, modes, lanes), full),
            pltpu.VMEM((modes, 8, lanes), full),
            pltpu.VMEM((modes, lanes), full),
            pltpu.VMEM((devices_seq, modes, lanes), full),
            pltpu.VMEM((4, devices_chan, channels, rows), half_type),
            pltpu.VMEM((4, twins - 1, devices_chan, channels, owned), half_type),
            pltpu.VMEM((4, devices_chan, channels, owned), full),
            pltpu.VMEM((4, twins - 1, devices_chan, channels, owned), half_type),
            pltpu.VMEM((4, devices_chan, channels, owned), half_type),
            pltpu.VMEM((4, planes, channels, owned), half_type),
            pltpu.VMEM((4, planes, channels, owned), half_type),
            pltpu.VMEM((4, channels, owned), full),
            pltpu.VMEM((2,) + residues.shape, full),
            dma((9,)),
            dma((18,)),
            dma((4, planes)),
            dma((4, twins)),
            dma((4, twins)),
            dma((4, twins - 1, planes)),
        ]
        + [dma((4, groups)), dma((4, groups - 1)), dma, dma((4, groups - 1)), dma((4, groups))]
        + [dma((4, twins - 1, planes))]
        + [dma((4, planes)), dma((4, planes - 1)), dma((4,))],
        compiler_params=pltpu.CompilerParams(collective_id=2, has_side_effects=True),
        name="conv_block",
    )(
        tokens,
        grad_out,
        in_weight.transpose(1, 2, 0),
        out_weight.T,
        conv_out.T,
        residues,
        decay_length,
    )
    grad_in, grad_proj = placed(grad_in, grad_proj)
    return grad_in.transpose(2, 0, 1), grad_proj.T


def local(tokens, grad_out, in_weight, out_weight, conv_out, residues, decay_length):
    if fits(tokens, conv_out, in_weight, residues):
        return blocked(tokens, grad_out, in_weight, out_weight, conv_out, residues, decay_length)
    channels = out_weight.shape[1]
    owned_rows = in_weight.shape[0]
    weights = jnp.concatenate([in_weight.reshape(owned_rows, 3 * channels), out_weight], axis=1)
    full_tokens, full_grads, projected, upstream = gathered(tokens, grad_out, weights)
    projected = projected[:, : 3 * channels]
    upstream = upstream[:, channels:]
    streams = lax.reduce_precision(projected, exponent_bits=8, mantissa_bits=7)
    gate_first = streams[:, :channels]
    gate_second = streams[:, channels : 2 * channels]
    value_stream = streams[:, 2 * channels :]
    conv_value = conv_out.astype(jnp.float32)
    gated = (gate_second * conv_value).astype(jnp.bfloat16)
    grad_second = (upstream * conv_value).astype(jnp.bfloat16)
    grad_conv = upstream * gate_second
    inner, state, rate, weight = correlate_block(grad_conv, residues, decay_length)
    blank = jnp.zeros_like(gated)
    owned = reduced(
        state,
        rate,
        weight,
        inner,
        value_stream,
        gate_first,
        jnp.concatenate([grad_second, blank], axis=1),
        jnp.concatenate([blank, gated], axis=1),
        full_tokens,
        full_grads,
        owned_rows,
    )
    grad_in = jnp.stack(
        [owned[1, :, :channels], owned[0, :, :channels], owned[1, :, channels:]], axis=1
    )
    return (grad_in, owned[0, :, channels:])


def solution(mesh):
    return jax.shard_map(
        local,
        mesh=mesh,
        in_specs=(
            P("seq", "chan"),
            P("seq", "chan"),
            P("seq", None, "chan"),
            P("seq", "chan"),
            P("seq", "chan"),
            P(None, "chan"),
            P(None, "chan"),
        ),
        out_specs=(P("seq", None, "chan"), P("seq", "chan")),
        check_vma=False,
    )
```

```python
import functools
import math

import jax
import jax.numpy as jnp
from jax import lax
from jax.experimental import pallas as pl
from jax.experimental.pallas import tpu as pltpu
from jax.sharding import PartitionSpec as P

precise = lax.Precision.HIGHEST
MESH = pl.DeviceIdType.MESH


def remote(source, target, send_sem, recv_sem, device):
    return pltpu.make_async_remote_copy(
        src_ref=source,
        dst_ref=target,
        send_sem=send_sem,
        recv_sem=recv_sem,
        device_id=device,
        device_id_type=MESH,
    )


def greet(devices_seq, devices_chan, seq_wide):
    seq, chan = lax.axis_index("seq"), lax.axis_index("chan")
    barrier = pltpu.get_barrier_semaphore()
    count = 0
    if seq_wide == "all":

        def hello(step, carry):
            pl.semaphore_signal(
                barrier,
                inc=1,
                device_id=(lax.rem(seq + step, devices_seq), chan),
                device_id_type=MESH,
            )
            return carry

        lax.fori_loop(1, devices_seq, hello, 0)
        count += devices_seq - 1
    else:
        groups = devices_seq // 2

        def hello_group(step, carry):
            there = lax.rem(seq // 2 + step, groups) * 2 + seq % 2
            pl.semaphore_signal(barrier, inc=1, device_id=(there, chan), device_id_type=MESH)
            return carry

        lax.fori_loop(1, groups, hello_group, 0)
        pl.semaphore_signal(
            barrier, inc=1, device_id=(seq + 1 - 2 * (seq % 2), chan), device_id_type=MESH
        )
        count += groups
    if devices_chan:
        groups = devices_chan // 2
        for step in range(1, groups):
            there = lax.rem(chan // 2 + step, groups) * 2 + chan % 2
            pl.semaphore_signal(barrier, inc=1, device_id=(seq, there), device_id_type=MESH)
        pl.semaphore_signal(
            barrier, inc=1, device_id=(seq, chan + 1 - 2 * (chan % 2)), device_id_type=MESH
        )
        count += groups
    pl.semaphore_wait(barrier, count)


def gather_kernel(
    devices_seq,
    devices_chan,
    tokens,
    grads,
    weights,
    tokens_out,
    grads_out,
    projected,
    upstream,
    all_tokens,
    all_grads,
    all_weights,
    keep_sem,
    store_sem,
    chan_send,
    chan_recv,
    chan_pass,
    chan_passed,
    seq_send,
    seq_recv,
    seq_pass,
    seq_passed,
):
    seq, chan = lax.axis_index("seq"), lax.axis_index("chan")
    seq_groups, chan_groups = devices_seq // 2, devices_chan // 2
    seq_pair = (seq + 1 - 2 * (seq % 2), chan)
    chan_pair = (seq, chan + 1 - 2 * (chan % 2))
    columns = tokens.shape[1]
    rows = weights.shape[0]
    greet(devices_seq, devices_chan, "pairs")

    def block(ref, lines, index):
        return ref.at[lines, pl.ds(pl.multiple_of(index * columns, columns), columns)]

    def piece(index):
        return all_weights.at[pl.ds(pl.multiple_of(index * rows, rows), rows)]

    def chan_member(step, parity):
        return lax.rem(chan // 2 - step + chan_groups, chan_groups) * 2 + parity

    def seq_member(step, parity):
        return lax.rem(seq // 2 - step + seq_groups, seq_groups) * 2 + parity

    height = tokens.shape[0] // 2
    parts = [
        (own, whole, out, pl.ds(half * height, height))
        for own, whole, out in ((tokens, all_tokens, tokens_out), (grads, all_grads, grads_out))
        for half in range(2)
    ]

    def chan_copy(array, step):
        own, whole, _, lines = parts[array]
        there = lax.rem(chan // 2 + step, chan_groups) * 2 + chan % 2
        return remote(
            own.at[lines],
            block(whole, lines, chan),
            chan_send.at[array, step],
            chan_recv.at[array, step],
            (seq, there),
        )

    def chan_forward(array, step):
        own, whole, _, lines = parts[array]
        here = chan_member(step, chan % 2)
        return remote(
            own.at[lines] if step == 0 else block(whole, lines, here),
            block(whole, lines, here),
            chan_pass.at[array, step],
            chan_passed.at[array, step],
            chan_pair,
        )

    def seq_copy(step):
        there = lax.rem(seq // 2 + step, seq_groups) * 2 + seq % 2
        return remote(weights, piece(seq), seq_send.at[step], seq_recv.at[step], (there, chan))

    def seq_forward(step):
        here = seq_member(step, seq % 2)
        return remote(piece(here), piece(here), seq_pass.at[step], seq_passed.at[step], seq_pair)

    own_piece = remote(weights, piece(seq), seq_pass.at[0], seq_passed.at[0], seq_pair)

    def each(call):
        def body(step, carry):
            call(step)
            return carry

        lax.fori_loop(1, seq_groups, body, 0)

    def store(array):
        _, whole, out, lines = parts[array]
        return pltpu.make_async_copy(whole.at[lines], out.at[lines], store_sem.at[array])

    for array in range(4):
        for step in range(1, chan_groups):
            chan_copy(array, step).start()
    each(lambda step: seq_copy(step).start())
    own_piece.start()
    for array in range(4):
        chan_forward(array, 0).start()
    keeps = [pltpu.make_async_copy(weights, piece(seq), keep_sem.at[4])]
    for array, (own, whole, _, lines) in enumerate(parts):
        keeps.append(
            pltpu.make_async_copy(own.at[lines], block(whole, lines, chan), keep_sem.at[array])
        )
    for keep in keeps:
        keep.start()

    def pass_on(step):
        seq_copy(step).wait_recv()
        seq_forward(step).start()

    def pass_part(array):
        for step in range(1, chan_groups):
            chan_copy(array, step).wait_recv()
            chan_forward(array, step).start()

    pass_part(0)
    each(pass_on)
    for keep in keeps:
        keep.wait()
    own_piece.wait()

    def finish(step):
        seq_copy(step).wait_send()
        seq_forward(step).wait()

    each(finish)
    tile = math.gcd(height, 128)
    for array, (_, whole, _, lines) in enumerate(parts):
        if array + 1 < len(parts):
            pass_part(array + 1)
        for step in range(chan_groups):
            chan_forward(array, step).wait()
        store(array).start()
        target, first = (projected, 0) if array < 2 else (upstream, all_weights.shape[1] // 2)

        def product(index, carry):
            here = pl.ds(pl.multiple_of(array % 2 * height + index * tile, tile), tile)
            target[here] = jnp.dot(
                whole[here], all_weights[:, first:], preferred_element_type=jnp.float32
            )
            return carry

        lax.fori_loop(0, height // tile, product, 0)
    for array in range(4):
        store(array).wait()
        for step in range(1, chan_groups):
            chan_copy(array, step).wait_send()


def gathered(tokens, grads, weights):
    devices_seq, devices_chan = lax.axis_size("seq"), lax.axis_size("chan")
    dma = pltpu.SemaphoreType.DMA
    seq_groups, chan_groups = devices_seq // 2, devices_chan // 2
    vmem, anywhere = pl.BlockSpec(memory_space=pltpu.VMEM), pl.BlockSpec(memory_space=pl.ANY)
    wide = jax.ShapeDtypeStruct((tokens.shape[0], tokens.shape[1] * devices_chan), tokens.dtype)
    tall = jax.ShapeDtypeStruct((weights.shape[0] * devices_seq, weights.shape[1]), weights.dtype)
    return pl.pallas_call(
        functools.partial(gather_kernel, devices_seq, devices_chan),
        out_shape=(
            wide,
            wide,
            jax.ShapeDtypeStruct((tokens.shape[0], weights.shape[1]), jnp.float32),
            jax.ShapeDtypeStruct((tokens.shape[0], weights.shape[1] // 2), jnp.float32),
        ),
        in_specs=[vmem] * 3,
        out_specs=(anywhere, anywhere, vmem, vmem),
        scratch_shapes=[
            pltpu.VMEM(wide.shape, wide.dtype),
            pltpu.VMEM(wide.shape, wide.dtype),
            pltpu.VMEM(tall.shape, tall.dtype),
            dma((5,)),
            dma((4,)),
        ]
        + [dma((4, chan_groups))] * 4
        + [dma((seq_groups,))] * 4,
        compiler_params=pltpu.CompilerParams(collective_id=0, has_side_effects=True),
        name="gather_inputs",
    )(tokens, grads, weights)


def reduce_kernel(
    devices_seq,
    tile,
    state,
    rate,
    weight,
    inner,
    value,
    gate,
    early_in,
    early_out,
    tokens_hbm,
    grads_hbm,
    total,
    tokens,
    grads,
    states,
    late,
    parts,
    near,
    paired,
    far,
    load_sem,
    state_send,
    state_recv,
    pair_send,
    pair_recv,
    far_send,
    far_recv,
):
    seq, chan = lax.axis_index("seq"), lax.axis_index("chan")
    groups = devices_seq // 2
    group, parity = seq // 2, seq % 2
    rows, channels = inner.shape
    owned = near.shape[2]
    loads = [
        pltpu.make_async_copy(tokens_hbm, tokens, load_sem.at[0]),
        pltpu.make_async_copy(grads_hbm, grads, load_sem.at[1]),
    ]
    for load in loads:
        load.start()
    greet(devices_seq, 0, "all")

    def loop(start, stop, call):
        def body(step, carry):
            call(step)
            return carry

        lax.fori_loop(start, stop, body, 0)

    def state_copy(step):
        there = lax.rem(seq + step, devices_seq)
        return remote(
            state, states.at[step], state_send.at[step], state_recv.at[step], (there, chan)
        )

    def member(step):
        return lax.rem(group + step, groups)

    def piece(half, index):
        return parts.at[half, pl.ds(pl.multiple_of(index * owned, owned), owned)]

    def pair_copy(half, step):
        return remote(
            piece(half, member(step) * 2 + 1 - parity),
            near.at[half, step],
            pair_send.at[half, step],
            pair_recv.at[half, step],
            (group * 2 + 1 - parity, chan),
        )

    def far_copy(half, step):
        return remote(
            paired.at[half, step],
            far.at[half, step],
            far_send.at[half, step],
            far_recv.at[half, step],
            (member(step) * 2 + parity, chan),
        )

    def summed(left, right):
        return lax.dot_general(
            left, right, (((0,), (0,)), ((), ())), preferred_element_type=jnp.float32
        )

    def span(index):
        return pl.ds(pl.multiple_of(index * tile, tile), tile)

    loop(1, devices_seq, lambda step: state_copy(step).start())
    for load in loads:
        load.wait()

    def early_tile(index):
        product = summed(tokens[:, span(index)], early_in[...])
        product += summed(grads[:, span(index)], early_out[...])
        parts[0, span(index)] = product.astype(parts.dtype)

    loop(0, tokens.shape[1] // tile, early_tile)
    loop(1, groups, lambda step: pair_copy(0, step).start())
    pair_copy(0, 0).start()

    def absorb(step, following):
        state_copy(step).wait_recv()
        gap = lax.rem(seq - step + devices_seq, devices_seq) - seq - 1
        reach = (jnp.maximum(gap, 0) * rows).astype(jnp.float32)
        present = (gap >= 0).astype(jnp.float32)
        return following + present * states[step] * jnp.exp(-reach * rate[...])

    following = lax.fori_loop(1, devices_seq, absorb, jnp.zeros(rate.shape, jnp.float32))
    entering = weight[...] * following
    rates = rate[...]
    band = math.gcd(rows, 64)

    def source_rows(index):
        here = pl.ds(pl.multiple_of(index * band, band), band)
        position = lax.broadcasted_iota(jnp.int32, (band, channels), 0) + index * band
        reach = (rows - position).astype(jnp.float32)
        source = inner[here]
        for mode in range(rates.shape[0]):
            source += entering[mode : mode + 1] * jnp.exp(-reach * rates[mode : mode + 1])
        late[here] = jnp.concatenate([source * value[here], source * gate[here]], axis=1).astype(
            late.dtype
        )

    loop(0, rows // band, source_rows)

    def late_tile(index):
        parts[1, span(index)] = summed(tokens[:, span(index)], late[...]).astype(parts.dtype)

    loop(0, tokens.shape[1] // tile, late_tile)
    loop(1, groups, lambda step: pair_copy(1, step).start())
    pair_copy(1, 0).start()

    def pair_sum(half, step):
        own = piece(half, member(step) * 2 + parity)[...].astype(jnp.float32)
        return own + near[half, step].astype(jnp.float32)

    for half in range(2):

        def pass_on(step):
            pair_copy(half, step).wait_recv()
            paired[half, step] = pair_sum(half, step).astype(paired.dtype)
            far_copy(half, step).start()

        loop(1, groups, pass_on)
    for half in range(2):
        pair_copy(half, 0).wait_recv()
        total[half] = pair_sum(half, 0)

        def collect(step):
            far_copy(half, step).wait_recv()
            total[half] += far[half, step].astype(jnp.float32)

        loop(1, groups, collect)

        def finish(step):
            pair_copy(half, step).wait_send()
            far_copy(half, step).wait_send()

        loop(1, groups, finish)
        pair_copy(half, 0).wait_send()
    loop(1, devices_seq, lambda step: state_copy(step).wait_send())


def reduced(state, rate, weight, inner, value, gate, early_in, early_out, tokens, grads, owned):
    devices_seq = lax.axis_size("seq")
    groups = devices_seq // 2
    rows, channels = inner.shape
    width = tokens.shape[1]
    wide = 2 * channels
    vmem, anywhere = pl.BlockSpec(memory_space=pltpu.VMEM), pl.BlockSpec(memory_space=pl.ANY)
    dma, half_type = pltpu.SemaphoreType.DMA, tokens.dtype
    return pl.pallas_call(
        functools.partial(reduce_kernel, devices_seq, math.gcd(width, 512)),
        out_shape=jax.ShapeDtypeStruct((2, owned, wide), jnp.float32),
        in_specs=[vmem] * 8 + [anywhere] * 2,
        out_specs=vmem,
        scratch_shapes=[pltpu.VMEM(tokens.shape, half_type)] * 2
        + [pltpu.VMEM((devices_seq,) + state.shape, jnp.float32)]
        + [pltpu.VMEM((rows, wide), half_type), pltpu.VMEM((2, width, wide), half_type)]
        + [pltpu.VMEM((2, groups, owned, wide), half_type)] * 3
        + [dma((2,)), dma((devices_seq,)), dma((devices_seq,))]
        + [dma((2, groups))] * 4,
        compiler_params=pltpu.CompilerParams(collective_id=1, has_side_effects=True),
        name="reduce_owned",
    )(state, rate, weight, inner, value, gate, early_in, early_out, tokens, grads)


def correlate_block(signal, residues, decay_length):
    rows, channels = signal.shape
    chunk = min(64, rows)
    chunks = rows // chunk
    per_filter = channels // residues.shape[1]
    rate = jnp.repeat(1.0 / decay_length, per_filter, axis=1)
    weight = jnp.repeat(residues, per_filter, axis=1) * jnp.sqrt(-jnp.expm1(-2.0 * rate))
    offset = jnp.arange(chunk, dtype=jnp.float32)
    exponent = rate.T[:, :, None] * offset
    grow = weight.T[:, :, None] * jnp.exp(exponent)
    fall = jnp.exp(-exponent)
    later = jnp.arange(chunk)[None, :] >= jnp.arange(chunk)[:, None]
    taps = jnp.einsum("cri,crj->cij", grow, fall, precision=precise)
    taps = jnp.where(later, taps, 0.0)
    pieces = signal.reshape(chunks, chunk, channels).transpose(2, 1, 0)
    both = jnp.einsum(
        "cij,cjn->cin", jnp.concatenate([taps, fall], axis=1), pieces, precision=precise
    )
    inner, sums = both[:, :chunk], both[:, chunk:]
    step = jnp.exp(-chunk * rate).T
    state = jnp.zeros_like(step)
    entering = []
    for index in reversed(range(chunks)):
        entering.append(step * state)
        state = sums[:, :, index] + step * state
    entering = jnp.stack(entering[::-1], axis=2)
    outer = jnp.einsum("cri,crn->cin", grow, entering, precision=precise)
    return (inner + outer).transpose(2, 1, 0).reshape(rows, channels), state.T, rate, weight


def block_kernel(
    devices_seq,
    devices_chan,
    tokens_hbm,
    grads_hbm,
    in_weight,
    out_weight,
    conv_hbm,
    residues,
    decay_length,
    grad_in,
    grad_out,
    tokens,
    grads,
    conv,
    pieces,
    crossed,
    weights,
    partial,
    pair_in,
    chip_sum,
    far_in,
    late_sum,
    late_in,
    signal,
    consts,
    bank,
    own_state,
    states,
    flows,
    parts,
    kept,
    near,
    summed,
    blocks,
    arrived,
    results,
    given,
    load_sem,
    sent,
    hop_recv,
    swap_recv,
    keep_sem,
    twin_recv,
    pair_recv,
    far_recv,
    state_recv,
    flow_recv,
    pass_recv,
    near_recv,
    turn_recv,
    home_recv,
    put_sem,
):
    seq, chan = lax.axis_index("seq"), lax.axis_index("chan")
    planes = devices_chan
    twins = devices_seq // planes
    groups = devices_chan // 2
    plane, twin = seq // twins, seq % twins
    group, parity = chan // 2, chan % 2
    partner = (seq, chan + 1 - 2 * parity)
    channels, rows = conv.shape
    owned = out_weight.shape[1]

    def ahead(index, step, count):
        return lax.rem(index + step, count)

    def behind(index, step, count):
        return lax.rem(index - step + count, count)

    sources = (in_weight.at[1], out_weight, in_weight.at[0], in_weight.at[2])
    count = len(sources)
    weight_loads = [
        pltpu.make_async_copy(sources[part], pieces.at[part, plane], load_sem.at[part])
        for part in range(count)
    ]
    bulk_loads = [
        pltpu.make_async_copy(tokens_hbm, tokens, load_sem.at[count]),
        pltpu.make_async_copy(grads_hbm, grads, load_sem.at[count + 1]),
        pltpu.make_async_copy(conv_hbm, conv, load_sem.at[count + 2]),
    ]
    filter_loads = [
        pltpu.make_async_copy(residues, given.at[0], load_sem.at[count + 3]),
        pltpu.make_async_copy(decay_length, given.at[1], load_sem.at[count + 4]),
    ]
    for load in weight_loads + filter_loads + bulk_loads:
        load.start()

    barrier = pltpu.get_barrier_semaphore()
    for step in range(1, devices_seq):
        pl.semaphore_signal(
            barrier, inc=1, device_id=(ahead(seq, step, devices_seq), chan), device_id_type=MESH
        )
    for step in range(1, devices_chan):
        pl.semaphore_signal(
            barrier, inc=1, device_id=(seq, ahead(chan, step, devices_chan)), device_id_type=MESH
        )
    pl.semaphore_wait(barrier, devices_seq + devices_chan - 2)

    bits = [1 << power for power in reversed(range(planes.bit_length() - 1))]

    def flip(index, mask):
        result = index
        for bit in bits:
            if mask & bit:
                result = result + bit - 2 * bit * (index // bit % 2)
        return result

    def hop(part, which, kind, side):
        return remote(
            pieces.at[part, which],
            pieces.at[part, which],
            sent.at[kind],
            hop_recv.at[part, which],
            ((plane + side) * twins + twin, chan),
        )

    def onward(part, which, kind, side):
        edge = planes - 1 if side > 0 else 0

        @pl.when(plane != edge)
        def _():
            hop(part, which, kind, side).start()

    def cross(part, step, mask):
        here = flip(plane, mask)
        return remote(
            pieces.at[part, here],
            crossed.at[part, step, here],
            sent.at[14 + part // early],
            twin_recv.at[part, step - 1, mask],
            (plane * twins + ahead(twin, step, twins), chan),
        )

    def held(part, step, target):
        return crossed.at[part, step, target] if step else pieces.at[part, target]

    def swap(part, step, target):
        return remote(
            held(part, step, target),
            weights.at[part, behind(twin, step, twins), chan],
            sent.at[2 + part // early if step else 1],
            swap_recv.at[part, step],
            (seq, target),
        )

    def swap_in(part, step):
        landed = weights.at[part, behind(twin, step, twins), pl.ds(0, devices_chan - 1)]
        return remote(landed, landed, sent.at[2 + part // early if step else 1], swap_recv.at[part, step], partner)

    def keep(part, step):
        return pltpu.make_async_copy(
            held(part, step, chan),
            weights.at[part, behind(twin, step, twins), chan],
            keep_sem.at[part, step],
        )

    def deliver(part, step, mask):
        target = flip(plane, mask)

        @pl.when(target == chan)
        def _():
            keep(part, step).start()

        @pl.when(target != chan)
        def _():
            swap(part, step, target).start()

    early = count // 2

    crossing = ((0, 1, 3), (3,))

    def crosses(part, mask):
        return mask in crossing[part // early]

    def here(part, mask):
        if crosses(part, mask):
            for step in range(1, twins):
                cross(part, step, mask).start()
        deliver(part, 0, mask)

    def depart(group):
        for part in group:
            for side in (1, -1):
                onward(part, plane, 0, side)

    def arrive(group, distance):
        for part in group:
            for mask in range(1, planes):
                which = flip(plane, mask)
                for side in (1, -1):

                    @pl.when(plane - which == side * distance)
                    def _(mask=mask, which=which, side=side, part=part):
                        hop(part, which, 0, -side).wait_recv()
                        onward(part, which, 16, side)
                        here(part, mask)

    def cross_on(part, mask):
        for step in range(1, twins):
            cross(part, step, mask).wait_recv()
            deliver(part, step, mask)

    def twin_copy(part, step):
        return remote(
            weights.at[part, twin],
            weights.at[part, twin],
            sent.at[4 + part // early],
            twin_recv.at[part, step - 1, 2],
            (plane * twins + ahead(twin, step, twins), chan),
        )

    def twin_in(part, step):
        there = behind(twin, step, twins)
        return remote(
            weights.at[part, there],
            weights.at[part, there],
            sent.at[4 + part // early],
            twin_recv.at[part, step - 1, 2],
            (plane * twins + there, chan),
        )

    def share(part, mask):
        @pl.when(flip(plane, mask) == chan)
        def _():
            swap_in(part, 0).wait_recv()
            keep(part, 0).wait()
            for step in range(1, twins):
                twin_copy(part, step).start()

    def loaded(part):
        weight_loads[part].wait()

    first, last = range(early), range(early, count)
    for part in range(count):
        loaded(part)
    depart(first)
    for part in first:
        here(part, 0)

    lanes = signal.shape[1]
    folds = lanes // channels
    groups_of_rows = 8
    span = signal.shape[0] // groups_of_rows
    modes, filters = residues.shape
    per_filter = channels // filters
    lane = lax.broadcasted_iota(jnp.int32, (filters, lanes), 1)
    which = lax.broadcasted_iota(jnp.int32, (filters, lanes), 0)
    spread = (lax.rem(lane, channels) // per_filter == which).astype(jnp.float32)
    for load in filter_loads:
        load.wait()
    inverse = 1.0 / given[1]
    twice = 2.0 * inverse
    series = jnp.zeros_like(twice)
    for order in range(10, 0, -1):
        series = (1.0 - series) * twice / order
    loss = jnp.where(twice < 0.5, series, 1.0 - jnp.exp(-twice))
    scale = given[0] * jnp.sqrt(loss)

    def widen(array):
        return jnp.dot(array, spread, precision=precise, preferred_element_type=jnp.float32)

    rate = widen(inverse)
    consts[0] = rate
    consts[1] = widen(scale)
    consts[2] = jnp.exp(-rate)

    inputs = (tokens, grads, tokens, tokens)

    def ready(part, step, mask):
        @pl.when(flip(plane, mask) == chan)
        def _():
            if crosses(part, mask):
                swap_in(part, step).wait_recv()
                keep(part, step).wait()
            elif step:
                twin_in(part, step).wait_recv()

    def project(part):
        for step in range(twins):
            block = behind(twin, step, twins)
            for mask in range(planes):
                ready(part, step, mask)
            columns = pl.ds(pl.multiple_of(block * owned, owned), owned)
            product = lax.dot_general(
                weights[part, block].reshape(devices_chan * channels, owned),
                inputs[part][:, columns],
                (((1,), (1,)), ((), ())),
                preferred_element_type=jnp.float32,
            )
            for target in range(devices_chan):
                piece = product[target * channels : (target + 1) * channels]
                place = (part, target % 2, target // 2)
                if step:
                    piece = partial[place] + piece
                partial[place] = piece

    def pair_copy(part, there):
        return remote(
            partial.at[part, 1 - parity, there],
            pair_in.at[part, there],
            sent.at[6],
            pair_recv.at[part, there],
            partner,
        )

    def far_copy(part, step):
        return remote(
            (chip_sum, late_sum)[part // early].at[part % early, step - 1],
            (far_in, late_in)[part // early].at[part % early, step - 1],
            sent.at[7 if part < early else 17],
            far_recv.at[part, step - 1],
            (seq, ahead(group, step, groups) * 2 + parity),
        )

    def pair_start(part):
        for step in range(1, groups + 1):
            pair_copy(part, ahead(group, step, groups)).start()

    def far_start(part):
        for step in range(1, groups):
            there = ahead(group, step, groups)
            pair_copy(part, there).wait_recv()
            total = partial[part, parity, there] + pair_in[part, there]
            if part < early:
                chip_sum[part, step - 1] = total
            else:
                late_sum[part - early, step - 1] = total.astype(late_sum.dtype)
            far_copy(part, step).start()

    def far_finish(part):
        pair_copy(part, group).wait_recv()
        total = partial[part, parity, group] + pair_in[part, group]
        for step in range(1, groups):
            far_copy(part, step).wait_recv()
            arriving = (far_in, late_in)[part // early]
            total = total + arriving[part % early, step - 1].astype(jnp.float32)
        return total

    def flow(part, step):
        return remote(
            flows.at[part, chan],
            flows.at[part, chan],
            sent.at[8],
            flow_recv.at[part, step - 1],
            (seq, ahead(group, step, groups) * 2 + parity),
        )

    def flow_in(part, step):
        source = behind(group, step, groups) * 2 + parity
        return remote(
            flows.at[part, source],
            flows.at[part, source],
            sent.at[8],
            flow_recv.at[part, step - 1],
            (seq, source),
        )

    def flow_pass(part, step):
        source = behind(group, step, groups) * 2 + parity
        return remote(
            flows.at[part, source],
            flows.at[part, source],
            sent.at[9],
            pass_recv.at[part, step],
            partner,
        )

    def flow_passed(part, step):
        source = behind(group, step, groups) * 2 + 1 - parity
        return remote(
            flows.at[part, source],
            flows.at[part, source],
            sent.at[9],
            pass_recv.at[part, step],
            partner,
        )

    def flow_start(part):
        for step in range(1, groups):
            flow(part, step).start()
        flow_pass(part, 0).start()

    def flow_on(part):
        for step in range(1, groups):
            flow_in(part, step).wait_recv()
            flow_pass(part, step).start()

    def flow_finish(part):
        for step in range(groups):
            flow_passed(part, step).wait_recv()

    def near_copy(part, step, target):
        return remote(
            parts.at[part, step - 1, target],
            near.at[part, step - 1, target],
            sent.at[10],
            near_recv.at[part, step - 1, target],
            (plane * twins + ahead(twin, step, twins), chan),
        )

    def multiply(part):
        for step in range(1, twins + 1):
            block = ahead(twin, step, twins)
            columns = pl.ds(pl.multiple_of(block * owned, owned), owned)
            product = jnp.dot(
                flows[part].reshape(devices_chan * channels, rows),
                inputs[part][:, columns],
                preferred_element_type=jnp.float32,
            )
            for target in range(devices_chan):
                piece = product[target * channels : (target + 1) * channels]
                if step < twins:
                    parts[part, step - 1, target] = piece.astype(parts.dtype)
                else:
                    kept[part, target] = piece
            if step < twins:
                for index in range(1, devices_chan + 1):
                    near_copy(part, step, ahead(chan, index, devices_chan)).start()

    def turn(part, target):
        return remote(
            summed.at[part, target],
            blocks.at[part, chan],
            sent.at[11],
            turn_recv.at[part, chan],
            (seq, target),
        )

    def turn_in(part, source):
        return remote(
            summed.at[part, source],
            blocks.at[part, source],
            sent.at[11],
            turn_recv.at[part, source],
            (seq, source),
        )

    straight = (0, 1, 2, 3)

    def home(part, mask):
        return remote(
            blocks.at[part, flip(plane, mask)],
            arrived.at[part, mask],
            sent.at[12],
            home_recv.at[part, mask - 1],
            (flip(plane, mask if part in straight else mask & -mask) * twins + twin, chan),
        )

    def turn_start(part, index):
        target = ahead(chan, index, devices_chan)
        total = kept[part, target]
        for step in range(1, twins):
            near_copy(part, step, target).wait_recv()
            total = total + near[part, step - 1, target].astype(jnp.float32)
        total = total.astype(blocks.dtype)
        if index < devices_chan:
            summed[part, target] = total
            turn(part, target).start()
        else:
            blocks[part, chan] = total

    def turned(part, index):
        source = behind(chan, index, devices_chan)
        if index < devices_chan:
            turn_in(part, source).wait_recv()

        for mask in range(1, planes, 1 if part in straight else 2):

            @pl.when(flip(plane, mask) == source)
            def _(mask=mask):
                home(part, mask).start()

    def gathered(part, mask):
        total = blocks[part, flip(plane, mask)].astype(jnp.float32)
        for other in range(1, planes) if part in straight else reversed(bits):
            if mask == 0 or other < mask & -mask:
                home(part, mask ^ other).wait_recv()
                total = total + arrived[part, mask ^ other].astype(jnp.float32)
        return total

    targets = (grad_in.at[1], grad_out, grad_in.at[0], grad_in.at[2])

    def put(part):
        return pltpu.make_async_copy(results.at[part], targets[part], put_sem.at[part])

    def finish(part):
        results[part] = gathered(part, 0)
        put(part).start()

    def home_on(part):
        for mask in range(planes - 1, 0, -1):
            if mask & -mask > 1 and part not in straight:
                blocks[part, flip(plane, mask)] = gathered(part, mask).astype(blocks.dtype)
                home(part, mask).start()

    def rowed(array):
        width = array.shape[1] // folds
        stacked = jnp.concatenate(
            [array[:, fold * width : (fold + 1) * width] for fold in range(folds)], axis=0
        )
        return stacked.T

    def unrowed(array):
        stacked = array.T
        return jnp.concatenate(
            [stacked[fold * channels : (fold + 1) * channels] for fold in range(folds)], axis=1
        )

    def mode_row(kind, mode):
        return jnp.broadcast_to(consts[kind, mode : mode + 1], (groups_of_rows, lanes))

    def line(index):
        return pl.ds(index, groups_of_rows, stride=span)

    def scan_states():
        fall = [mode_row(2, mode) for mode in range(modes)]

        def body(step, carry):
            here = signal[line(span - 1 - step)]
            return tuple(carry[mode] * fall[mode] + here for mode in range(modes))

        zero = jnp.zeros((groups_of_rows, lanes), jnp.float32)
        found = lax.fori_loop(0, span, body, (zero,) * modes)
        position = lax.broadcasted_iota(jnp.int32, (groups_of_rows, lanes), 0)
        for mode in range(modes):
            each = mode_row(0, mode) * span
            total = found[mode]
            shift = 1
            while shift < groups_of_rows:
                moved = pltpu.roll(total, groups_of_rows - shift, 0)
                moved = moved * jnp.exp(-each * shift)
                total = total + jnp.where(position < groups_of_rows - shift, moved, 0.0)
                shift *= 2
            moved = pltpu.roll(total, groups_of_rows - 1, 0)
            bank[mode] = jnp.where(position < groups_of_rows - 1, moved, 0.0)
            own_state[mode : mode + 1] = total[0:1]
        heads = own_state[...]
        reach = consts[0] * (span * groups_of_rows)
        later = pltpu.roll(heads, channels, 1)
        first = lax.broadcasted_iota(jnp.int32, (modes, lanes), 1) < channels
        consts[3] = jnp.where(first, later, 0.0)
        own_state[...] = jnp.where(first, heads + later * jnp.exp(-reach), 0.0)

    def state_copy(step):
        return remote(
            own_state,
            states.at[step],
            sent.at[13],
            state_recv,
            (ahead(seq, step, devices_seq), chan),
        )

    def scan_source():
        rates = consts[0]
        following = jnp.zeros((modes, lanes), jnp.float32)
        landed = states.at[pl.ds(1, devices_seq - 1)]
        remote(landed, landed, sent.at[13], state_recv, partner).wait_recv()
        for step in range(1, devices_seq):
            gap = behind(seq, step, devices_seq) - seq - 1
            reach = (jnp.maximum(gap, 0) * rows).astype(jnp.float32)
            present = (gap >= 0).astype(jnp.float32)
            following = following + present * states[step] * jnp.exp(-reach * rates)
        first = lax.broadcasted_iota(jnp.int32, (modes, lanes), 1) < channels
        after = pltpu.roll(following, channels, 1)
        within = following * jnp.exp(-(rates * (span * groups_of_rows)))
        consts[3] = jnp.where(first, consts[3] + within, after)
        fall = [mode_row(2, mode) for mode in range(modes)]
        weigh = [mode_row(1, mode) for mode in range(modes)]
        position = lax.broadcasted_iota(jnp.int32, (groups_of_rows, lanes), 0)
        left = ((groups_of_rows - 1 - position) * span).astype(jnp.float32)
        start = tuple(
            bank[mode] + mode_row(3, mode) * jnp.exp(-left * mode_row(0, mode))
            for mode in range(modes)
        )

        def body(step, carry):
            here = line(span - 1 - step)
            entry = signal[here]
            following = tuple(carry[mode] * fall[mode] + entry for mode in range(modes))
            terms = [following[mode] * weigh[mode] for mode in range(modes)]
            while len(terms) > 1:
                terms = [sum(terms[at : at + 2]) for at in range(0, len(terms), 2)]
            signal[here] = terms[0]
            return following

        lax.fori_loop(0, span, body, start)

    def settle(group, mask):
        for part in group:
            if crosses(part, mask):
                cross_on(part, mask)
            else:
                share(part, mask)

    arrive(first, 1)
    settle(first, 0)
    arrive(first, 2)
    depart(last)
    for part in last:
        here(part, 0)
    settle(first, 1)
    arrive(first, 3)
    settle(first, 2)
    arrive(last, 1)
    settle(last, 0)
    settle(first, 3)
    arrive(last, 2)
    settle(last, 1)
    for load in bulk_loads:
        load.wait()
    project(0)
    pair_start(0)
    project(1)
    pair_start(1)
    arrive(last, 3)
    settle(last, 2)
    far_start(0)
    far_start(1)
    taken = conv[...].astype(jnp.float32)
    second = far_finish(0).astype(flows.dtype).astype(jnp.float32)
    flows[1, chan] = (second * taken).astype(flows.dtype)
    flow_start(1)
    settle(last, 3)
    upstream = far_finish(1)
    flows[0, chan] = (upstream * taken).astype(flows.dtype)
    flow_start(0)
    signal[...] = rowed(upstream * second)
    flow_on(1)
    scan_states()
    for step in range(1, devices_seq):
        state_copy(step).start()
    project(2)
    pair_start(2)
    flow_finish(1)
    multiply(1)
    project(3)
    pair_start(3)
    far_start(2)
    far_start(3)
    flow_on(0)
    flow_finish(0)
    multiply(0)
    turn_start(1, 1)
    scan_source()
    source = unrowed(signal[...])
    turn_start(1, 2)
    late = far_finish(2).astype(flows.dtype).astype(jnp.float32)
    flows[3, chan] = (source * late).astype(flows.dtype)
    flow_start(3)
    late = far_finish(3).astype(flows.dtype).astype(jnp.float32)
    flows[2, chan] = (source * late).astype(flows.dtype)
    flow_start(2)
    turn_start(1, 3)
    turned(1, 1)
    turn_start(1, 4)
    turned(1, 2)
    flow_on(3)
    turn_start(0, 1)
    flow_on(2)
    turn_start(0, 2)
    flow_finish(3)
    turned(1, 3)
    multiply(3)
    flow_finish(2)
    multiply(2)
    turned(1, 4)
    turn_start(0, 3)
    turned(0, 1)
    turn_start(0, 4)
    turned(0, 2)
    turned(0, 3)
    turned(0, 4)
    turn_start(3, 1)
    turn_start(3, 2)
    turn_start(3, 4)
    turn_start(3, 3)
    turned(3, 1)
    turned(3, 2)
    turn_start(2, 1)
    turned(3, 3)
    turn_start(2, 2)
    turned(3, 4)
    turn_start(2, 3)
    turned(2, 1)
    turn_start(2, 4)
    turned(2, 2)
    turned(2, 3)
    turned(2, 4)
    finish(1)
    finish(0)
    finish(3)
    finish(2)
    for part in range(count):
        put(part).wait()

    def left(kind, ref):
        remote(ref, ref, sent.at[kind], state_recv, partner).wait_send()

    fewer = pl.ds(0, planes - 1)
    others = pl.ds(1, twins - 1)
    inner = jnp.logical_and(plane > 0, plane < planes - 1)

    @pl.when(inner)
    def _():
        left(0, pieces.at[:, pl.ds(0, 2)])
        left(16, pieces.at[:, fewer])

    @pl.when(jnp.logical_not(inner))
    def _():
        left(0, pieces.at[:, pl.ds(0, 1)])

    left(1, pieces.at[:, fewer])
    for group in range(2):
        span_of = pl.ds(group * early, early)
        masks = crossing[group]
        if masks:
            left(14 + group, crossed.at[span_of, others, pl.ds(0, len(masks))])
        for mask in range(planes):

            @pl.when(flip(plane, mask) == chan)
            def _(mask=mask):
                swaps = len(masks) - (mask in masks)
                if swaps:
                    left(2 + group, crossed.at[span_of, others, pl.ds(0, swaps)])
                if mask not in masks:
                    left(4 + group, weights.at[span_of, others])

    left(6, partial.at[:, 0])
    left(7, chip_sum)
    left(17, late_sum)
    left(8, flows.at[:, pl.ds(0, groups - 1)])
    left(9, flows.at[:, pl.ds(0, groups)])
    left(10, parts)
    left(11, summed.at[:, fewer])
    left(12, blocks.at[:, fewer])
    left(13, states.at[pl.ds(1, devices_seq - 1)])


def place_kernel(grad_in, grad_proj, out_in, out_proj, held, take_sem, give_sem):
    streams = grad_in.shape[0]
    ends = [(grad_in.at[at], out_in.at[at]) for at in range(streams)] + [(grad_proj, out_proj)]
    takes = [
        pltpu.make_async_copy(source, held.at[at], take_sem.at[at])
        for at, (source, _) in enumerate(ends)
    ]
    gives = [
        pltpu.make_async_copy(held.at[at], target, give_sem.at[at])
        for at, (_, target) in enumerate(ends)
    ]
    for take in takes:
        take.start()
    for take, give in zip(takes, gives):
        take.wait()
        give.start()
    for give in gives:
        give.wait()


def placed(grad_in, grad_proj):
    anywhere, dma = pl.BlockSpec(memory_space=pl.ANY), pltpu.SemaphoreType.DMA
    count = grad_in.shape[0] + 1
    return pl.pallas_call(
        place_kernel,
        out_shape=tuple(jax.ShapeDtypeStruct(a.shape, a.dtype) for a in (grad_in, grad_proj)),
        in_specs=[anywhere] * 2,
        out_specs=(anywhere, anywhere),
        scratch_shapes=[
            pltpu.VMEM((count,) + grad_proj.shape, grad_proj.dtype),
            dma((count,)),
            dma((count,)),
        ],
        name="place_outputs",
    )(grad_in, grad_proj)


def fits(tokens, conv_out, in_weight, residues):
    devices_seq, devices_chan = lax.axis_size("seq"), lax.axis_size("chan")
    rows, channels = conv_out.shape
    return (
        devices_chan == 4
        and devices_seq % devices_chan == 0
        and devices_seq > devices_chan
        and in_weight.shape[0] % 128 == 0
        and 2 * channels == 128
        and channels % residues.shape[1] == 0
        and rows % 256 == 0
        and tokens.shape[1] * devices_chan == in_weight.shape[0] * devices_seq
    )


def blocked(tokens, grad_out, in_weight, out_weight, conv_out, residues, decay_length):
    devices_seq, devices_chan = lax.axis_size("seq"), lax.axis_size("chan")
    planes, groups = devices_chan, devices_chan // 2
    twins = devices_seq // planes
    rows, width = tokens.shape
    channels, owned = out_weight.shape[1], out_weight.shape[0]
    modes = residues.shape[0]
    anywhere = pl.BlockSpec(memory_space=pl.ANY)
    dma, half_type, full = pltpu.SemaphoreType.DMA, tokens.dtype, jnp.float32
    lanes = 2 * channels
    grad_in, grad_proj = pl.pallas_call(
        functools.partial(block_kernel, devices_seq, devices_chan),
        out_shape=(
            jax.ShapeDtypeStruct((3, channels, owned), full),
            jax.ShapeDtypeStruct((channels, owned), full),
        ),
        in_specs=[anywhere] * 7,
        out_specs=(anywhere, anywhere),
        scratch_shapes=[
            pltpu.VMEM((rows, width), half_type),
            pltpu.VMEM((rows, width), half_type),
            pltpu.VMEM((channels, rows), half_type),
            pltpu.VMEM((4, planes, channels, owned), half_type),
            pltpu.VMEM((4, twins, planes, channels, owned), half_type),
            pltpu.VMEM((4, twins, devices_chan, channels, owned), half_type),
            pltpu.VMEM((4, 2, groups, channels, rows), full),
            pltpu.VMEM((4, groups, channels, rows), full),
            pltpu.VMEM((2, groups - 1, channels, rows), full),
            pltpu.VMEM((2, groups - 1, channels, rows), full),
            pltpu.VMEM((2, groups - 1, channels, rows), half_type),
            pltpu.VMEM((2, groups - 1, channels, rows), half_type),
            pltpu.VMEM((rows * channels // lanes, lanes), full),
            pltpu.VMEM((4, modes, lanes), full),
            pltpu.VMEM((modes, 8, lanes), full),
            pltpu.VMEM((modes, lanes), full),
            pltpu.VMEM((devices_seq, modes, lanes), full),
            pltpu.VMEM((4, devices_chan, channels, rows), half_type),
            pltpu.VMEM((4, twins - 1, devices_chan, channels, owned), half_type),
            pltpu.VMEM((4, devices_chan, channels, owned), full),
            pltpu.VMEM((4, twins - 1, devices_chan, channels, owned), half_type),
            pltpu.VMEM((4, devices_chan, channels, owned), half_type),
            pltpu.VMEM((4, planes, channels, owned), half_type),
            pltpu.VMEM((4, planes, channels, owned), half_type),
            pltpu.VMEM((4, channels, owned), full),
            pltpu.VMEM((2,) + residues.shape, full),
            dma((9,)),
            dma((18,)),
            dma((4, planes)),
            dma((4, twins)),
            dma((4, twins)),
            dma((4, twins - 1, planes)),
        ]
        + [dma((4, groups)), dma((4, groups - 1)), dma, dma((4, groups - 1)), dma((4, groups))]
        + [dma((4, twins - 1, planes))]
        + [dma((4, planes)), dma((4, planes - 1)), dma((4,))],
        compiler_params=pltpu.CompilerParams(collective_id=2, has_side_effects=True),
        name="conv_block",
    )(
        tokens,
        grad_out,
        in_weight.transpose(1, 2, 0),
        out_weight.T,
        conv_out.T,
        residues,
        decay_length,
    )
    grad_in, grad_proj = placed(grad_in, grad_proj)
    return grad_in.transpose(2, 0, 1), grad_proj.T


def local(tokens, grad_out, in_weight, out_weight, conv_out, residues, decay_length):
    if fits(tokens, conv_out, in_weight, residues):
        return blocked(tokens, grad_out, in_weight, out_weight, conv_out, residues, decay_length)
    channels = out_weight.shape[1]
    owned_rows = in_weight.shape[0]
    weights = jnp.concatenate([in_weight.reshape(owned_rows, 3 * channels), out_weight], axis=1)
    full_tokens, full_grads, projected, upstream = gathered(tokens, grad_out, weights)
    projected = projected[:, : 3 * channels]
    upstream = upstream[:, channels:]
    streams = lax.reduce_precision(projected, exponent_bits=8, mantissa_bits=7)
    gate_first = streams[:, :channels]
    gate_second = streams[:, channels : 2 * channels]
    value_stream = streams[:, 2 * channels :]
    conv_value = conv_out.astype(jnp.float32)
    gated = (gate_second * conv_value).astype(jnp.bfloat16)
    grad_second = (upstream * conv_value).astype(jnp.bfloat16)
    grad_conv = upstream * gate_second
    inner, state, rate, weight = correlate_block(grad_conv, residues, decay_length)
    blank = jnp.zeros_like(gated)
    owned = reduced(
        state,
        rate,
        weight,
        inner,
        value_stream,
        gate_first,
        jnp.concatenate([grad_second, blank], axis=1),
        jnp.concatenate([blank, gated], axis=1),
        full_tokens,
        full_grads,
        owned_rows,
    )
    grad_in = jnp.stack(
        [owned[1, :, :channels], owned[0, :, :channels], owned[1, :, channels:]], axis=1
    )
    return (grad_in, owned[0, :, channels:])


def solution(mesh):
    return jax.shard_map(
        local,
        mesh=mesh,
        in_specs=(
            P("seq", "chan"),
            P("seq", "chan"),
            P("seq", None, "chan"),
            P("seq", "chan"),
            P("seq", "chan"),
            P(None, "chan"),
            P(None, "chan"),
        ),
        out_specs=(P("seq", None, "chan"), P("seq", "chan")),
        check_vma=False,
    )
```

```python
import functools
import math

import jax
import jax.numpy as jnp
from jax import lax
from jax.experimental import pallas as pl
from jax.experimental.pallas import tpu as pltpu
from jax.sharding import PartitionSpec as P

precise = lax.Precision.HIGHEST
MESH = pl.DeviceIdType.MESH


def remote(source, target, send_sem, recv_sem, device):
    return pltpu.make_async_remote_copy(
        src_ref=source,
        dst_ref=target,
        send_sem=send_sem,
        recv_sem=recv_sem,
        device_id=device,
        device_id_type=MESH,
    )


def greet(devices_seq, devices_chan, seq_wide):
    seq, chan = lax.axis_index("seq"), lax.axis_index("chan")
    barrier = pltpu.get_barrier_semaphore()
    count = 0
    if seq_wide == "all":

        def hello(step, carry):
            pl.semaphore_signal(
                barrier,
                inc=1,
                device_id=(lax.rem(seq + step, devices_seq), chan),
                device_id_type=MESH,
            )
            return carry

        lax.fori_loop(1, devices_seq, hello, 0)
        count += devices_seq - 1
    else:
        groups = devices_seq // 2

        def hello_group(step, carry):
            there = lax.rem(seq // 2 + step, groups) * 2 + seq % 2
            pl.semaphore_signal(barrier, inc=1, device_id=(there, chan), device_id_type=MESH)
            return carry

        lax.fori_loop(1, groups, hello_group, 0)
        pl.semaphore_signal(
            barrier, inc=1, device_id=(seq + 1 - 2 * (seq % 2), chan), device_id_type=MESH
        )
        count += groups
    if devices_chan:
        groups = devices_chan // 2
        for step in range(1, groups):
            there = lax.rem(chan // 2 + step, groups) * 2 + chan % 2
            pl.semaphore_signal(barrier, inc=1, device_id=(seq, there), device_id_type=MESH)
        pl.semaphore_signal(
            barrier, inc=1, device_id=(seq, chan + 1 - 2 * (chan % 2)), device_id_type=MESH
        )
        count += groups
    pl.semaphore_wait(barrier, count)


def gather_kernel(
    devices_seq,
    devices_chan,
    tokens,
    grads,
    weights,
    tokens_out,
    grads_out,
    projected,
    upstream,
    all_tokens,
    all_grads,
    all_weights,
    keep_sem,
    store_sem,
    chan_send,
    chan_recv,
    chan_pass,
    chan_passed,
    seq_send,
    seq_recv,
    seq_pass,
    seq_passed,
):
    seq, chan = lax.axis_index("seq"), lax.axis_index("chan")
    seq_groups, chan_groups = devices_seq // 2, devices_chan // 2
    seq_pair = (seq + 1 - 2 * (seq % 2), chan)
    chan_pair = (seq, chan + 1 - 2 * (chan % 2))
    columns = tokens.shape[1]
    rows = weights.shape[0]
    greet(devices_seq, devices_chan, "pairs")

    def block(ref, lines, index):
        return ref.at[lines, pl.ds(pl.multiple_of(index * columns, columns), columns)]

    def piece(index):
        return all_weights.at[pl.ds(pl.multiple_of(index * rows, rows), rows)]

    def chan_member(step, parity):
        return lax.rem(chan // 2 - step + chan_groups, chan_groups) * 2 + parity

    def seq_member(step, parity):
        return lax.rem(seq // 2 - step + seq_groups, seq_groups) * 2 + parity

    height = tokens.shape[0] // 2
    parts = [
        (own, whole, out, pl.ds(half * height, height))
        for own, whole, out in ((tokens, all_tokens, tokens_out), (grads, all_grads, grads_out))
        for half in range(2)
    ]

    def chan_copy(array, step):
        own, whole, _, lines = parts[array]
        there = lax.rem(chan // 2 + step, chan_groups) * 2 + chan % 2
        return remote(
            own.at[lines],
            block(whole, lines, chan),
            chan_send.at[array, step],
            chan_recv.at[array, step],
            (seq, there),
        )

    def chan_forward(array, step):
        own, whole, _, lines = parts[array]
        here = chan_member(step, chan % 2)
        return remote(
            own.at[lines] if step == 0 else block(whole, lines, here),
            block(whole, lines, here),
            chan_pass.at[array, step],
            chan_passed.at[array, step],
            chan_pair,
        )

    def seq_copy(step):
        there = lax.rem(seq // 2 + step, seq_groups) * 2 + seq % 2
        return remote(weights, piece(seq), seq_send.at[step], seq_recv.at[step], (there, chan))

    def seq_forward(step):
        here = seq_member(step, seq % 2)
        return remote(piece(here), piece(here), seq_pass.at[step], seq_passed.at[step], seq_pair)

    own_piece = remote(weights, piece(seq), seq_pass.at[0], seq_passed.at[0], seq_pair)

    def each(call):
        def body(step, carry):
            call(step)
            return carry

        lax.fori_loop(1, seq_groups, body, 0)

    def store(array):
        _, whole, out, lines = parts[array]
        return pltpu.make_async_copy(whole.at[lines], out.at[lines], store_sem.at[array])

    for array in range(4):
        for step in range(1, chan_groups):
            chan_copy(array, step).start()
    each(lambda step: seq_copy(step).start())
    own_piece.start()
    for array in range(4):
        chan_forward(array, 0).start()
    keeps = [pltpu.make_async_copy(weights, piece(seq), keep_sem.at[4])]
    for array, (own, whole, _, lines) in enumerate(parts):
        keeps.append(
            pltpu.make_async_copy(own.at[lines], block(whole, lines, chan), keep_sem.at[array])
        )
    for keep in keeps:
        keep.start()

    def pass_on(step):
        seq_copy(step).wait_recv()
        seq_forward(step).start()

    def pass_part(array):
        for step in range(1, chan_groups):
            chan_copy(array, step).wait_recv()
            chan_forward(array, step).start()

    pass_part(0)
    each(pass_on)
    for keep in keeps:
        keep.wait()
    own_piece.wait()

    def finish(step):
        seq_copy(step).wait_send()
        seq_forward(step).wait()

    each(finish)
    tile = math.gcd(height, 128)
    for array, (_, whole, _, lines) in enumerate(parts):
        if array + 1 < len(parts):
            pass_part(array + 1)
        for step in range(chan_groups):
            chan_forward(array, step).wait()
        store(array).start()
        target, first = (projected, 0) if array < 2 else (upstream, all_weights.shape[1] // 2)

        def product(index, carry):
            here = pl.ds(pl.multiple_of(array % 2 * height + index * tile, tile), tile)
            target[here] = jnp.dot(
                whole[here], all_weights[:, first:], preferred_element_type=jnp.float32
            )
            return carry

        lax.fori_loop(0, height // tile, product, 0)
    for array in range(4):
        store(array).wait()
        for step in range(1, chan_groups):
            chan_copy(array, step).wait_send()


def gathered(tokens, grads, weights):
    devices_seq, devices_chan = lax.axis_size("seq"), lax.axis_size("chan")
    dma = pltpu.SemaphoreType.DMA
    seq_groups, chan_groups = devices_seq // 2, devices_chan // 2
    vmem, anywhere = pl.BlockSpec(memory_space=pltpu.VMEM), pl.BlockSpec(memory_space=pl.ANY)
    wide = jax.ShapeDtypeStruct((tokens.shape[0], tokens.shape[1] * devices_chan), tokens.dtype)
    tall = jax.ShapeDtypeStruct((weights.shape[0] * devices_seq, weights.shape[1]), weights.dtype)
    return pl.pallas_call(
        functools.partial(gather_kernel, devices_seq, devices_chan),
        out_shape=(
            wide,
            wide,
            jax.ShapeDtypeStruct((tokens.shape[0], weights.shape[1]), jnp.float32),
            jax.ShapeDtypeStruct((tokens.shape[0], weights.shape[1] // 2), jnp.float32),
        ),
        in_specs=[vmem] * 3,
        out_specs=(anywhere, anywhere, vmem, vmem),
        scratch_shapes=[
            pltpu.VMEM(wide.shape, wide.dtype),
            pltpu.VMEM(wide.shape, wide.dtype),
            pltpu.VMEM(tall.shape, tall.dtype),
            dma((5,)),
            dma((4,)),
        ]
        + [dma((4, chan_groups))] * 4
        + [dma((seq_groups,))] * 4,
        compiler_params=pltpu.CompilerParams(collective_id=0, has_side_effects=True),
        name="gather_inputs",
    )(tokens, grads, weights)


def reduce_kernel(
    devices_seq,
    tile,
    state,
    rate,
    weight,
    inner,
    value,
    gate,
    early_in,
    early_out,
    tokens_hbm,
    grads_hbm,
    total,
    tokens,
    grads,
    states,
    late,
    parts,
    near,
    paired,
    far,
    load_sem,
    state_send,
    state_recv,
    pair_send,
    pair_recv,
    far_send,
    far_recv,
):
    seq, chan = lax.axis_index("seq"), lax.axis_index("chan")
    groups = devices_seq // 2
    group, parity = seq // 2, seq % 2
    rows, channels = inner.shape
    owned = near.shape[2]
    loads = [
        pltpu.make_async_copy(tokens_hbm, tokens, load_sem.at[0]),
        pltpu.make_async_copy(grads_hbm, grads, load_sem.at[1]),
    ]
    for load in loads:
        load.start()
    greet(devices_seq, 0, "all")

    def loop(start, stop, call):
        def body(step, carry):
            call(step)
            return carry

        lax.fori_loop(start, stop, body, 0)

    def state_copy(step):
        there = lax.rem(seq + step, devices_seq)
        return remote(
            state, states.at[step], state_send.at[step], state_recv.at[step], (there, chan)
        )

    def member(step):
        return lax.rem(group + step, groups)

    def piece(half, index):
        return parts.at[half, pl.ds(pl.multiple_of(index * owned, owned), owned)]

    def pair_copy(half, step):
        return remote(
            piece(half, member(step) * 2 + 1 - parity),
            near.at[half, step],
            pair_send.at[half, step],
            pair_recv.at[half, step],
            (group * 2 + 1 - parity, chan),
        )

    def far_copy(half, step):
        return remote(
            paired.at[half, step],
            far.at[half, step],
            far_send.at[half, step],
            far_recv.at[half, step],
            (member(step) * 2 + parity, chan),
        )

    def summed(left, right):
        return lax.dot_general(
            left, right, (((0,), (0,)), ((), ())), preferred_element_type=jnp.float32
        )

    def span(index):
        return pl.ds(pl.multiple_of(index * tile, tile), tile)

    loop(1, devices_seq, lambda step: state_copy(step).start())
    for load in loads:
        load.wait()

    def early_tile(index):
        product = summed(tokens[:, span(index)], early_in[...])
        product += summed(grads[:, span(index)], early_out[...])
        parts[0, span(index)] = product.astype(parts.dtype)

    loop(0, tokens.shape[1] // tile, early_tile)
    loop(1, groups, lambda step: pair_copy(0, step).start())
    pair_copy(0, 0).start()

    def absorb(step, following):
        state_copy(step).wait_recv()
        gap = lax.rem(seq - step + devices_seq, devices_seq) - seq - 1
        reach = (jnp.maximum(gap, 0) * rows).astype(jnp.float32)
        present = (gap >= 0).astype(jnp.float32)
        return following + present * states[step] * jnp.exp(-reach * rate[...])

    following = lax.fori_loop(1, devices_seq, absorb, jnp.zeros(rate.shape, jnp.float32))
    entering = weight[...] * following
    rates = rate[...]
    band = math.gcd(rows, 64)

    def source_rows(index):
        here = pl.ds(pl.multiple_of(index * band, band), band)
        position = lax.broadcasted_iota(jnp.int32, (band, channels), 0) + index * band
        reach = (rows - position).astype(jnp.float32)
        source = inner[here]
        for mode in range(rates.shape[0]):
            source += entering[mode : mode + 1] * jnp.exp(-reach * rates[mode : mode + 1])
        late[here] = jnp.concatenate([source * value[here], source * gate[here]], axis=1).astype(
            late.dtype
        )

    loop(0, rows // band, source_rows)

    def late_tile(index):
        parts[1, span(index)] = summed(tokens[:, span(index)], late[...]).astype(parts.dtype)

    loop(0, tokens.shape[1] // tile, late_tile)
    loop(1, groups, lambda step: pair_copy(1, step).start())
    pair_copy(1, 0).start()

    def pair_sum(half, step):
        own = piece(half, member(step) * 2 + parity)[...].astype(jnp.float32)
        return own + near[half, step].astype(jnp.float32)

    for half in range(2):

        def pass_on(step):
            pair_copy(half, step).wait_recv()
            paired[half, step] = pair_sum(half, step).astype(paired.dtype)
            far_copy(half, step).start()

        loop(1, groups, pass_on)
    for half in range(2):
        pair_copy(half, 0).wait_recv()
        total[half] = pair_sum(half, 0)

        def collect(step):
            far_copy(half, step).wait_recv()
            total[half] += far[half, step].astype(jnp.float32)

        loop(1, groups, collect)

        def finish(step):
            pair_copy(half, step).wait_send()
            far_copy(half, step).wait_send()

        loop(1, groups, finish)
        pair_copy(half, 0).wait_send()
    loop(1, devices_seq, lambda step: state_copy(step).wait_send())


def reduced(state, rate, weight, inner, value, gate, early_in, early_out, tokens, grads, owned):
    devices_seq = lax.axis_size("seq")
    groups = devices_seq // 2
    rows, channels = inner.shape
    width = tokens.shape[1]
    wide = 2 * channels
    vmem, anywhere = pl.BlockSpec(memory_space=pltpu.VMEM), pl.BlockSpec(memory_space=pl.ANY)
    dma, half_type = pltpu.SemaphoreType.DMA, tokens.dtype
    return pl.pallas_call(
        functools.partial(reduce_kernel, devices_seq, math.gcd(width, 512)),
        out_shape=jax.ShapeDtypeStruct((2, owned, wide), jnp.float32),
        in_specs=[vmem] * 8 + [anywhere] * 2,
        out_specs=vmem,
        scratch_shapes=[pltpu.VMEM(tokens.shape, half_type)] * 2
        + [pltpu.VMEM((devices_seq,) + state.shape, jnp.float32)]
        + [pltpu.VMEM((rows, wide), half_type), pltpu.VMEM((2, width, wide), half_type)]
        + [pltpu.VMEM((2, groups, owned, wide), half_type)] * 3
        + [dma((2,)), dma((devices_seq,)), dma((devices_seq,))]
        + [dma((2, groups))] * 4,
        compiler_params=pltpu.CompilerParams(collective_id=1, has_side_effects=True),
        name="reduce_owned",
    )(state, rate, weight, inner, value, gate, early_in, early_out, tokens, grads)


def correlate_block(signal, residues, decay_length):
    rows, channels = signal.shape
    chunk = min(64, rows)
    chunks = rows // chunk
    per_filter = channels // residues.shape[1]
    rate = jnp.repeat(1.0 / decay_length, per_filter, axis=1)
    weight = jnp.repeat(residues, per_filter, axis=1) * jnp.sqrt(-jnp.expm1(-2.0 * rate))
    offset = jnp.arange(chunk, dtype=jnp.float32)
    exponent = rate.T[:, :, None] * offset
    grow = weight.T[:, :, None] * jnp.exp(exponent)
    fall = jnp.exp(-exponent)
    later = jnp.arange(chunk)[None, :] >= jnp.arange(chunk)[:, None]
    taps = jnp.einsum("cri,crj->cij", grow, fall, precision=precise)
    taps = jnp.where(later, taps, 0.0)
    pieces = signal.reshape(chunks, chunk, channels).transpose(2, 1, 0)
    both = jnp.einsum(
        "cij,cjn->cin", jnp.concatenate([taps, fall], axis=1), pieces, precision=precise
    )
    inner, sums = both[:, :chunk], both[:, chunk:]
    step = jnp.exp(-chunk * rate).T
    state = jnp.zeros_like(step)
    entering = []
    for index in reversed(range(chunks)):
        entering.append(step * state)
        state = sums[:, :, index] + step * state
    entering = jnp.stack(entering[::-1], axis=2)
    outer = jnp.einsum("cri,crn->cin", grow, entering, precision=precise)
    return (inner + outer).transpose(2, 1, 0).reshape(rows, channels), state.T, rate, weight


def block_kernel(
    devices_seq,
    devices_chan,
    tokens_hbm,
    grads_hbm,
    in_weight,
    out_weight,
    conv_hbm,
    residues,
    decay_length,
    grad_in,
    grad_out,
    tokens,
    grads,
    conv,
    pieces,
    crossed,
    weights,
    partial,
    pair_in,
    chip_sum,
    far_in,
    late_sum,
    late_in,
    signal,
    consts,
    bank,
    own_state,
    states,
    flows,
    parts,
    kept,
    near,
    summed,
    blocks,
    arrived,
    results,
    given,
    load_sem,
    sent,
    hop_recv,
    swap_recv,
    keep_sem,
    twin_recv,
    pair_recv,
    far_recv,
    state_recv,
    flow_recv,
    pass_recv,
    near_recv,
    turn_recv,
    home_recv,
    put_sem,
):
    seq, chan = lax.axis_index("seq"), lax.axis_index("chan")
    planes = devices_chan
    twins = devices_seq // planes
    groups = devices_chan // 2
    plane, twin = seq // twins, seq % twins
    group, parity = chan // 2, chan % 2
    partner = (seq, chan + 1 - 2 * parity)
    channels, rows = conv.shape
    owned = out_weight.shape[1]

    def ahead(index, step, count):
        return lax.rem(index + step, count)

    def behind(index, step, count):
        return lax.rem(index - step + count, count)

    sources = (in_weight.at[1], out_weight, in_weight.at[0], in_weight.at[2])
    count = len(sources)
    weight_loads = [
        pltpu.make_async_copy(sources[part], pieces.at[part, plane], load_sem.at[part])
        for part in range(count)
    ]
    bulk_loads = [
        pltpu.make_async_copy(tokens_hbm, tokens, load_sem.at[count]),
        pltpu.make_async_copy(grads_hbm, grads, load_sem.at[count + 1]),
        pltpu.make_async_copy(conv_hbm, conv, load_sem.at[count + 2]),
    ]
    filter_loads = [
        pltpu.make_async_copy(residues, given.at[0], load_sem.at[count + 3]),
        pltpu.make_async_copy(decay_length, given.at[1], load_sem.at[count + 4]),
    ]
    for load in weight_loads + filter_loads + bulk_loads:
        load.start()

    barrier = pltpu.get_barrier_semaphore()
    for step in range(1, devices_seq):
        pl.semaphore_signal(
            barrier, inc=1, device_id=(ahead(seq, step, devices_seq), chan), device_id_type=MESH
        )
    for step in range(1, devices_chan):
        pl.semaphore_signal(
            barrier, inc=1, device_id=(seq, ahead(chan, step, devices_chan)), device_id_type=MESH
        )
    pl.semaphore_wait(barrier, devices_seq + devices_chan - 2)

    bits = [1 << power for power in reversed(range(planes.bit_length() - 1))]

    def flip(index, mask):
        result = index
        for bit in bits:
            if mask & bit:
                result = result + bit - 2 * bit * (index // bit % 2)
        return result

    def hop(part, which, kind, side):
        return remote(
            pieces.at[part, which],
            pieces.at[part, which],
            sent.at[kind],
            hop_recv.at[part, which],
            ((plane + side) * twins + twin, chan),
        )

    def onward(part, which, kind, side):
        edge = planes - 1 if side > 0 else 0

        @pl.when(plane != edge)
        def _():
            hop(part, which, kind, side).start()

    def cross(part, step, mask):
        here = flip(plane, mask)
        return remote(
            pieces.at[part, here],
            crossed.at[part, step, here],
            sent.at[14 + part // early],
            twin_recv.at[part, step - 1, mask],
            (plane * twins + ahead(twin, step, twins), chan),
        )

    def held(part, step, target):
        return crossed.at[part, step, target] if step else pieces.at[part, target]

    def swap(part, step, target):
        return remote(
            held(part, step, target),
            weights.at[part, behind(twin, step, twins), chan],
            sent.at[2 + part // early if step else 1],
            swap_recv.at[part, step],
            (seq, target),
        )

    def swap_in(part, step):
        landed = weights.at[part, behind(twin, step, twins), pl.ds(0, devices_chan - 1)]
        return remote(landed, landed, sent.at[2 + part // early if step else 1], swap_recv.at[part, step], partner)

    def keep(part, step):
        return pltpu.make_async_copy(
            held(part, step, chan),
            weights.at[part, behind(twin, step, twins), chan],
            keep_sem.at[part, step],
        )

    def deliver(part, step, mask):
        target = flip(plane, mask)

        @pl.when(target == chan)
        def _():
            keep(part, step).start()

        @pl.when(target != chan)
        def _():
            swap(part, step, target).start()

    early = count // 2

    crossing = ((0, 1, 3), (3,))

    def crosses(part, mask):
        return mask in crossing[part // early]

    def here(part, mask):
        if crosses(part, mask):
            for step in range(1, twins):
                cross(part, step, mask).start()
        deliver(part, 0, mask)

    def depart(group):
        for part in group:
            for side in (1, -1):
                onward(part, plane, 0, side)

    def arrive(group, distance):
        for part in group:
            for mask in range(1, planes):
                which = flip(plane, mask)
                for side in (1, -1):

                    @pl.when(plane - which == side * distance)
                    def _(mask=mask, which=which, side=side, part=part):
                        hop(part, which, 0, -side).wait_recv()
                        onward(part, which, 16, side)
                        here(part, mask)

    def cross_on(part, mask):
        for step in range(1, twins):
            cross(part, step, mask).wait_recv()
            deliver(part, step, mask)

    def twin_copy(part, step):
        return remote(
            weights.at[part, twin],
            weights.at[part, twin],
            sent.at[4 + part // early],
            twin_recv.at[part, step - 1, 2],
            (plane * twins + ahead(twin, step, twins), chan),
        )

    def twin_in(part, step):
        there = behind(twin, step, twins)
        return remote(
            weights.at[part, there],
            weights.at[part, there],
            sent.at[4 + part // early],
            twin_recv.at[part, step - 1, 2],
            (plane * twins + there, chan),
        )

    def share(part, mask):
        @pl.when(flip(plane, mask) == chan)
        def _():
            swap_in(part, 0).wait_recv()
            keep(part, 0).wait()
            for step in range(1, twins):
                twin_copy(part, step).start()

    def loaded(part):
        weight_loads[part].wait()

    first, last = range(early), range(early, count)
    for part in range(count):
        loaded(part)
    depart(first)
    for part in first:
        here(part, 0)

    lanes = signal.shape[1]
    folds = lanes // channels
    groups_of_rows = 8
    span = signal.shape[0] // groups_of_rows
    modes, filters = residues.shape
    per_filter = channels // filters
    lane = lax.broadcasted_iota(jnp.int32, (filters, lanes), 1)
    which = lax.broadcasted_iota(jnp.int32, (filters, lanes), 0)
    spread = (lax.rem(lane, channels) // per_filter == which).astype(jnp.float32)
    for load in filter_loads:
        load.wait()
    inverse = 1.0 / given[1]
    twice = 2.0 * inverse
    series = jnp.zeros_like(twice)
    for order in range(10, 0, -1):
        series = (1.0 - series) * twice / order
    loss = jnp.where(twice < 0.5, series, 1.0 - jnp.exp(-twice))
    scale = given[0] * jnp.sqrt(loss)

    def widen(array):
        return jnp.dot(array, spread, precision=precise, preferred_element_type=jnp.float32)

    rate = widen(inverse)
    consts[0] = rate
    consts[1] = widen(scale)
    consts[2] = jnp.exp(-rate)

    inputs = (tokens, grads, tokens, tokens)

    def ready(part, step, mask):
        @pl.when(flip(plane, mask) == chan)
        def _():
            if crosses(part, mask):
                swap_in(part, step).wait_recv()
                keep(part, step).wait()
            elif step:
                twin_in(part, step).wait_recv()

    def project(part):
        for step in range(twins):
            block = behind(twin, step, twins)
            for mask in range(planes):
                ready(part, step, mask)
            columns = pl.ds(pl.multiple_of(block * owned, owned), owned)
            product = lax.dot_general(
                weights[part, block].reshape(devices_chan * channels, owned),
                inputs[part][:, columns],
                (((1,), (1,)), ((), ())),
                preferred_element_type=jnp.float32,
            )
            for target in range(devices_chan):
                piece = product[target * channels : (target + 1) * channels]
                place = (part, target % 2, target // 2)
                if step:
                    piece = partial[place] + piece
                partial[place] = piece

    def pair_copy(part, there):
        return remote(
            partial.at[part, 1 - parity, there],
            pair_in.at[part, there],
            sent.at[6],
            pair_recv.at[part, there],
            partner,
        )

    def far_copy(part, step):
        return remote(
            (chip_sum, late_sum)[part // early].at[part % early, step - 1],
            (far_in, late_in)[part // early].at[part % early, step - 1],
            sent.at[7 if part < early else 17],
            far_recv.at[part, step - 1],
            (seq, ahead(group, step, groups) * 2 + parity),
        )

    def pair_start(part):
        for step in range(1, groups + 1):
            pair_copy(part, ahead(group, step, groups)).start()

    def far_start(part):
        for step in range(1, groups):
            there = ahead(group, step, groups)
            pair_copy(part, there).wait_recv()
            total = partial[part, parity, there] + pair_in[part, there]
            if part < early:
                chip_sum[part, step - 1] = total
            else:
                late_sum[part - early, step - 1] = total.astype(late_sum.dtype)
            far_copy(part, step).start()

    def far_finish(part):
        pair_copy(part, group).wait_recv()
        total = partial[part, parity, group] + pair_in[part, group]
        for step in range(1, groups):
            far_copy(part, step).wait_recv()
            arriving = (far_in, late_in)[part // early]
            total = total + arriving[part % early, step - 1].astype(jnp.float32)
        return total

    def flow(part, step):
        return remote(
            flows.at[part, chan],
            flows.at[part, chan],
            sent.at[8],
            flow_recv.at[part, step - 1],
            (seq, ahead(group, step, groups) * 2 + parity),
        )

    def flow_in(part, step):
        source = behind(group, step, groups) * 2 + parity
        return remote(
            flows.at[part, source],
            flows.at[part, source],
            sent.at[8],
            flow_recv.at[part, step - 1],
            (seq, source),
        )

    def flow_pass(part, step):
        source = behind(group, step, groups) * 2 + parity
        return remote(
            flows.at[part, source],
            flows.at[part, source],
            sent.at[9],
            pass_recv.at[part, step],
            partner,
        )

    def flow_passed(part, step):
        source = behind(group, step, groups) * 2 + 1 - parity
        return remote(
            flows.at[part, source],
            flows.at[part, source],
            sent.at[9],
            pass_recv.at[part, step],
            partner,
        )

    def flow_start(part):
        for step in range(1, groups):
            flow(part, step).start()
        flow_pass(part, 0).start()

    def flow_on(part):
        for step in range(1, groups):
            flow_in(part, step).wait_recv()
            flow_pass(part, step).start()

    def flow_finish(part):
        for step in range(groups):
            flow_passed(part, step).wait_recv()

    def near_copy(part, step, target):
        return remote(
            parts.at[part, step - 1, target],
            near.at[part, step - 1, target],
            sent.at[10],
            near_recv.at[part, step - 1, target],
            (plane * twins + ahead(twin, step, twins), chan),
        )

    def multiply(part):
        for step in range(1, twins + 1):
            block = ahead(twin, step, twins)
            columns = pl.ds(pl.multiple_of(block * owned, owned), owned)
            product = jnp.dot(
                flows[part].reshape(devices_chan * channels, rows),
                inputs[part][:, columns],
                preferred_element_type=jnp.float32,
            )
            for target in range(devices_chan):
                piece = product[target * channels : (target + 1) * channels]
                if step < twins:
                    parts[part, step - 1, target] = piece.astype(parts.dtype)
                else:
                    kept[part, target] = piece
            if step < twins:
                for index in range(1, devices_chan + 1):
                    near_copy(part, step, ahead(chan, index, devices_chan)).start()

    def turn(part, target):
        return remote(
            summed.at[part, target],
            blocks.at[part, chan],
            sent.at[11],
            turn_recv.at[part, chan],
            (seq, target),
        )

    def turn_in(part, source):
        return remote(
            summed.at[part, source],
            blocks.at[part, source],
            sent.at[11],
            turn_recv.at[part, source],
            (seq, source),
        )

    straight = (0, 1, 2, 3)

    def home(part, mask):
        return remote(
            blocks.at[part, flip(plane, mask)],
            arrived.at[part, mask],
            sent.at[12],
            home_recv.at[part, mask - 1],
            (flip(plane, mask if part in straight else mask & -mask) * twins + twin, chan),
        )

    def turn_start(part, index):
        target = ahead(chan, index, devices_chan)
        total = kept[part, target]
        for step in range(1, twins):
            near_copy(part, step, target).wait_recv()
            total = total + near[part, step - 1, target].astype(jnp.float32)
        total = total.astype(blocks.dtype)
        if index < devices_chan:
            summed[part, target] = total
            turn(part, target).start()
        else:
            blocks[part, chan] = total

    def turned(part, index):
        source = behind(chan, index, devices_chan)
        if index < devices_chan:
            turn_in(part, source).wait_recv()

        for mask in range(1, planes, 1 if part in straight else 2):

            @pl.when(flip(plane, mask) == source)
            def _(mask=mask):
                home(part, mask).start()

    def gathered(part, mask):
        total = blocks[part, flip(plane, mask)].astype(jnp.float32)
        for other in range(1, planes) if part in straight else reversed(bits):
            if mask == 0 or other < mask & -mask:
                home(part, mask ^ other).wait_recv()
                total = total + arrived[part, mask ^ other].astype(jnp.float32)
        return total

    targets = (grad_in.at[1], grad_out, grad_in.at[0], grad_in.at[2])

    def put(part):
        return pltpu.make_async_copy(results.at[part], targets[part], put_sem.at[part])

    def finish(part):
        results[part] = gathered(part, 0)
        put(part).start()

    def home_on(part):
        for mask in range(planes - 1, 0, -1):
            if mask & -mask > 1 and part not in straight:
                blocks[part, flip(plane, mask)] = gathered(part, mask).astype(blocks.dtype)
                home(part, mask).start()

    def rowed(array):
        width = array.shape[1] // folds
        stacked = jnp.concatenate(
            [array[:, fold * width : (fold + 1) * width] for fold in range(folds)], axis=0
        )
        return stacked.T

    def unrowed(array):
        stacked = array.T
        return jnp.concatenate(
            [stacked[fold * channels : (fold + 1) * channels] for fold in range(folds)], axis=1
        )

    def mode_row(kind, mode):
        return jnp.broadcast_to(consts[kind, mode : mode + 1], (groups_of_rows, lanes))

    def line(index):
        return pl.ds(index, groups_of_rows, stride=span)

    def scan_states():
        fall = [mode_row(2, mode) for mode in range(modes)]

        def body(step, carry):
            here = signal[line(span - 1 - step)]
            return tuple(carry[mode] * fall[mode] + here for mode in range(modes))

        zero = jnp.zeros((groups_of_rows, lanes), jnp.float32)
        found = lax.fori_loop(0, span, body, (zero,) * modes)
        position = lax.broadcasted_iota(jnp.int32, (groups_of_rows, lanes), 0)
        for mode in range(modes):
            each = mode_row(0, mode) * span
            total = found[mode]
            shift = 1
            while shift < groups_of_rows:
                moved = pltpu.roll(total, groups_of_rows - shift, 0)
                moved = moved * jnp.exp(-each * shift)
                total = total + jnp.where(position < groups_of_rows - shift, moved, 0.0)
                shift *= 2
            moved = pltpu.roll(total, groups_of_rows - 1, 0)
            bank[mode] = jnp.where(position < groups_of_rows - 1, moved, 0.0)
            own_state[mode : mode + 1] = total[0:1]
        heads = own_state[...]
        reach = consts[0] * (span * groups_of_rows)
        later = pltpu.roll(heads, channels, 1)
        first = lax.broadcasted_iota(jnp.int32, (modes, lanes), 1) < channels
        consts[3] = jnp.where(first, later, 0.0)
        own_state[...] = jnp.where(first, heads + later * jnp.exp(-reach), 0.0)

    def state_copy(step):
        return remote(
            own_state,
            states.at[step],
            sent.at[13],
            state_recv,
            (ahead(seq, step, devices_seq), chan),
        )

    def scan_source():
        rates = consts[0]
        following = jnp.zeros((modes, lanes), jnp.float32)
        landed = states.at[pl.ds(1, devices_seq - 1)]
        remote(landed, landed, sent.at[13], state_recv, partner).wait_recv()
        for step in range(1, devices_seq):
            gap = behind(seq, step, devices_seq) - seq - 1
            reach = (jnp.maximum(gap, 0) * rows).astype(jnp.float32)
            present = (gap >= 0).astype(jnp.float32)
            following = following + present * states[step] * jnp.exp(-reach * rates)
        first = lax.broadcasted_iota(jnp.int32, (modes, lanes), 1) < channels
        after = pltpu.roll(following, channels, 1)
        within = following * jnp.exp(-(rates * (span * groups_of_rows)))
        consts[3] = jnp.where(first, consts[3] + within, after)
        fall = [mode_row(2, mode) for mode in range(modes)]
        weigh = [mode_row(1, mode) for mode in range(modes)]
        position = lax.broadcasted_iota(jnp.int32, (groups_of_rows, lanes), 0)
        left = ((groups_of_rows - 1 - position) * span).astype(jnp.float32)
        start = tuple(
            bank[mode] + mode_row(3, mode) * jnp.exp(-left * mode_row(0, mode))
            for mode in range(modes)
        )

        def body(step, carry):
            here = line(span - 1 - step)
            entry = signal[here]
            following = tuple(carry[mode] * fall[mode] + entry for mode in range(modes))
            terms = [following[mode] * weigh[mode] for mode in range(modes)]
            while len(terms) > 1:
                terms = [sum(terms[at : at + 2]) for at in range(0, len(terms), 2)]
            signal[here] = terms[0]
            return following

        lax.fori_loop(0, span, body, start)

    def settle(group, mask):
        for part in group:
            if crosses(part, mask):
                cross_on(part, mask)
            else:
                share(part, mask)

    arrive(first, 1)
    settle(first, 0)
    arrive(first, 2)
    depart(last)
    for part in last:
        here(part, 0)
    settle(first, 1)
    arrive(first, 3)
    settle(first, 2)
    arrive(last, 1)
    settle(last, 0)
    settle(first, 3)
    arrive(last, 2)
    settle(last, 1)
    for load in bulk_loads:
        load.wait()
    project(0)
    pair_start(0)
    project(1)
    pair_start(1)
    arrive(last, 3)
    settle(last, 2)
    far_start(0)
    far_start(1)
    taken = conv[...].astype(jnp.float32)
    second = far_finish(0).astype(flows.dtype).astype(jnp.float32)
    flows[1, chan] = (second * taken).astype(flows.dtype)
    flow_start(1)
    settle(last, 3)
    upstream = far_finish(1)
    flows[0, chan] = (upstream * taken).astype(flows.dtype)
    flow_start(0)
    signal[...] = rowed(upstream * second)
    flow_on(1)
    scan_states()
    for step in range(1, devices_seq):
        state_copy(step).start()
    project(2)
    pair_start(2)
    flow_finish(1)
    multiply(1)
    project(3)
    pair_start(3)
    far_start(2)
    far_start(3)
    flow_on(0)
    flow_finish(0)
    multiply(0)
    turn_start(1, 1)
    scan_source()
    source = unrowed(signal[...])
    turn_start(1, 2)
    late = far_finish(2).astype(flows.dtype).astype(jnp.float32)
    flows[3, chan] = (source * late).astype(flows.dtype)
    flow_start(3)
    late = far_finish(3).astype(flows.dtype).astype(jnp.float32)
    flows[2, chan] = (source * late).astype(flows.dtype)
    flow_start(2)
    turn_start(1, 3)
    turned(1, 1)
    turn_start(1, 4)
    turned(1, 2)
    flow_on(3)
    turn_start(0, 1)
    flow_on(2)
    turn_start(0, 2)
    flow_finish(3)
    turned(1, 3)
    multiply(3)
    flow_finish(2)
    multiply(2)
    turned(1, 4)
    turn_start(0, 3)
    turned(0, 1)
    turn_start(0, 4)
    turned(0, 2)
    turned(0, 3)
    turned(0, 4)
    turn_start(3, 1)
    turn_start(3, 2)
    turn_start(3, 4)
    turn_start(3, 3)
    turned(3, 1)
    turned(3, 2)
    turn_start(2, 1)
    turned(3, 3)
    turn_start(2, 2)
    turned(3, 4)
    finish(1)
    turn_start(2, 3)
    turned(2, 1)
    finish(0)
    turn_start(2, 4)
    turned(2, 2)
    turned(2, 3)
    turned(2, 4)
    finish(3)
    finish(2)
    for part in range(count):
        put(part).wait()

    def left(kind, ref):
        remote(ref, ref, sent.at[kind], state_recv, partner).wait_send()

    fewer = pl.ds(0, planes - 1)
    others = pl.ds(1, twins - 1)
    inner = jnp.logical_and(plane > 0, plane < planes - 1)

    @pl.when(inner)
    def _():
        left(0, pieces.at[:, pl.ds(0, 2)])
        left(16, pieces.at[:, fewer])

    @pl.when(jnp.logical_not(inner))
    def _():
        left(0, pieces.at[:, pl.ds(0, 1)])

    left(1, pieces.at[:, fewer])
    for group in range(2):
        span_of = pl.ds(group * early, early)
        masks = crossing[group]
        if masks:
            left(14 + group, crossed.at[span_of, others, pl.ds(0, len(masks))])
        for mask in range(planes):

            @pl.when(flip(plane, mask) == chan)
            def _(mask=mask):
                swaps = len(masks) - (mask in masks)
                if swaps:
                    left(2 + group, crossed.at[span_of, others, pl.ds(0, swaps)])
                if mask not in masks:
                    left(4 + group, weights.at[span_of, others])

    left(6, partial.at[:, 0])
    left(7, chip_sum)
    left(17, late_sum)
    left(8, flows.at[:, pl.ds(0, groups - 1)])
    left(9, flows.at[:, pl.ds(0, groups)])
    left(10, parts)
    left(11, summed.at[:, fewer])
    left(12, blocks.at[:, fewer])
    left(13, states.at[pl.ds(1, devices_seq - 1)])


def place_kernel(grad_in, grad_proj, out_in, out_proj, held, take_sem, give_sem):
    streams = grad_in.shape[0]
    ends = [(grad_in.at[at], out_in.at[at]) for at in range(streams)] + [(grad_proj, out_proj)]
    takes = [
        pltpu.make_async_copy(source, held.at[at], take_sem.at[at])
        for at, (source, _) in enumerate(ends)
    ]
    gives = [
        pltpu.make_async_copy(held.at[at], target, give_sem.at[at])
        for at, (_, target) in enumerate(ends)
    ]
    for take in takes:
        take.start()
    for take, give in zip(takes, gives):
        take.wait()
        give.start()
    for give in gives:
        give.wait()


def placed(grad_in, grad_proj):
    anywhere, dma = pl.BlockSpec(memory_space=pl.ANY), pltpu.SemaphoreType.DMA
    count = grad_in.shape[0] + 1
    return pl.pallas_call(
        place_kernel,
        out_shape=tuple(jax.ShapeDtypeStruct(a.shape, a.dtype) for a in (grad_in, grad_proj)),
        in_specs=[anywhere] * 2,
        out_specs=(anywhere, anywhere),
        scratch_shapes=[
            pltpu.VMEM((count,) + grad_proj.shape, grad_proj.dtype),
            dma((count,)),
            dma((count,)),
        ],
        name="place_outputs",
    )(grad_in, grad_proj)


def fits(tokens, conv_out, in_weight, residues):
    devices_seq, devices_chan = lax.axis_size("seq"), lax.axis_size("chan")
    rows, channels = conv_out.shape
    return (
        devices_chan == 4
        and devices_seq % devices_chan == 0
        and devices_seq > devices_chan
        and in_weight.shape[0] % 128 == 0
        and 2 * channels == 128
        and channels % residues.shape[1] == 0
        and rows % 256 == 0
        and tokens.shape[1] * devices_chan == in_weight.shape[0] * devices_seq
    )


def blocked(tokens, grad_out, in_weight, out_weight, conv_out, residues, decay_length):
    devices_seq, devices_chan = lax.axis_size("seq"), lax.axis_size("chan")
    planes, groups = devices_chan, devices_chan // 2
    twins = devices_seq // planes
    rows, width = tokens.shape
    channels, owned = out_weight.shape[1], out_weight.shape[0]
    modes = residues.shape[0]
    anywhere = pl.BlockSpec(memory_space=pl.ANY)
    dma, half_type, full = pltpu.SemaphoreType.DMA, tokens.dtype, jnp.float32
    lanes = 2 * channels
    grad_in, grad_proj = pl.pallas_call(
        functools.partial(block_kernel, devices_seq, devices_chan),
        out_shape=(
            jax.ShapeDtypeStruct((3, channels, owned), full),
            jax.ShapeDtypeStruct((channels, owned), full),
        ),
        in_specs=[anywhere] * 7,
        out_specs=(anywhere, anywhere),
        scratch_shapes=[
            pltpu.VMEM((rows, width), half_type),
            pltpu.VMEM((rows, width), half_type),
            pltpu.VMEM((channels, rows), half_type),
            pltpu.VMEM((4, planes, channels, owned), half_type),
            pltpu.VMEM((4, twins, planes, channels, owned), half_type),
            pltpu.VMEM((4, twins, devices_chan, channels, owned), half_type),
            pltpu.VMEM((4, 2, groups, channels, rows), full),
            pltpu.VMEM((4, groups, channels, rows), full),
            pltpu.VMEM((2, groups - 1, channels, rows), full),
            pltpu.VMEM((2, groups - 1, channels, rows), full),
            pltpu.VMEM((2, groups - 1, channels, rows), half_type),
            pltpu.VMEM((2, groups - 1, channels, rows), half_type),
            pltpu.VMEM((rows * channels // lanes, lanes), full),
            pltpu.VMEM((4, modes, lanes), full),
            pltpu.VMEM((modes, 8, lanes), full),
            pltpu.VMEM((modes, lanes), full),
            pltpu.VMEM((devices_seq, modes, lanes), full),
            pltpu.VMEM((4, devices_chan, channels, rows), half_type),
            pltpu.VMEM((4, twins - 1, devices_chan, channels, owned), half_type),
            pltpu.VMEM((4, devices_chan, channels, owned), full),
            pltpu.VMEM((4, twins - 1, devices_chan, channels, owned), half_type),
            pltpu.VMEM((4, devices_chan, channels, owned), half_type),
            pltpu.VMEM((4, planes, channels, owned), half_type),
            pltpu.VMEM((4, planes, channels, owned), half_type),
            pltpu.VMEM((4, channels, owned), full),
            pltpu.VMEM((2,) + residues.shape, full),
            dma((9,)),
            dma((18,)),
            dma((4, planes)),
            dma((4, twins)),
            dma((4, twins)),
            dma((4, twins - 1, planes)),
        ]
        + [dma((4, groups)), dma((4, groups - 1)), dma, dma((4, groups - 1)), dma((4, groups))]
        + [dma((4, twins - 1, planes))]
        + [dma((4, planes)), dma((4, planes - 1)), dma((4,))],
        compiler_params=pltpu.CompilerParams(collective_id=2, has_side_effects=True),
        name="conv_block",
    )(
        tokens,
        grad_out,
        in_weight.transpose(1, 2, 0),
        out_weight.T,
        conv_out.T,
        residues,
        decay_length,
    )
    grad_in, grad_proj = placed(grad_in, grad_proj)
    return grad_in.transpose(2, 0, 1), grad_proj.T


def local(tokens, grad_out, in_weight, out_weight, conv_out, residues, decay_length):
    if fits(tokens, conv_out, in_weight, residues):
        return blocked(tokens, grad_out, in_weight, out_weight, conv_out, residues, decay_length)
    channels = out_weight.shape[1]
    owned_rows = in_weight.shape[0]
    weights = jnp.concatenate([in_weight.reshape(owned_rows, 3 * channels), out_weight], axis=1)
    full_tokens, full_grads, projected, upstream = gathered(tokens, grad_out, weights)
    projected = projected[:, : 3 * channels]
    upstream = upstream[:, channels:]
    streams = lax.reduce_precision(projected, exponent_bits=8, mantissa_bits=7)
    gate_first = streams[:, :channels]
    gate_second = streams[:, channels : 2 * channels]
    value_stream = streams[:, 2 * channels :]
    conv_value = conv_out.astype(jnp.float32)
    gated = (gate_second * conv_value).astype(jnp.bfloat16)
    grad_second = (upstream * conv_value).astype(jnp.bfloat16)
    grad_conv = upstream * gate_second
    inner, state, rate, weight = correlate_block(grad_conv, residues, decay_length)
    blank = jnp.zeros_like(gated)
    owned = reduced(
        state,
        rate,
        weight,
        inner,
        value_stream,
        gate_first,
        jnp.concatenate([grad_second, blank], axis=1),
        jnp.concatenate([blank, gated], axis=1),
        full_tokens,
        full_grads,
        owned_rows,
    )
    grad_in = jnp.stack(
        [owned[1, :, :channels], owned[0, :, :channels], owned[1, :, channels:]], axis=1
    )
    return (grad_in, owned[0, :, channels:])


def solution(mesh):
    return jax.shard_map(
        local,
        mesh=mesh,
        in_specs=(
            P("seq", "chan"),
            P("seq", "chan"),
            P("seq", None, "chan"),
            P("seq", "chan"),
            P("seq", "chan"),
            P(None, "chan"),
            P(None, "chan"),
        ),
        out_specs=(P("seq", None, "chan"), P("seq", "chan")),
        check_vma=False,
    )
```
